768 devices in a mesh: px: 48 (over z, y_hi), py: 4 (over x), dz: 4 (over y_lo, core).
Axes of the slice: x: 4, y: 8 (y_hi: 4, y_lo: 2; y = y_hi * 2 + y_lo), z: 12, core: 2. Of those that a mesh axis runs over, the one named last changes fastest.
Arguments:
- near_state: float32 [3, 384, 192, 1024], P(None, 'px', 'dz', 'py'), may hold values from -1 to 1, as said below
- column_owner: int32 [48, 16, 512, 1], P('px', ('py', 'dz')), may hold values from 0 to 15; in each aligned block of 512 rows (0 to 511, 512 to 1023, ..., all dimensions but the last counted through in order) at most 128 rows name the same one
- landing: int32 [48, 16, 512], P('px', ('py', 'dz')), may hold values from 0 to 16383
- far_depth: float32 [3072, 4096], P('px', ('py', 'dz')), may hold values from 3 to 6
- far_flows: float32 [2, 3072, 4096], P(None, 'px', ('py', 'dz')), may hold values from -3 to 3
- wet_mask: int32 [3072, 4096], P('px', ('py', 'dz')), may hold values 0 or 1
Outputs:
- near_fraction: float32 [384, 192, 1024], P('px', 'dz', 'py')
- far_new: float32 [3, 3072, 4096], P(None, 'px', ('py', 'dz'))
The draws below stay inside these ranges and needn't reach their ends.
Inputs may be any that keep to these rules, and one draw needn't show every extreme that they name: `near_state`: the volume fraction (first field) lies in 0 to 1; the velocities lie in -1 to 1. `column_owner`: in each near tile no owner receives more than 128 columns; some owner receives exactly 128.
All inputs are finite; a program needn't handle non-finite values. No bound on the sum of `wet_mask` on one device may be relied on, other than what follows from the above.
Results may differ from the reference program's by a relative error of at most 0.00002.
Values sent between devices are 32-bit elements; how exact they have to be, the bound alone decides.
No kernel may reach another device: no remote copies, remote signals or barrier semaphores. Data moves between devices by JAX's collectives and lax.ppermute only.
A program may use at most 32 MiB of HBM per device.

```python
import math
import jax
import jax.numpy as jnp
import numpy as np
from jax import lax

CX = 8
FX = 64
FY = 256
CAP = 128
NXN = 384
NYN = 1024
NZN = 192
NDEST = 16
QY = 64
NCOL = 512
FNX = 3072
FNY = 4096
N_PX = 48


def draw_near_state(key, part):
    subkeys = jax.random.split(key, 4)
    cell_shape = (NXN, NZN, NYN)
    column_shape = (NXN, 1, NYN)
    column_factor = jax.random.uniform(subkeys[0], column_shape, jnp.float32, 0.3, 1.0)
    cell_factor = jax.random.uniform(subkeys[1], cell_shape, jnp.float32, 0.4, 1.0)
    slowest = 0.2
    fraction = column_factor * cell_factor
    speed_x = jax.random.uniform(subkeys[2], cell_shape, jnp.float32, slowest, 1.0)
    speed_y = jax.random.uniform(subkeys[3], cell_shape, jnp.float32, slowest, 1.0)
    return jnp.stack([fraction, speed_x, speed_y]).astype(jnp.float32)


def plant(drawn, own_key, least, largest):
    index_at = [jax.random.randint(jax.random.fold_in(own_key, axis), (), 0, length) for axis, length in enumerate(drawn.shape)]
    widest = drawn.shape.index(max(drawn.shape))
    neighbour = index_at[:widest] + [(index_at[widest] + 1) % drawn.shape[widest]] + index_at[widest + 1:]
    return drawn.at[tuple(index_at)].set(least).at[tuple(neighbour)].set(largest)


def steps_of(own_key, extent, shards, low, high):
    level, own = 1.0, jax.random.fold_in(own_key, 6)
    for dim, parts in shards:
        heights = jnp.exp(jax.random.uniform(jax.random.fold_in(own, dim), (parts,), jnp.float32, low / len(shards), high / len(shards)))
        level = level * jnp.repeat(heights, extent[dim] // parts).reshape([-1 if axis == dim else 1 for axis in range(len(extent))])
    return level


def routed_block(rng, own, number, rows, number_of, top, most, skew):
    sequence = jax.random.permutation(rng, number_of)
    heavy_load, common = portions_of(number_of, rows * top, most, skew, True), portions_of(number_of, rows * top, most, skew, False)
    places = jnp.arange(number_of)

    def named(sizes, offset_by):
        used = int((sizes > 0).sum())
        fixed = max(1, used // 4)
        moved = fixed + (places - fixed + offset_by * (used - fixed)) % max(1, number_of - fixed)
        return jnp.zeros((number_of,), jnp.int32).at[sequence[jnp.where(places < fixed, places, moved)]].set(jnp.asarray(sizes, jnp.int32))

    sizes = jnp.where(number % 4 == 0, named(heavy_load, number // 4), named(common, number - number // 4 - 1))
    mixed = jax.random.permutation(jax.random.fold_in(own, 3), number_of)
    source_of, sink = mixed[0:number_of // 2 * 2:2], mixed[1:number_of // 2 * 2:2]
    margin = jnp.minimum(sizes[source_of] - 1, most - sizes[sink]) // 2
    margin = jnp.where((source_of == sequence[0]) | (sink == sequence[0]) | (sizes[sink] == 0), 0, jnp.maximum(margin, 0))
    moved = jax.random.randint(jax.random.fold_in(own, 4), (number_of // 2,), 0, 1 << 20) % (margin + 1)
    sizes = sizes.at[source_of].add(-moved).at[sink].add(moved)
    members = jnp.searchsorted(jnp.cumsum(sizes), jnp.arange(rows * top), side="right").astype(jnp.int32)
    grid = members.reshape(top, rows).T
    grid = grid[jax.random.permutation(jax.random.fold_in(own, 1), rows)]
    offset_by = jax.random.randint(jax.random.fold_in(own, 2), (rows, 1), 0, top)
    return jnp.take_along_axis(grid, (jnp.arange(top)[None, :] + offset_by) % top, axis=1)


def portions_of(count, total, most, lean, full):
    portions = [(1 << 20) // math.isqrt(standing ** lean) + 1 for standing in range(1, count + 1)]
    largest = most if full else min(most, max(-(-total // count), total * portions[0] // sum(portions)))
    least = 1 if total - largest >= count - 1 else 0
    counts, surplus = [largest] + [least] * (count - 1), total - largest - least * (count - 1)
    while surplus > 0:
        candidates = [i for i in range(1, count) if counts[i] < largest] or [i for i in range(1, count) if counts[i] < most]
        pool, budget = sum([portions[i] for i in candidates]), surplus
        for i in candidates:
            extra = min(most - counts[i], max(1, budget * portions[i] // pool), surplus)
            counts[i] = counts[i] + extra
            surplus = surplus - extra
    return np.array(counts)


def centred(stream_key, extent, spread, most, pieces=(), held_as=jnp.bfloat16):
    drawn = spread * jax.random.normal(stream_key, extent, jnp.float32)
    if pieces:
        drawn = drawn * steps_of(stream_key, extent, pieces, -0.22, 0.18)
    return jnp.clip(drawn, -most, most).astype(held_as)


def setup_inputs(seed: int = 0) -> dict:
    streams_of = jax.random.split(jax.random.key(seed), 7)
    near_state = draw_near_state(jax.random.fold_in(streams_of[6], 71), 0)
    column_owner_keys = jax.random.split(jax.random.fold_in(streams_of[1], 1), N_PX * NDEST * NCOL // NCOL)
    column_owner_turns = jax.random.permutation(jax.random.fold_in(streams_of[1], 3), N_PX * NDEST * NCOL // NCOL)
    column_owner = jax.vmap(lambda own, number: routed_block(jax.random.fold_in(streams_of[1], 2), own, number, NCOL, NDEST, 1, CAP, 2))(column_owner_keys, column_owner_turns).reshape((N_PX, NDEST, NCOL, 1))
    landing = plant(jax.random.randint(streams_of[2], (N_PX, NDEST, NCOL), 0, FX * FY), jax.random.fold_in(streams_of[2], 1), 0, (FX * FY) - 1).astype(jnp.int32)
    far_depth = jnp.clip(3.0 + 3.0 * jax.random.uniform(streams_of[3], (FNX, FNY), jnp.float32) ** steps_of(streams_of[3], (FNX, FNY), ((0, 48), (1, 16)), -0.2, 0.2), 3.0, 6.0)
    far_flows = centred(streams_of[4], (2, FNX, FNY), 0.5, 3.0, ((1, 48), (2, 16)), jnp.float32)
    wet_mask = plant((jax.random.randint(streams_of[5], (FNX, FNY), 0, 5) < 4).astype(jnp.int32), jax.random.fold_in(streams_of[5], 1), 0, 1)
    return dict(near_state=near_state, column_owner=column_owner, landing=landing, far_depth=far_depth, far_flows=far_flows, wet_mask=wet_mask)


advect_coef = 0.25
diffuse_coef = 0.1
slope_coef = 0.5
flux_coef = 0.1
gravity = 1.0
column_height = 4.0


def near_update(center, xplus, xminus, yplus, yminus, zplus, zminus):
    velx = center[1]
    vely = center[2]
    lap = xplus + xminus + yplus + yminus + zplus + zminus - 6.0 * center
    moved = center - advect_coef * (velx * (xplus - xminus) + vely * (yplus - yminus)) + diffuse_coef * lap
    new_frac = moved[0]
    new_velx = moved[1] - slope_coef * (xplus[0] - xminus[0])
    new_vely = moved[2] - slope_coef * (yplus[0] - yminus[0])
    return new_frac, new_velx, new_vely


def far_update(padded):
    state = padded[0:3]
    xflux = padded[3:6]
    yflux = padded[6:9]
    avg = 0.25 * (state[:, 2:, 1:-1] + state[:, :-2, 1:-1] + state[:, 1:-1, 2:] + state[:, 1:-1, :-2])
    return avg - flux_coef * (xflux[:, 2:, 1:-1] - xflux[:, :-2, 1:-1]) - flux_coef * (yflux[:, 1:-1, 2:] - yflux[:, 1:-1, :-2])


def fluxes(state):
    depth = state[0]
    flow_x = state[1]
    flow_y = state[2]
    cross = flow_x * flow_y / depth
    press = 0.5 * gravity * depth * depth
    xflux = jnp.stack([flow_x, flow_x * flow_x / depth + press, cross])
    yflux = jnp.stack([flow_y, cross, flow_y * flow_y / depth + press])
    return xflux, yflux


def reference(near_state, column_owner, landing, far_depth, far_flows, wet_mask):
    padded = jnp.pad(near_state, ((0, 0), (1, 1), (1, 1), (1, 1)))
    inv_depth = column_height / NZN

    def tile(index):
        sl = lax.dynamic_slice_in_dim(padded, index * CX, CX + 2, 1)
        center = sl[:, 1:-1, 1:-1, 1:-1]
        new_frac, new_velx, new_vely = near_update(center, sl[:, 2:, 1:-1, 1:-1], sl[:, :-2, 1:-1, 1:-1], sl[:, 1:-1, 1:-1, 2:], sl[:, 1:-1, 1:-1, :-2], sl[:, 1:-1, 2:, 1:-1], sl[:, 1:-1, :-2, 1:-1])
        sums = jnp.stack([jnp.sum(new_frac, axis=1), jnp.sum(new_frac * new_velx, axis=1), jnp.sum(new_frac * new_vely, axis=1)]) * inv_depth
        return new_frac, sums

    fracs, sums = lax.map(tile, jnp.arange(N_PX, dtype=jnp.int32))
    near_fraction = fracs.reshape(NXN, NZN, NYN)
    columns = jnp.transpose(sums, (1, 0, 2, 3)).reshape(3, N_PX, CX, NDEST, QY)
    columns = jnp.transpose(columns, (0, 1, 3, 2, 4)).reshape(3, N_PX * NDEST * NCOL)
    owner = column_owner[..., 0]
    tile_x = jnp.arange(N_PX, dtype=jnp.int32)[:, None, None]
    glob_x = tile_x * FX + landing // FY
    glob_y = owner * FY + landing % FY
    flat = (glob_x * FNY + glob_y).reshape(-1)
    source = jnp.zeros((3, FNX * FNY), jnp.float32).at[:, flat].add(columns).reshape(3, FNX, FNY)
    wet = wet_mask.astype(jnp.float32)
    state = jnp.stack([far_depth, far_flows[0], far_flows[1]]) + source
    state = jnp.stack([state[0], state[1] * wet, state[2] * wet])
    xflux, yflux = fluxes(state)
    stacked = jnp.concatenate([state, xflux, yflux], axis=0)
    far_new = far_update(jnp.pad(stacked, ((0, 0), (1, 1), (1, 1))))
    return near_fraction, far_new
```

```python
import functools

import jax
import jax.numpy as jnp
from jax import lax
from jax.experimental import pallas as pl
from jax.experimental.pallas import tpu as pltpu
from jax.sharding import PartitionSpec as P

advect_coef = 0.25
diffuse_coef = 0.1
slope_coef = 0.5
flux_coef = 0.1
gravity = 1.0
column_height = 4.0

NPY = 4
NDZ = 4
GRP = NPY * NDZ
CX = 8
CZ = 48
CY = 256
FX = 64
FY = 256
ROWS = CX * 3 * 2
BLK = ROWS + 8
NROW = FY + 16

f32 = jnp.float32
GROUP = ("py", "dz")
VM = pl.BlockSpec(memory_space=pltpu.VMEM)
PARAMS = pltpu.CompilerParams(vmem_limit_bytes=24 << 20)


def lane_iota(shape):
    return lax.broadcasted_iota(jnp.int32, shape, len(shape) - 1)


def x_order(row):
    return 2 * row if row < 4 else 2 * (row - 4) + 1


def pack_kernel(near, owner, land, depth, flows, mask, out, xlo, xhi):
    py = lax.axis_index("py")
    dz = lax.axis_index("dz")
    me = py * NDZ + dz
    xlo[...] = near[:, 0]
    xhi[...] = near[:, CX - 1]
    code = (owner[...] * (FX * FY) + land[...]).astype(f32)
    swap = pltpu.roll(code, 64, 1)
    odd = (me % 2) == 1
    codes = jnp.concatenate([jnp.where(odd, swap, code), jnp.where(odd, code, swap)], axis=0)
    lanes = lane_iota((8, 128))
    mine = jnp.where(odd, lanes, 127 - lanes) >= 64
    codes = jnp.where(mine, codes, 0.0)
    zero = jnp.zeros((ROWS, 128), f32)
    for b in range(GRP):
        out[b, 0:ROWS] = zero
        out[b, ROWS:BLK] = codes

    def edge(col):
        k = lane_iota((FX, 128))
        m = jnp.zeros((FX, 128), f32)
        for n, part in enumerate((depth[...], flows[0], flows[1], mask[...].astype(f32))):
            m = jnp.where(k == n, part[:, col : col + 1], m)
        turned = jnp.concatenate([m, m], axis=0).T
        return jnp.where(mine, codes, turned[0:8])

    @pl.when(me > 0)
    def _():
        out[me - 1, ROWS:BLK] = edge(0)

    @pl.when(me < GRP - 1)
    def _():
        out[me + 1, ROWS:BLK] = edge(FY - 1)

    def zface(dst, z):
        for f in range(3):
            face = near[f, :, z, :]
            for h in range(2):
                r = (f * 2 + h) * 8
                out[dst, r : r + 8] = face[:, h * 128 : (h + 1) * 128]

    def yface(dst, y):
        k = lane_iota((CZ, 128))
        m = jnp.zeros((CZ, 128), f32)
        for f in range(3):
            for x in range(CX):
                m = jnp.where(k == f * CX + x, near[f, x, :, y : y + 1], m)
        out[dst, 0:ROWS] = m

    @pl.when(dz > 0)
    def _():
        zface(me - 1, 0)

    @pl.when(dz < NDZ - 1)
    def _():
        zface(me + 1, CZ - 1)

    @pl.when(py > 0)
    def _():
        yface(me - NDZ, 0)

    @pl.when(py < NPY - 1)
    def _():
        yface(me + NDZ, CY - 1)


def near_kernel(near, got, xlow, xhigh, frac, sums):
    py = lax.axis_index("py")
    dz = lax.axis_index("dz")
    me = py * NDZ + dz
    at_l = jnp.maximum(me - NDZ, 0)
    at_r = jnp.minimum(me + NDZ, GRP - 1)
    at_d = jnp.maximum(me - 1, 0)
    at_u = jnp.minimum(me + 1, GRP - 1)
    left = jnp.where(py > 0, got[at_l, 0:ROWS], 0.0)
    right = jnp.where(py < NPY - 1, got[at_r, 0:ROWS], 0.0)
    down = jnp.where(dz > 0, got[at_d, 0:ROWS], 0.0)
    up = jnp.where(dz < NDZ - 1, got[at_u, 0:ROWS], 0.0)
    lane = lane_iota((CZ, CY))
    row = lax.broadcasted_iota(jnp.int32, (CZ, CY), 0)

    def face_row(face, f, x):
        return jnp.concatenate(
            [face[(f * 2 + h) * 8 + x : (f * 2 + h) * 8 + x + 1] for h in range(2)], axis=1
        )

    for p in range(CX):
        x = x_order(p)
        velx = near[1, x]
        vely = near[2, x]
        new = []
        for f in range(3):
            q = near[f, x]
            k = f * CX + x
            xp = near[f, x + 1] if x < CX - 1 else xhigh[f]
            xm = near[f, x - 1] if x > 0 else xlow[f]
            yp = jnp.where(lane == CY - 1, right[:, k : k + 1], pltpu.roll(q, CY - 1, 1))
            ym = jnp.where(lane == 0, left[:, k : k + 1], pltpu.roll(q, 1, 1))
            zp = jnp.where(row == CZ - 1, face_row(up, f, x), pltpu.roll(q, CZ - 1, 0))
            zm = jnp.where(row == 0, face_row(down, f, x), pltpu.roll(q, 1, 0))
            dx = xp - xm
            dy = yp - ym
            lap = xp + xm + yp + ym + zp + zm - 6.0 * q
            moved = q - advect_coef * (velx * dx + vely * dy) + diffuse_coef * lap
            if f == 0:
                fdx, fdy = dx, dy
            new.append(moved)
        frac[x] = new[0]
        parts = (
            new[0],
            new[0] * (new[1] - slope_coef * fdx),
            new[0] * (new[2] - slope_coef * fdy),
        )
        for f in range(3):
            total = jnp.sum(parts[f], axis=0, keepdims=True)
            for h in range(2):
                r = (f * 2 + h) * 8 + p
                sums[0, r : r + 1] = total[:, h * 128 : (h + 1) * 128]
    whole = sums[0]
    for b in range(1, GRP):
        sums[b] = whole


def scatter_kernel(scale, got, sums, depth, flows, mask, state, edges, top, bottom, bt, ah, al):
    me = lax.axis_index("py") * NDZ + lax.axis_index("dz")
    lanes = lane_iota((8, 128))
    ycell = lax.broadcasted_iota(jnp.int32, (NROW, 128), 0)
    xcell = lax.broadcasted_iota(jnp.int32, (FX, 128), 0)
    acc = jnp.zeros((NROW, 3 * FX), f32)
    for a in range(NPY):
        total = sums[a * NDZ]
        for b in range(1, NDZ):
            total = total + sums[a * NDZ + b]
        total = total * scale
        for h in range(2):
            d = a * NDZ + 2 * h
            code = jnp.where(lanes < 64, got[d, ROWS:BLK], got[d + 1, ROWS:BLK]).astype(jnp.int32)
            y = (code >> 14) * FY + (code & (FY - 1)) - me * FY
            y = jnp.where(y == -1, FY + 1, jnp.where(y > FY, -1, y))
            x = (code >> 8) & (FX - 1)
            for p in range(8):
                at = slice(p * 128, (p + 1) * 128)
                bt[:, at] = jnp.where(ycell == y[p : p + 1], 1.0, 0.0).astype(jnp.bfloat16)
                here = xcell == x[p : p + 1]
                for f in range(3):
                    r = (f * 2 + h) * 8 + p
                    value = total[r : r + 1]
                    high = value.astype(jnp.bfloat16).astype(f32)
                    cells = slice(f * FX, (f + 1) * FX)
                    ah[cells, at] = jnp.where(here, high, 0.0).astype(jnp.bfloat16)
                    al[cells, at] = jnp.where(here, value - high, 0.0).astype(jnp.bfloat16)
            over = (((1,), (1,)), ((), ()))
            acc = acc + lax.dot_general(bt[...], ah[...], over, preferred_element_type=f32)
            acc = acc + lax.dot_general(bt[...], al[...], over, preferred_element_type=f32)
    source = acc.T
    wet = mask[...].astype(f32)
    raw = (depth[...], flows[0], flows[1])
    cells = []
    for f in range(3):
        s = raw[f] + source[f * FX : (f + 1) * FX, 0:FY]
        cells.append(s if f == 0 else s * wet)
        state[f] = cells[f]
    blank = jnp.zeros((5, FY), f32)
    top[...] = jnp.concatenate([c[0:1] for c in cells] + [blank], axis=0)
    bottom[...] = jnp.concatenate([c[FX - 1 : FX] for c in cells] + [blank], axis=0)
    k = lane_iota((FX, 128))
    m = jnp.zeros((FX, 128), f32)
    for side in range(2):
        other = jnp.maximum(me - 1, 0) if side == 0 else jnp.minimum(me + 1, GRP - 1)
        block = got[other, ROWS:BLK]
        block = jnp.where((other % 2) == 1, block, pltpu.roll(block, 64, 1))
        e = jnp.concatenate([block] * 16, axis=0).T[0:FX]
        inside = (me > 0) if side == 0 else (me < GRP - 1)
        wet_e = e[:, 3:4]
        col = FY + 1 if side == 0 else FY
        for f in range(3):
            s = e[:, f : f + 1] + source[f * FX : (f + 1) * FX, col : col + 1]
            s = s if f == 0 else s * wet_e
            m = jnp.where((k == side * 3 + f) & inside, s, m)
    edges[...] = m


def terms(h, hu, hv, ok):
    inv = 1.0 / jnp.where(ok, h, 1.0)
    cross = hu * hv * inv
    press = 0.5 * gravity * h * h
    xf = (hu, hu * hu * inv + press, cross)
    yf = (hv, cross, hv * hv * inv + press)
    s = (h, hu, hv)
    return [
        (
            0.25 * s[f] - flux_coef * xf[f],
            0.25 * s[f] + flux_coef * xf[f],
            0.25 * s[f] - flux_coef * yf[f],
            0.25 * s[f] + flux_coef * yf[f],
        )
        for f in range(3)
    ]


def far_kernel(state, edges, above, below, out):
    px = lax.axis_index("px")
    n_px = lax.axis_size("px")
    me = lax.axis_index("py") * NDZ + lax.axis_index("dz")
    body = terms(state[0], state[1], state[2], True)
    e = edges[...]
    lo = terms(e[:, 0:1], e[:, 1:2], e[:, 2:3], me > 0)
    hi = terms(e[:, 3:4], e[:, 4:5], e[:, 5:6], me < GRP - 1)
    up = terms(above[0:1], above[1:2], above[2:3], px > 0)
    dn = terms(below[0:1], below[1:2], below[2:3], px < n_px - 1)
    lane = lane_iota((FX, FY))
    row = lax.broadcasted_iota(jnp.int32, (FX, FY), 0)
    for f in range(3):
        xp = jnp.where(row == FX - 1, dn[f][0], pltpu.roll(body[f][0], FX - 1, 0))
        xm = jnp.where(row == 0, up[f][1], pltpu.roll(body[f][1], 1, 0))
        yp = jnp.where(lane == FY - 1, hi[f][2], pltpu.roll(body[f][2], FY - 1, 1))
        ym = jnp.where(lane == 0, lo[f][3], pltpu.roll(body[f][3], 1, 1))
        out[f] = (xp + xm) + (yp + ym)


def shape(*dims):
    return jax.ShapeDtypeStruct(dims, f32)


def local(near_state, column_owner, landing, far_depth, far_flows, wet_mask):
    n_px = lax.axis_size("px")
    forth = [(i, i + 1) for i in range(n_px - 1)]
    back = [(i + 1, i) for i in range(n_px - 1)]
    owner = column_owner.reshape(4, 128)
    land = landing.reshape(4, 128)
    send, xlo, xhi = pl.pallas_call(
        pack_kernel,
        out_shape=(shape(GRP, BLK, 128), shape(3, CZ, CY), shape(3, CZ, CY)),
        in_specs=[VM] * 6,
        out_specs=(VM,) * 3,
        compiler_params=PARAMS,
        name="pack",
    )(near_state, owner, land, far_depth, far_flows, wet_mask)
    xlow = lax.ppermute(xhi, "px", forth)
    xhigh = lax.ppermute(xlo, "px", back)
    got = lax.all_to_all(send, GROUP, split_axis=0, concat_axis=0, tiled=True)
    new_frac, sums = pl.pallas_call(
        near_kernel,
        out_shape=(shape(CX, CZ, CY), shape(GRP, ROWS, 128)),
        in_specs=[VM] * 4,
        out_specs=(VM,) * 2,
        compiler_params=PARAMS,
        name="near",
    )(near_state, got, xlow, xhigh)
    sums = lax.all_to_all(sums, GROUP, split_axis=0, concat_axis=0, tiled=True)
    scale = column_height / (CZ * NDZ)
    state, edges, top, bottom = pl.pallas_call(
        functools.partial(scatter_kernel, scale),
        out_shape=(shape(3, FX, FY), shape(FX, 128), shape(8, FY), shape(8, FY)),
        in_specs=[VM] * 5,
        out_specs=(VM,) * 4,
        scratch_shapes=[
            pltpu.VMEM((NROW, 1024), jnp.bfloat16),
            pltpu.VMEM((3 * FX, 1024), jnp.bfloat16),
            pltpu.VMEM((3 * FX, 1024), jnp.bfloat16),
        ],
        compiler_params=PARAMS,
        name="scatter",
    )(got, sums, far_depth, far_flows, wet_mask)
    above = lax.ppermute(bottom, "px", forth)
    below = lax.ppermute(top, "px", back)
    far_new = pl.pallas_call(
        far_kernel,
        out_shape=shape(3, FX, FY),
        in_specs=[VM] * 4,
        out_specs=VM,
        compiler_params=PARAMS,
        name="far",
    )(state, edges, above, below)
    return (new_frac, far_new)


def solution(mesh):
    return jax.shard_map(
        local,
        mesh=mesh,
        in_specs=(
            P(None, "px", "dz", "py"),
            P("px", ("py", "dz"), None, None),
            P("px", ("py", "dz"), None),
            P("px", ("py", "dz")),
            P(None, "px", ("py", "dz")),
            P("px", ("py", "dz")),
        ),
        out_specs=(P("px", "dz", "py"), P(None, "px", ("py", "dz"))),
        check_vma=False,
    )
```

```python
import functools

import jax
import jax.numpy as jnp
from jax import lax
from jax.experimental import pallas as pl
from jax.experimental.pallas import tpu as pltpu
from jax.sharding import PartitionSpec as P


advect_coef = 0.25
diffuse_coef = 0.1
slope_coef = 0.5
flux_coef = 0.1
gravity = 1.0
column_height = 4.0

NPY = 4
NDZ = 4
GRP = NPY * NDZ
CX = 8
CZ = 48
CY = 256
FX = 64
FY = 256
ROWS = CX * 3 * 2
BLK = ROWS + 8
NROW = FY + 16

f32 = jnp.float32
GROUP = ("py", "dz")
VM = pl.BlockSpec(memory_space=pltpu.VMEM)
ANY = pl.BlockSpec(memory_space=pl.ANY)
PARAMS = pltpu.CompilerParams(vmem_limit_bytes=8 << 20)
HBM = pl.BlockSpec(memory_space=pltpu.HBM)


def lane_iota(shape):
    return lax.broadcasted_iota(jnp.int32, shape, len(shape) - 1)


def x_order(row):
    return 2 * row if row < 4 else 2 * (row - 4) + 1


def load_kernel(*refs):
    sources, copies, (xlo, xhi), sem = refs[:6], refs[6:12], refs[12:14], refs[14]
    moves = [(sources[0].at[:, 0], xlo), (sources[0].at[:, CX - 1], xhi), *zip(sources, copies)]
    moves = [pltpu.make_async_copy(a, b, sem.at[n]) for n, (a, b) in enumerate(moves)]
    for move in moves:
        move.start()
    for move in moves:
        move.wait()


def pack_kernel(near, owner, land, depth, flows, mask, out):
    py = lax.axis_index("py")
    dz = lax.axis_index("dz")
    me = py * NDZ + dz
    code = (owner[...] * (FX * FY) + land[...]).astype(f32)
    swap = pltpu.roll(code, 64, 1)
    odd = (me % 2) == 1
    codes = jnp.concatenate([jnp.where(odd, swap, code), jnp.where(odd, code, swap)], axis=0)
    lanes = lane_iota((8, 128))
    mine = jnp.where(odd, lanes, 127 - lanes) >= 64
    codes = jnp.where(mine, codes, 0.0)
    zero = jnp.zeros((ROWS, 128), f32)
    for b in range(GRP):
        out[b, 0:ROWS] = zero
        out[b, ROWS:BLK] = codes

    def edge(col):
        k = lane_iota((FX, 128))
        m = jnp.zeros((FX, 128), f32)
        for n, part in enumerate((depth[...], flows[0], flows[1], mask[...].astype(f32))):
            m = jnp.where(k == n, part[:, col : col + 1], m)
        turned = jnp.concatenate([m, m], axis=0).T
        return jnp.where(mine, codes, turned[0:8])

    @pl.when(me > 0)
    def _():
        out[me - 1, ROWS:BLK] = edge(0)

    @pl.when(me < GRP - 1)
    def _():
        out[me + 1, ROWS:BLK] = edge(FY - 1)

    def zface(dst, z):
        for f in range(3):
            face = near[f, :, z, :]
            for h in range(2):
                r = (f * 2 + h) * 8
                out[dst, r : r + 8] = face[:, h * 128 : (h + 1) * 128]

    def yface(dst, y):
        k = lane_iota((CZ, 128))
        m = jnp.zeros((CZ, 128), f32)
        for f in range(3):
            for x in range(CX):
                m = jnp.where(k == f * CX + x, near[f, x, :, y : y + 1], m)
        out[dst, 0:ROWS] = m

    @pl.when(dz > 0)
    def _():
        zface(me - 1, 0)

    @pl.when(dz < NDZ - 1)
    def _():
        zface(me + 1, CZ - 1)

    @pl.when(py > 0)
    def _():
        yface(me - NDZ, 0)

    @pl.when(py < NPY - 1)
    def _():
        yface(me + NDZ, CY - 1)


def near_kernel(near, got, xlow, xhigh, frac, sums):
    py = lax.axis_index("py")
    dz = lax.axis_index("dz")
    me = py * NDZ + dz
    at_l = jnp.maximum(me - NDZ, 0)
    at_r = jnp.minimum(me + NDZ, GRP - 1)
    at_d = jnp.maximum(me - 1, 0)
    at_u = jnp.minimum(me + 1, GRP - 1)
    left = jnp.where(py > 0, got[at_l, 0:ROWS], 0.0)
    right = jnp.where(py < NPY - 1, got[at_r, 0:ROWS], 0.0)
    down = jnp.where(dz > 0, got[at_d, 0:ROWS], 0.0)
    up = jnp.where(dz < NDZ - 1, got[at_u, 0:ROWS], 0.0)
    lane = lane_iota((CZ, CY))
    row = lax.broadcasted_iota(jnp.int32, (CZ, CY), 0)

    def face_row(face, f, x):
        return jnp.concatenate(
            [face[(f * 2 + h) * 8 + x : (f * 2 + h) * 8 + x + 1] for h in range(2)], axis=1
        )

    for p in range(CX):
        x = x_order(p)
        velx = near[1, x]
        vely = near[2, x]
        new = []
        for f in range(3):
            q = near[f, x]
            k = f * CX + x
            xp = near[f, x + 1] if x < CX - 1 else xhigh[f]
            xm = near[f, x - 1] if x > 0 else xlow[f]
            yp = jnp.where(lane == CY - 1, right[:, k : k + 1], pltpu.roll(q, CY - 1, 1))
            ym = jnp.where(lane == 0, left[:, k : k + 1], pltpu.roll(q, 1, 1))
            zp = jnp.where(row == CZ - 1, face_row(up, f, x), pltpu.roll(q, CZ - 1, 0))
            zm = jnp.where(row == 0, face_row(down, f, x), pltpu.roll(q, 1, 0))
            dx = xp - xm
            dy = yp - ym
            lap = xp + xm + yp + ym + zp + zm - 6.0 * q
            moved = q - advect_coef * (velx * dx + vely * dy) + diffuse_coef * lap
            if f == 0:
                fdx, fdy = dx, dy
            new.append(moved)
        frac[x] = new[0]
        parts = (
            new[0],
            new[0] * (new[1] - slope_coef * fdx),
            new[0] * (new[2] - slope_coef * fdy),
        )
        for f in range(3):
            total = jnp.sum(parts[f], axis=0, keepdims=True)
            for h in range(2):
                r = (f * 2 + h) * 8 + p
                sums[0, r : r + 1] = total[:, h * 128 : (h + 1) * 128]
    whole = sums[0]
    for b in range(1, GRP):
        sums[b] = whole


def decode(got, me, a, h):
    d = a * NDZ + 2 * h
    lanes = lane_iota((8, 128))
    code = jnp.where(lanes < 64, got[d, ROWS:BLK], got[d + 1, ROWS:BLK]).astype(jnp.int32)
    y = (code >> 14) * FY + (code & (FY - 1)) - me * FY
    y = jnp.where((y < -1) | (y > FY), -128, y)
    return y.astype(f32), ((code >> 8) & (FX - 1)).astype(f32)


def tall(row, rows):
    tile = jnp.broadcast_to(row, (16, 128)).astype(jnp.bfloat16)
    return jnp.concatenate([tile] * (rows // 16), axis=0)


def cell_rows(rows):
    r = lax.broadcasted_iota(jnp.int32, (rows, 128), 0)
    r = jnp.where(r > FY, FY - r, r)
    return r.astype(f32).astype(jnp.bfloat16)


OVER = (((1,), (1,)), ((), ()))


def split(row, rows):
    tile = jnp.broadcast_to(row, (16, 128))
    high = tile.astype(jnp.bfloat16)
    low = (tile - high.astype(f32)).astype(jnp.bfloat16)
    return [jnp.concatenate([t] * (rows // 16), axis=0) for t in (high, low)]


def edge_kernel(scale, got, sums, depth, flows, mask, total, top, bottom, bits, lhs):
    me = lax.axis_index("py") * NDZ + lax.axis_index("dz")
    row = lax.broadcasted_iota(jnp.int32, (16, 128), 0)
    part = row & 7
    field = jnp.where(part >= 3, part - 3, part)
    edge = jnp.where(part >= 3, FX - 1, 0)
    edge = jnp.where(part >= 6, -1, edge)
    edge = edge.astype(f32)
    low = row >= 8
    ycell = cell_rows(FY)
    one = jnp.ones((FY, 128), jnp.bfloat16)
    acc = jnp.zeros((16, FY), f32)
    for a in range(NPY):
        t = sums[a * NDZ]
        for b in range(1, NDZ):
            t = t + sums[a * NDZ + b]
        t = t * scale
        total[a] = t
        for h in range(2):
            y, x = decode(got, me, a, h)
            for p in range(8):
                at = slice(p * 128, (p + 1) * 128)
                bits[:, at] = jnp.where(ycell == tall(y[p : p + 1], FY), one, one * 0)
                value = None
                for f in range(3):
                    r = (f * 2 + h) * 8 + p
                    whole = jnp.broadcast_to(t[r : r + 1], (16, 128))
                    high = whole.astype(jnp.bfloat16).astype(f32)
                    both = jnp.where(low, whole - high, high)
                    value = both if f == 0 else jnp.where(field == f, both, value)
                value = jnp.where(edge == x[p : p + 1], value, 0.0)
                lhs[:, at] = value.astype(jnp.bfloat16)
            acc = acc + lax.dot_general(lhs[...], bits[...], OVER, preferred_element_type=f32)
    acc = acc[0:8] + acc[8:16]
    blank = jnp.zeros((5, FY), f32)
    for e, out in ((0, top), (1, bottom)):
        at = 0 if e == 0 else FX - 1
        wet = mask[at : at + 1].astype(f32)
        h = depth[at : at + 1] + acc[e * 3 : e * 3 + 1]
        hu = (flows[0, at : at + 1] + acc[e * 3 + 1 : e * 3 + 2]) * wet
        hv = (flows[1, at : at + 1] + acc[e * 3 + 2 : e * 3 + 3]) * wet
        out[...] = jnp.concatenate([h, hu, hv, blank], axis=0)


def terms(h, hu, hv, ok):
    inv = 1.0 / jnp.where(ok, h, 1.0)
    cross = hu * hv * inv
    press = 0.5 * gravity * h * h
    xf = (hu, hu * hu * inv + press, cross)
    yf = (hv, cross, hv * hv * inv + press)
    s = (h, hu, hv)
    return [
        (
            0.25 * s[f] - flux_coef * xf[f],
            0.25 * s[f] + flux_coef * xf[f],
            0.25 * s[f] - flux_coef * yf[f],
            0.25 * s[f] + flux_coef * yf[f],
        )
        for f in range(3)
    ]


def far_kernel(got, total, depth, flows, mask, out, head, tail, bits, ah, al):
    me = lax.axis_index("py") * NDZ + lax.axis_index("dz")
    xcell = lax.broadcasted_iota(jnp.int32, (FX, 128), 0).astype(f32).astype(jnp.bfloat16)
    ycell = cell_rows(NROW)
    one = jnp.ones((NROW, 128), jnp.bfloat16)
    zero = jnp.zeros((FX, 128), jnp.bfloat16)
    acc = jnp.zeros((NROW, 3 * FX), f32)
    for a in range(NPY):
        for h in range(2):
            y, x = decode(got, me, a, h)
            for p in range(8):
                at = slice(p * 128, (p + 1) * 128)
                bits[:, at] = jnp.where(ycell == tall(y[p : p + 1], NROW), one, one * 0)
                here = xcell == tall(x[p : p + 1], FX)
                for f in range(3):
                    r = (f * 2 + h) * 8 + p
                    high, low = split(total[a, r : r + 1], FX)
                    cells = slice(f * FX, (f + 1) * FX)
                    ah[cells, at] = jnp.where(here, high, zero)
                    al[cells, at] = jnp.where(here, low, zero)
            for part in (ah, al):
                acc = acc + lax.dot_general(bits[...], part[...], OVER, preferred_element_type=f32)
    source = acc.T
    wet = mask[...].astype(f32)
    raw = (depth[...], flows[0], flows[1])
    cells = []
    for f in range(3):
        s = raw[f] + source[f * FX : (f + 1) * FX, 0:FY]
        cells.append(s if f == 0 else s * wet)
    body = terms(*cells, True)
    sides = []
    for side in range(2):
        other = jnp.maximum(me - 1, 0) if side == 0 else jnp.minimum(me + 1, GRP - 1)
        block = got[other, ROWS:BLK]
        block = jnp.where((other % 2) == 1, block, pltpu.roll(block, 64, 1))
        e = jnp.concatenate([block] * 16, axis=0).T[0:FX]
        inside = (me > 0) if side == 0 else (me < GRP - 1)
        col = FY + 1 if side == 0 else FY
        s = []
        for f in range(3):
            v = e[:, f : f + 1] + source[f * FX : (f + 1) * FX, col : col + 1]
            v = v if f == 0 else v * e[:, 3:4]
            s.append(jnp.where(inside, v, 0.0))
        sides.append(terms(*s, inside))
    lane = lane_iota((FX, FY))
    row = lax.broadcasted_iota(jnp.int32, (FX, FY), 0)
    for f in range(3):
        xp = jnp.where(row == FX - 1, 0.0, pltpu.roll(body[f][0], FX - 1, 0))
        xm = jnp.where(row == 0, 0.0, pltpu.roll(body[f][1], 1, 0))
        yp = jnp.where(lane == FY - 1, sides[1][f][2], pltpu.roll(body[f][2], FY - 1, 1))
        ym = jnp.where(lane == 0, sides[0][f][3], pltpu.roll(body[f][3], 1, 1))
        new = (xp + xm) + (yp + ym)
        out[f] = new
        head[f] = new[0:8]
        tail[f] = new[FX - 8 : FX]


def join_kernel(part, head, tail, above, below, out, new, sem):
    px = lax.axis_index("px")
    up = terms(above[0:1], above[1:2], above[2:3], px > 0)
    dn = terms(below[0:1], below[1:2], below[2:3], px < lax.axis_size("px") - 1)
    row = lax.broadcasted_iota(jnp.int32, (8, FY), 0)
    for f in range(3):
        new[0, f] = head[f] + jnp.where(row == 0, up[f][1], 0.0)
        new[1, f] = tail[f] + jnp.where(row == 7, dn[f][0], 0.0)
    first = pltpu.make_async_copy(new.at[0], out.at[:, 0:8], sem.at[0])
    last = pltpu.make_async_copy(new.at[1], out.at[:, FX - 8 : FX], sem.at[1])
    first.start()
    last.start()
    first.wait()
    last.wait()


def shape(*dims):
    return jax.ShapeDtypeStruct(dims, f32)


def vmem(*dims):
    return pltpu.VMEM(dims, f32)


def cost(micros):
    return pl.CostEstimate(flops=0, bytes_accessed=micros * 3_000_000, transcendentals=0)


def local(near_state, column_owner, landing, far_depth, far_flows, wet_mask):
    n_px = lax.axis_size("px")
    forth = [(i, i + 1) for i in range(n_px - 1)]
    back = [(i + 1, i) for i in range(n_px - 1)]
    owner = column_owner.reshape(4, 128)
    land = landing.reshape(4, 128)
    given = (near_state, owner, land, far_depth, far_flows, wet_mask)
    *given, xlo, xhi = pl.pallas_call(
        load_kernel,
        out_shape=[pltpu.VMEM(x.shape, x.dtype) for x in given]
        + [vmem(3, CZ, CY)] * 2,
        in_specs=[HBM] * 6,
        out_specs=[VM] * 8,
        scratch_shapes=[pltpu.SemaphoreType.DMA((8,))],
        compiler_params=PARAMS,
        cost_estimate=cost(1),
        name="load",
    )(*[pltpu.with_memory_space_constraint(x, pltpu.HBM) for x in given])
    near_state, owner, land, far_depth, far_flows, wet_mask = given
    xlow = lax.ppermute(xhi, "px", forth)
    xhigh = lax.ppermute(xlo, "px", back)
    send = pl.pallas_call(
        pack_kernel,
        out_shape=shape(GRP, BLK, 128),
        in_specs=[VM] * 6,
        out_specs=VM,
        compiler_params=PARAMS,
        cost_estimate=cost(2),
        name="pack",
    )(near_state, owner, land, far_depth, far_flows, wet_mask)
    got = lax.all_to_all(send, GROUP, split_axis=0, concat_axis=0, tiled=True)
    new_frac, sums = pl.pallas_call(
        near_kernel,
        out_shape=(shape(CX, CZ, CY), shape(GRP, ROWS, 128)),
        in_specs=[VM] * 4,
        out_specs=(VM,) * 2,
        compiler_params=PARAMS,
        cost_estimate=cost(2),
        name="near",
    )(near_state, got, xlow, xhigh)
    sums = lax.all_to_all(sums, GROUP, split_axis=0, concat_axis=0, tiled=True)
    total, top, bottom = pl.pallas_call(
        functools.partial(edge_kernel, column_height / (CZ * NDZ)),
        out_shape=(vmem(NPY, ROWS, 128), vmem(8, FY), vmem(8, FY)),
        in_specs=[VM] * 5,
        out_specs=(VM,) * 3,
        scratch_shapes=[
            pltpu.VMEM((FY, 1024), jnp.bfloat16),
            pltpu.VMEM((16, 1024), jnp.bfloat16),
        ],
        compiler_params=PARAMS,
        cost_estimate=cost(2),
        name="edge",
    )(got, sums, far_depth, far_flows, wet_mask)
    above = lax.ppermute(bottom, "px", forth)
    below = lax.ppermute(top, "px", back)
    part, head, tail = pl.pallas_call(
        far_kernel,
        out_shape=(shape(3, FX, FY), vmem(3, 8, FY), vmem(3, 8, FY)),
        in_specs=[VM] * 5,
        out_specs=(VM,) * 3,
        scratch_shapes=[
            pltpu.VMEM((NROW, 1024), jnp.bfloat16),
            pltpu.VMEM((3 * FX, 1024), jnp.bfloat16),
            pltpu.VMEM((3 * FX, 1024), jnp.bfloat16),
        ],
        compiler_params=PARAMS,
        cost_estimate=cost(5),
        name="far",
    )(got, total, far_depth, far_flows, wet_mask)
    far_new = pl.pallas_call(
        join_kernel,
        out_shape=shape(3, FX, FY),
        in_specs=[ANY] + [VM] * 4,
        out_specs=ANY,
        scratch_shapes=[pltpu.VMEM((2, 3, 8, FY), f32), pltpu.SemaphoreType.DMA((2,))],
        input_output_aliases={0: 0},
        compiler_params=PARAMS,
        cost_estimate=cost(1),
        name="join",
    )(part, head, tail, above, below)
    return (new_frac, far_new)


def solution(mesh):
    return jax.shard_map(
        local,
        mesh=mesh,
        in_specs=(
            P(None, "px", "dz", "py"),
            P("px", ("py", "dz"), None, None),
            P("px", ("py", "dz"), None),
            P("px", ("py", "dz")),
            P(None, "px", ("py", "dz")),
            P("px", ("py", "dz")),
        ),
        out_specs=(P("px", "dz", "py"), P(None, "px", ("py", "dz"))),
        check_vma=False,
    )
```

```python
import functools

import jax
import jax.numpy as jnp
from jax import lax
from jax.experimental import pallas as pl
from jax.experimental.pallas import tpu as pltpu
from jax.sharding import PartitionSpec as P


advect_coef = 0.25
diffuse_coef = 0.1
slope_coef = 0.5
flux_coef = 0.1
gravity = 1.0
column_height = 4.0

NPY = 4
NDZ = 4
GRP = NPY * NDZ
CX = 8
CZ = 48
CY = 256
FX = 64
FY = 256
ROWS = CX * 3 * 2
BLK = ROWS + 8

f32 = jnp.float32
GROUP = ("py", "dz")
VM = pl.BlockSpec(memory_space=pltpu.VMEM)
ANY = pl.BlockSpec(memory_space=pl.ANY)
PARAMS = pltpu.CompilerParams(vmem_limit_bytes=8 << 20)
HBM = pl.BlockSpec(memory_space=pltpu.HBM)


def lane_iota(shape):
    return lax.broadcasted_iota(jnp.int32, shape, len(shape) - 1)


def x_order(row):
    return 2 * row if row < 4 else 2 * (row - 4) + 1


def load_kernel(*refs):
    sources, copies, (xlo, xhi), sem = refs[:6], refs[6:12], refs[12:14], refs[14]
    moves = [(sources[0].at[:, 0], xlo), (sources[0].at[:, CX - 1], xhi), *zip(sources, copies)]
    moves = [pltpu.make_async_copy(a, b, sem.at[n]) for n, (a, b) in enumerate(moves)]
    for move in moves:
        move.start()
    for move in moves:
        move.wait()


def pack_kernel(near, owner, land, depth, flows, mask, out):
    py = lax.axis_index("py")
    dz = lax.axis_index("dz")
    me = py * NDZ + dz
    code = (owner[...] * (FX * FY) + land[...]).astype(f32)
    swap = pltpu.roll(code, 64, 1)
    odd = (me % 2) == 1
    codes = jnp.concatenate([jnp.where(odd, swap, code), jnp.where(odd, code, swap)], axis=0)
    lanes = lane_iota((8, 128))
    mine = jnp.where(odd, lanes, 127 - lanes) >= 64
    codes = jnp.where(mine, codes, 0.0)
    zero = jnp.zeros((ROWS, 128), f32)
    for b in range(GRP):
        out[b, 0:ROWS] = zero
        out[b, ROWS:BLK] = codes

    def edge(col):
        k = lane_iota((FX, 128))
        m = jnp.zeros((FX, 128), f32)
        for n, part in enumerate((depth[...], flows[0], flows[1], mask[...].astype(f32))):
            m = jnp.where(k == n, part[:, col : col + 1], m)
        turned = jnp.concatenate([m, m], axis=0).T
        return jnp.where(mine, codes, turned[0:8])

    @pl.when(me > 0)
    def _():
        out[me - 1, ROWS:BLK] = edge(0)

    @pl.when(me < GRP - 1)
    def _():
        out[me + 1, ROWS:BLK] = edge(FY - 1)

    def zface(dst, z):
        for f in range(3):
            face = near[f, :, z, :]
            for h in range(2):
                r = (f * 2 + h) * 8
                out[dst, r : r + 8] = face[:, h * 128 : (h + 1) * 128]

    def yface(dst, y):
        k = lane_iota((CZ, 128))
        m = jnp.zeros((CZ, 128), f32)
        for f in range(3):
            for x in range(CX):
                m = jnp.where(k == f * CX + x, near[f, x, :, y : y + 1], m)
        out[dst, 0:ROWS] = m

    @pl.when(dz > 0)
    def _():
        zface(me - 1, 0)

    @pl.when(dz < NDZ - 1)
    def _():
        zface(me + 1, CZ - 1)

    @pl.when(py > 0)
    def _():
        yface(me - NDZ, 0)

    @pl.when(py < NPY - 1)
    def _():
        yface(me + NDZ, CY - 1)


def near_kernel(near, got, xlow, xhigh, frac, sums):
    py = lax.axis_index("py")
    dz = lax.axis_index("dz")
    me = py * NDZ + dz
    at_l = jnp.maximum(me - NDZ, 0)
    at_r = jnp.minimum(me + NDZ, GRP - 1)
    at_d = jnp.maximum(me - 1, 0)
    at_u = jnp.minimum(me + 1, GRP - 1)
    left = jnp.where(py > 0, got[at_l, 0:ROWS], 0.0)
    right = jnp.where(py < NPY - 1, got[at_r, 0:ROWS], 0.0)
    down = jnp.where(dz > 0, got[at_d, 0:ROWS], 0.0)
    up = jnp.where(dz < NDZ - 1, got[at_u, 0:ROWS], 0.0)
    lane = lane_iota((CZ, CY))
    row = lax.broadcasted_iota(jnp.int32, (CZ, CY), 0)

    def face_row(face, f, x):
        return jnp.concatenate(
            [face[(f * 2 + h) * 8 + x : (f * 2 + h) * 8 + x + 1] for h in range(2)], axis=1
        )

    for p in range(CX):
        x = x_order(p)
        velx = near[1, x]
        vely = near[2, x]
        new = []
        for f in range(3):
            q = near[f, x]
            k = f * CX + x
            xp = near[f, x + 1] if x < CX - 1 else xhigh[f]
            xm = near[f, x - 1] if x > 0 else xlow[f]
            yp = jnp.where(lane == CY - 1, right[:, k : k + 1], pltpu.roll(q, CY - 1, 1))
            ym = jnp.where(lane == 0, left[:, k : k + 1], pltpu.roll(q, 1, 1))
            zp = jnp.where(row == CZ - 1, face_row(up, f, x), pltpu.roll(q, CZ - 1, 0))
            zm = jnp.where(row == 0, face_row(down, f, x), pltpu.roll(q, 1, 0))
            dx = xp - xm
            dy = yp - ym
            lap = xp + xm + yp + ym + zp + zm - 6.0 * q
            moved = q - advect_coef * (velx * dx + vely * dy) + diffuse_coef * lap
            if f == 0:
                fdx, fdy = dx, dy
            new.append(moved)
        frac[x] = new[0]
        parts = (
            new[0],
            new[0] * (new[1] - slope_coef * fdx),
            new[0] * (new[2] - slope_coef * fdy),
        )
        for f in range(3):
            total = jnp.sum(parts[f], axis=0, keepdims=True)
            for h in range(2):
                r = (f * 2 + h) * 8 + p
                sums[0, r : r + 1] = total[:, h * 128 : (h + 1) * 128]
    whole = sums[0]
    for b in range(1, GRP):
        sums[b] = whole


def decode(got, me, a, h):
    d = a * NDZ + 2 * h
    lanes = lane_iota((8, 128))
    code = jnp.where(lanes < 64, got[d, ROWS:BLK], got[d + 1, ROWS:BLK]).astype(jnp.int32)
    y = (code >> 14) * FY + (code & (FY - 1)) - me * FY
    y = jnp.where((y < -1) | (y > FY), -128, y)
    return y.astype(f32), ((code >> 8) & (FX - 1)).astype(f32)


def tall(row, rows):
    tile = jnp.broadcast_to(row, (16, 128)).astype(jnp.bfloat16)
    return jnp.concatenate([tile] * (rows // 16), axis=0)


def cell_rows(rows):
    return lax.broadcasted_iota(jnp.int32, (rows, 128), 0).astype(f32).astype(jnp.bfloat16)


OVER = (((1,), (1,)), ((), ()))


def spread(parts, wide):
    for m, part in enumerate(parts):
        wide[m * 8 : m * 8 + 8] = part


def gathered(wide, p):
    return wide[pl.ds(p, 16, stride=8), :].astype(jnp.bfloat16)


def pairs(build):
    for p in range(0, 8, 2):
        yield [jnp.concatenate(two, axis=1) for two in zip(build(p), build(p + 1))]


def edge_kernel(scale, got, sums, depth, flows, mask, pieces, top, bottom, wide):
    me = lax.axis_index("py") * NDZ + lax.axis_index("dz")
    ycell = cell_rows(FY)
    one = jnp.ones((FY, 128), jnp.bfloat16)
    zero = jnp.zeros((8, 128), f32)
    acc = jnp.zeros((16, FY), f32)
    for a in range(NPY):
        t = sums[a * NDZ]
        for b in range(1, NDZ):
            t = t + sums[a * NDZ + b]
        t = t * scale
        high = t.astype(jnp.bfloat16).astype(f32)
        low = t - high
        pieces[0, a] = high
        pieces[1, a] = low
        for h in range(2):
            g = a * 2 + h
            y, x = decode(got, me, a, h)
            rows = []
            for part in (high, low):
                for cell in (0, FX - 1):
                    for f in range(3):
                        r = (f * 2 + h) * 8
                        rows.append(jnp.where(x == cell, part[r : r + 8], 0.0))
                rows += [zero, zero]
            spread(rows, wide.at[g])

            def build(p):
                bits = jnp.where(ycell == tall(y[p : p + 1], FY), one, one * 0)
                return gathered(wide.at[g], p), bits

            for lhs, bits in pairs(build):
                acc = acc + lax.dot_general(lhs, bits, OVER, preferred_element_type=f32)
    acc = acc[0:8] + acc[8:16]
    blank = jnp.zeros((5, FY), f32)
    for e, out in ((0, top), (1, bottom)):
        at = 0 if e == 0 else FX - 1
        wet = mask[at : at + 1].astype(f32)
        h = depth[at : at + 1] + acc[e * 3 : e * 3 + 1]
        hu = (flows[0, at : at + 1] + acc[e * 3 + 1 : e * 3 + 2]) * wet
        hv = (flows[1, at : at + 1] + acc[e * 3 + 2 : e * 3 + 3]) * wet
        out[...] = jnp.concatenate([h, hu, hv, blank], axis=0)


def terms(h, hu, hv, ok):
    inv = 1.0 / jnp.where(ok, h, 1.0)
    cross = hu * hv * inv
    press = 0.5 * gravity * h * h
    xf = (hu, hu * hu * inv + press, cross)
    yf = (hv, cross, hv * hv * inv + press)
    s = (h, hu, hv)
    return [
        (
            0.25 * s[f] - flux_coef * xf[f],
            0.25 * s[f] + flux_coef * xf[f],
            0.25 * s[f] - flux_coef * yf[f],
            0.25 * s[f] + flux_coef * yf[f],
        )
        for f in range(3)
    ]


def far_kernel(
    got, pieces, depth, flows, mask, out, head, tail, wide
):
    me = lax.axis_index("py") * NDZ + lax.axis_index("dz")
    xcell = cell_rows(FX)
    ycell = cell_rows(FY)
    one = jnp.ones((FY, 128), jnp.bfloat16)
    none = jnp.zeros((FX, 128), jnp.bfloat16)
    zero = jnp.zeros((8, 128), f32)
    acc = jnp.zeros((6 * FX, FY), f32)
    side = jnp.zeros((16, FX), f32)
    for a in range(NPY):
        for h in range(2):
            g = a * 2 + h
            y, x = decode(got, me, a, h)
            rows = []
            for n in range(2):
                for cell in (-1, FY):
                    for f in range(3):
                        r = (f * 2 + h) * 8
                        rows.append(jnp.where(y == cell, pieces[n, a, r : r + 8], 0.0))
                rows += [zero, zero]
            spread(rows, wide.at[g])

            def build(p):
                bits = jnp.where(ycell == tall(y[p : p + 1], FY), one, one * 0)
                here = xcell == tall(x[p : p + 1], FX)
                parts = []
                for n in range(2):
                    for f in range(3):
                        r = (f * 2 + h) * 8 + p
                        value = tall(pieces[n, a, r : r + 1], FX)
                        parts.append(jnp.where(here, value, none))
                xbits = jnp.where(here, one[0:FX], none)
                return jnp.concatenate(parts, axis=0), bits, gathered(wide.at[g], p), xbits

            for lhs, bits, side_lhs, xbits in pairs(build):
                acc = acc + lax.dot_general(lhs, bits, OVER, preferred_element_type=f32)
                side = side + lax.dot_general(side_lhs, xbits, OVER, preferred_element_type=f32)
    source = acc[0 : 3 * FX] + acc[3 * FX :]
    side = side[0:8] + side[8:16]
    side = jnp.concatenate([side] * 16, axis=0)
    side = jnp.concatenate([side, side], axis=1).T
    wet = mask[...].astype(f32)
    raw = (depth[...], flows[0], flows[1])
    cells = []
    for f in range(3):
        s = raw[f] + source[f * FX : (f + 1) * FX]
        cells.append(s if f == 0 else s * wet)
    body = terms(*cells, True)
    sides = []
    for n in range(2):
        other = jnp.maximum(me - 1, 0) if n == 0 else jnp.minimum(me + 1, GRP - 1)
        block = got[other, ROWS:BLK]
        block = jnp.where((other % 2) == 1, block, pltpu.roll(block, 64, 1))
        e = jnp.concatenate([block] * 16, axis=0).T[0:FX]
        inside = (me > 0) if n == 0 else (me < GRP - 1)
        s = []
        for f in range(3):
            col = n * 3 + f
            v = e[:, f : f + 1] + side[0:FX, col : col + 1]
            v = v if f == 0 else v * e[:, 3:4]
            s.append(jnp.where(inside, v, 0.0))
        sides.append(terms(*s, inside))
    lane = lane_iota((FX, FY))
    row = lax.broadcasted_iota(jnp.int32, (FX, FY), 0)
    for f in range(3):
        xp = jnp.where(row == FX - 1, 0.0, pltpu.roll(body[f][0], FX - 1, 0))
        xm = jnp.where(row == 0, 0.0, pltpu.roll(body[f][1], 1, 0))
        yp = jnp.where(lane == FY - 1, sides[1][f][2], pltpu.roll(body[f][2], FY - 1, 1))
        ym = jnp.where(lane == 0, sides[0][f][3], pltpu.roll(body[f][3], 1, 1))
        new = (xp + xm) + (yp + ym)
        out[f] = new
        head[f] = new[0:8]
        tail[f] = new[FX - 8 : FX]


def join_kernel(part, head, tail, above, below, out, new, sem):
    px = lax.axis_index("px")
    up = terms(above[0:1], above[1:2], above[2:3], px > 0)
    dn = terms(below[0:1], below[1:2], below[2:3], px < lax.axis_size("px") - 1)
    row = lax.broadcasted_iota(jnp.int32, (8, FY), 0)
    for f in range(3):
        new[0, f] = head[f] + jnp.where(row == 0, up[f][1], 0.0)
        new[1, f] = tail[f] + jnp.where(row == 7, dn[f][0], 0.0)
    first = pltpu.make_async_copy(new.at[0], out.at[:, 0:8], sem.at[0])
    last = pltpu.make_async_copy(new.at[1], out.at[:, FX - 8 : FX], sem.at[1])
    first.start()
    last.start()
    first.wait()
    last.wait()


def shape(*dims):
    return jax.ShapeDtypeStruct(dims, f32)


def vmem(*dims):
    return pltpu.VMEM(dims, f32)


def cost(micros):
    return pl.CostEstimate(flops=0, bytes_accessed=micros * 3_000_000, transcendentals=0)


def local(near_state, column_owner, landing, far_depth, far_flows, wet_mask):
    n_px = lax.axis_size("px")
    forth = [(i, i + 1) for i in range(n_px - 1)]
    back = [(i + 1, i) for i in range(n_px - 1)]
    owner = column_owner.reshape(4, 128)
    land = landing.reshape(4, 128)
    given = (near_state, owner, land, far_depth, far_flows, wet_mask)
    *given, xlo, xhi = pl.pallas_call(
        load_kernel,
        out_shape=[pltpu.VMEM(x.shape, x.dtype) for x in given]
        + [vmem(3, CZ, CY)] * 2,
        in_specs=[HBM] * 6,
        out_specs=[VM] * 8,
        scratch_shapes=[pltpu.SemaphoreType.DMA((8,))],
        compiler_params=PARAMS,
        cost_estimate=cost(1),
        name="load",
    )(*[pltpu.with_memory_space_constraint(x, pltpu.HBM) for x in given])
    near_state, owner, land, far_depth, far_flows, wet_mask = given
    xlow = lax.ppermute(xhi, "px", forth)
    xhigh = lax.ppermute(xlo, "px", back)
    send = pl.pallas_call(
        pack_kernel,
        out_shape=shape(GRP, BLK, 128),
        in_specs=[VM] * 6,
        out_specs=VM,
        compiler_params=PARAMS,
        cost_estimate=cost(2),
        name="pack",
    )(near_state, owner, land, far_depth, far_flows, wet_mask)
    got = lax.all_to_all(send, GROUP, split_axis=0, concat_axis=0, tiled=True)
    new_frac, sums = pl.pallas_call(
        near_kernel,
        out_shape=(shape(CX, CZ, CY), shape(GRP, ROWS, 128)),
        in_specs=[VM] * 4,
        out_specs=(VM,) * 2,
        compiler_params=PARAMS,
        cost_estimate=cost(2),
        name="near",
    )(near_state, got, xlow, xhigh)
    sums = lax.all_to_all(sums, GROUP, split_axis=0, concat_axis=0, tiled=True)
    pieces, top, bottom = pl.pallas_call(
        functools.partial(edge_kernel, column_height / (CZ * NDZ)),
        out_shape=(vmem(2, NPY, ROWS, 128), vmem(8, FY), vmem(8, FY)),
        in_specs=[VM] * 5,
        out_specs=(VM,) * 3,
        scratch_shapes=[vmem(8, 128, 128)],
        compiler_params=PARAMS,
        cost_estimate=cost(2),
        name="edge",
    )(got, sums, far_depth, far_flows, wet_mask)
    above = lax.ppermute(bottom, "px", forth)
    below = lax.ppermute(top, "px", back)
    part, head, tail = pl.pallas_call(
        far_kernel,
        out_shape=(shape(3, FX, FY), vmem(3, 8, FY), vmem(3, 8, FY)),
        in_specs=[VM] * 5,
        out_specs=(VM,) * 3,
        scratch_shapes=[vmem(8, 128, 128)],
        compiler_params=pltpu.CompilerParams(vmem_limit_bytes=20 << 20),
        cost_estimate=cost(5),
        name="far",
    )(got, pieces, far_depth, far_flows, wet_mask)
    far_new = pl.pallas_call(
        join_kernel,
        out_shape=shape(3, FX, FY),
        in_specs=[ANY] + [VM] * 4,
        out_specs=ANY,
        scratch_shapes=[pltpu.VMEM((2, 3, 8, FY), f32), pltpu.SemaphoreType.DMA((2,))],
        input_output_aliases={0: 0},
        compiler_params=PARAMS,
        cost_estimate=cost(1),
        name="join",
    )(part, head, tail, above, below)
    return (new_frac, far_new)


def solution(mesh):
    return jax.shard_map(
        local,
        mesh=mesh,
        in_specs=(
            P(None, "px", "dz", "py"),
            P("px", ("py", "dz"), None, None),
            P("px", ("py", "dz"), None),
            P("px", ("py", "dz")),
            P(None, "px", ("py", "dz")),
            P("px", ("py", "dz")),
        ),
        out_specs=(P("px", "dz", "py"), P(None, "px", ("py", "dz"))),
        check_vma=False,
    )
```

```python
import functools

import jax
import jax.numpy as jnp
from jax import lax
from jax.experimental import pallas as pl
from jax.experimental.pallas import tpu as pltpu
from jax.sharding import PartitionSpec as P


advect_coef = 0.25
diffuse_coef = 0.1
slope_coef = 0.5
flux_coef = 0.1
gravity = 1.0
column_height = 4.0

NPY = 4
NDZ = 4
GRP = NPY * NDZ
CX = 8
CZ = 48
CY = 256
FX = 64
FY = 256
ROWS = CX * 3 * 2
SIDE = CZ // 3
BLK = SIDE + 8

f32 = jnp.float32
GROUP = ("py", "dz")
VM = pl.BlockSpec(memory_space=pltpu.VMEM)
ANY = pl.BlockSpec(memory_space=pl.ANY)
PARAMS = pltpu.CompilerParams(vmem_limit_bytes=8 << 20)
HBM = pl.BlockSpec(memory_space=pltpu.HBM)


def lane_iota(shape):
    return lax.broadcasted_iota(jnp.int32, shape, len(shape) - 1)


def x_order(row):
    return 2 * row if row < 4 else 2 * (row - 4) + 1


def load_kernel(*refs):
    sources, copies, (xlo, xhi), sem = refs[:6], refs[6:12], refs[12:14], refs[14]
    moves = [(sources[0].at[:, 0], xlo), (sources[0].at[:, CX - 1], xhi), *zip(sources, copies)]
    moves = [pltpu.make_async_copy(a, b, sem.at[n]) for n, (a, b) in enumerate(moves)]
    for move in moves:
        move.start()
    for move in moves:
        move.wait()


def pack_kernel(near, owner, land, depth, flows, mask, out, zlo, zhi):
    py = lax.axis_index("py")
    dz = lax.axis_index("dz")
    me = py * NDZ + dz
    code = (owner[...] * (FX * FY) + land[...]).astype(f32)
    swap = pltpu.roll(code, 64, 1)
    odd = (me % 2) == 1
    codes = jnp.concatenate([jnp.where(odd, swap, code), jnp.where(odd, code, swap)], axis=0)
    lanes = lane_iota((8, 128))
    mine = jnp.where(odd, lanes, 127 - lanes) >= 64
    codes = jnp.where(mine, codes, 0.0)
    zero = jnp.zeros((SIDE, 128), f32)
    for b in range(GRP):
        out[b, 0:SIDE] = zero
        out[b, SIDE:BLK] = codes

    def edge(col):
        k = lane_iota((FX, 128))
        m = jnp.zeros((FX, 128), f32)
        for n, part in enumerate((depth[...], flows[0], flows[1], mask[...].astype(f32))):
            m = jnp.where(k == n, part[:, col : col + 1], m)
        turned = jnp.concatenate([m, m], axis=0).T
        return jnp.where(mine, codes, turned[0:8])

    @pl.when(me > 0)
    def _():
        out[me - 1, SIDE:BLK] = edge(0)

    @pl.when(me < GRP - 1)
    def _():
        out[me + 1, SIDE:BLK] = edge(FY - 1)

    for f in range(3):
        zlo[f] = near[f, :, 0, :]
        zhi[f] = near[f, :, CZ - 1, :]

    def yface(dst, y):
        k = lane_iota((CZ, 128))
        m = jnp.zeros((CZ, 128), f32)
        for f in range(3):
            for x in range(CX):
                m = jnp.where(k == f * CX + x, near[f, x, :, y : y + 1], m)
        layers = [pltpu.roll(m[SIDE * n : SIDE * (n + 1)], 32 * n, 1) for n in range(3)]
        out[dst, 0:SIDE] = layers[0] + layers[1] + layers[2]

    @pl.when(py > 0)
    def _():
        yface(me - NDZ, 0)

    @pl.when(py < NPY - 1)
    def _():
        yface(me + NDZ, CY - 1)


def near_kernel(near, got, xlow, xhigh, down, up, frac, sums):
    py = lax.axis_index("py")
    me = py * NDZ + lax.axis_index("dz")

    def yface(at, inside):
        m = jnp.where(inside, got[at, 0:SIDE], 0.0)
        return jnp.concatenate([m] + [pltpu.roll(m, 128 - 32 * n, 1) for n in (1, 2)], axis=0)

    left = yface(jnp.maximum(me - NDZ, 0), py > 0)
    right = yface(jnp.minimum(me + NDZ, GRP - 1), py < NPY - 1)
    lane = lane_iota((CZ, CY))
    row = lax.broadcasted_iota(jnp.int32, (CZ, CY), 0)

    for p in range(CX):
        x = x_order(p)
        velx = near[1, x]
        vely = near[2, x]
        new = []
        for f in range(3):
            q = near[f, x]
            k = f * CX + x
            xp = near[f, x + 1] if x < CX - 1 else xhigh[f]
            xm = near[f, x - 1] if x > 0 else xlow[f]
            yp = jnp.where(lane == CY - 1, right[:, k : k + 1], pltpu.roll(q, CY - 1, 1))
            ym = jnp.where(lane == 0, left[:, k : k + 1], pltpu.roll(q, 1, 1))
            zp = jnp.where(row == CZ - 1, up[f, x : x + 1], pltpu.roll(q, CZ - 1, 0))
            zm = jnp.where(row == 0, down[f, x : x + 1], pltpu.roll(q, 1, 0))
            dx = xp - xm
            dy = yp - ym
            lap = xp + xm + yp + ym + zp + zm - 6.0 * q
            moved = q - advect_coef * (velx * dx + vely * dy) + diffuse_coef * lap
            if f == 0:
                fdx, fdy = dx, dy
            new.append(moved)
        frac[x] = new[0]
        parts = (
            new[0],
            new[0] * (new[1] - slope_coef * fdx),
            new[0] * (new[2] - slope_coef * fdy),
        )
        for f in range(3):
            total = jnp.sum(parts[f], axis=0, keepdims=True)
            for h in range(2):
                r = (f * 2 + h) * 8 + p
                sums[0, r : r + 1] = total[:, h * 128 : (h + 1) * 128]
    whole = sums[0]
    for b in range(1, GRP):
        sums[b] = whole


def decode(got, me, a, h):
    d = a * NDZ + 2 * h
    lanes = lane_iota((8, 128))
    code = jnp.where(lanes < 64, got[d, SIDE:BLK], got[d + 1, SIDE:BLK]).astype(jnp.int32)
    y = (code >> 14) * FY + (code & (FY - 1)) - me * FY
    y = jnp.where((y < -1) | (y > FY), -128, y)
    return y.astype(f32), ((code >> 8) & (FX - 1)).astype(f32)


def tall(row, rows):
    tile = jnp.broadcast_to(row, (16, 128)).astype(jnp.bfloat16)
    return jnp.concatenate([tile] * (rows // 16), axis=0)


def cell_rows(rows):
    return lax.broadcasted_iota(jnp.int32, (rows, 128), 0).astype(f32).astype(jnp.bfloat16)


OVER = (((1,), (1,)), ((), ()))


def spread(parts, wide):
    for m, part in enumerate(parts):
        wide[m * 8 : m * 8 + 8] = part


def gathered(wide, p):
    return wide[pl.ds(p, 16, stride=8), :].astype(jnp.bfloat16)


def pairs(build):
    for p in range(0, 8, 2):
        yield [jnp.concatenate(two, axis=1) for two in zip(build(p), build(p + 1))]


def edge_kernel(scale, got, sums, depth, flows, mask, pieces, top, bottom, wide):
    me = lax.axis_index("py") * NDZ + lax.axis_index("dz")
    ycell = cell_rows(FY)
    one = jnp.ones((FY, 128), jnp.bfloat16)
    zero = jnp.zeros((8, 128), f32)
    acc = jnp.zeros((16, FY), f32)
    for a in range(NPY):
        t = sums[a * NDZ]
        for b in range(1, NDZ):
            t = t + sums[a * NDZ + b]
        t = t * scale
        high = t.astype(jnp.bfloat16).astype(f32)
        low = t - high
        pieces[0, a] = high
        pieces[1, a] = low
        for h in range(2):
            g = a * 2 + h
            y, x = decode(got, me, a, h)
            rows = []
            for part in (high, low):
                for cell in (0, FX - 1):
                    for f in range(3):
                        r = (f * 2 + h) * 8
                        rows.append(jnp.where(x == cell, part[r : r + 8], 0.0))
                rows += [zero, zero]
            spread(rows, wide.at[g])

            def build(p):
                bits = jnp.where(ycell == tall(y[p : p + 1], FY), one, one * 0)
                return gathered(wide.at[g], p), bits

            for lhs, bits in pairs(build):
                acc = acc + lax.dot_general(lhs, bits, OVER, preferred_element_type=f32)
    acc = acc[0:8] + acc[8:16]
    blank = jnp.zeros((5, FY), f32)
    for e, out in ((0, top), (1, bottom)):
        at = 0 if e == 0 else FX - 1
        wet = mask[at : at + 1].astype(f32)
        h = depth[at : at + 1] + acc[e * 3 : e * 3 + 1]
        hu = (flows[0, at : at + 1] + acc[e * 3 + 1 : e * 3 + 2]) * wet
        hv = (flows[1, at : at + 1] + acc[e * 3 + 2 : e * 3 + 3]) * wet
        out[...] = jnp.concatenate([h, hu, hv, blank], axis=0)


def terms(h, hu, hv, ok):
    inv = 1.0 / jnp.where(ok, h, 1.0)
    cross = hu * hv * inv
    press = 0.5 * gravity * h * h
    xf = (hu, hu * hu * inv + press, cross)
    yf = (hv, cross, hv * hv * inv + press)
    s = (h, hu, hv)
    return [
        (
            0.25 * s[f] - flux_coef * xf[f],
            0.25 * s[f] + flux_coef * xf[f],
            0.25 * s[f] - flux_coef * yf[f],
            0.25 * s[f] + flux_coef * yf[f],
        )
        for f in range(3)
    ]


def far_kernel(
    got, pieces, depth, flows, mask, out, head, tail, wide
):
    me = lax.axis_index("py") * NDZ + lax.axis_index("dz")
    xcell = cell_rows(FX)
    ycell = cell_rows(FY)
    one = jnp.ones((FY, 128), jnp.bfloat16)
    none = jnp.zeros((FX, 128), jnp.bfloat16)
    zero = jnp.zeros((8, 128), f32)
    acc = jnp.zeros((6 * FX, FY), f32)
    side = jnp.zeros((16, FX), f32)
    for a in range(NPY):
        for h in range(2):
            g = a * 2 + h
            y, x = decode(got, me, a, h)
            rows = []
            for n in range(2):
                for cell in (-1, FY):
                    for f in range(3):
                        r = (f * 2 + h) * 8
                        rows.append(jnp.where(y == cell, pieces[n, a, r : r + 8], 0.0))
                rows += [zero, zero]
            spread(rows, wide.at[g])

            def build(p):
                bits = jnp.where(ycell == tall(y[p : p + 1], FY), one, one * 0)
                here = xcell == tall(x[p : p + 1], FX)
                parts = []
                for n in range(2):
                    for f in range(3):
                        r = (f * 2 + h) * 8 + p
                        value = tall(pieces[n, a, r : r + 1], FX)
                        parts.append(jnp.where(here, value, none))
                xbits = jnp.where(here, one[0:FX], none)
                return jnp.concatenate(parts, axis=0), bits, gathered(wide.at[g], p), xbits

            for lhs, bits, side_lhs, xbits in pairs(build):
                acc = acc + lax.dot_general(lhs, bits, OVER, preferred_element_type=f32)
                side = side + lax.dot_general(side_lhs, xbits, OVER, preferred_element_type=f32)
    source = acc[0 : 3 * FX] + acc[3 * FX :]
    side = side[0:8] + side[8:16]
    side = jnp.concatenate([side] * 16, axis=0)
    side = jnp.concatenate([side, side], axis=1).T
    wet = mask[...].astype(f32)
    raw = (depth[...], flows[0], flows[1])
    cells = []
    for f in range(3):
        s = raw[f] + source[f * FX : (f + 1) * FX]
        cells.append(s if f == 0 else s * wet)
    body = terms(*cells, True)
    sides = []
    for n in range(2):
        other = jnp.maximum(me - 1, 0) if n == 0 else jnp.minimum(me + 1, GRP - 1)
        block = got[other, SIDE:BLK]
        block = jnp.where((other % 2) == 1, block, pltpu.roll(block, 64, 1))
        e = jnp.concatenate([block] * 16, axis=0).T[0:FX]
        inside = (me > 0) if n == 0 else (me < GRP - 1)
        s = []
        for f in range(3):
            col = n * 3 + f
            v = e[:, f : f + 1] + side[0:FX, col : col + 1]
            v = v if f == 0 else v * e[:, 3:4]
            s.append(jnp.where(inside, v, 0.0))
        sides.append(terms(*s, inside))
    lane = lane_iota((FX, FY))
    row = lax.broadcasted_iota(jnp.int32, (FX, FY), 0)
    for f in range(3):
        xp = jnp.where(row == FX - 1, 0.0, pltpu.roll(body[f][0], FX - 1, 0))
        xm = jnp.where(row == 0, 0.0, pltpu.roll(body[f][1], 1, 0))
        yp = jnp.where(lane == FY - 1, sides[1][f][2], pltpu.roll(body[f][2], FY - 1, 1))
        ym = jnp.where(lane == 0, sides[0][f][3], pltpu.roll(body[f][3], 1, 1))
        new = (xp + xm) + (yp + ym)
        out[f] = new
        head[f] = new[0:8]
        tail[f] = new[FX - 8 : FX]


def join_kernel(part, head, tail, above, below, out, new, sem):
    px = lax.axis_index("px")
    up = terms(above[0:1], above[1:2], above[2:3], px > 0)
    dn = terms(below[0:1], below[1:2], below[2:3], px < lax.axis_size("px") - 1)
    row = lax.broadcasted_iota(jnp.int32, (8, FY), 0)
    for f in range(3):
        new[0, f] = head[f] + jnp.where(row == 0, up[f][1], 0.0)
        new[1, f] = tail[f] + jnp.where(row == 7, dn[f][0], 0.0)
    first = pltpu.make_async_copy(new.at[0], out.at[:, 0:8], sem.at[0])
    last = pltpu.make_async_copy(new.at[1], out.at[:, FX - 8 : FX], sem.at[1])
    first.start()
    last.start()
    first.wait()
    last.wait()


def shape(*dims):
    return jax.ShapeDtypeStruct(dims, f32)


def vmem(*dims):
    return pltpu.VMEM(dims, f32)


def cost(micros):
    return pl.CostEstimate(flops=0, bytes_accessed=micros * 3_000_000, transcendentals=0)


def local(near_state, column_owner, landing, far_depth, far_flows, wet_mask):
    n_px = lax.axis_size("px")
    forth = [(i, i + 1) for i in range(n_px - 1)]
    back = [(i + 1, i) for i in range(n_px - 1)]
    owner = column_owner.reshape(4, 128)
    land = landing.reshape(4, 128)
    given = (near_state, owner, land, far_depth, far_flows, wet_mask)
    *given, xlo, xhi = pl.pallas_call(
        load_kernel,
        out_shape=[pltpu.VMEM(x.shape, x.dtype) for x in given]
        + [vmem(3, CZ, CY)] * 2,
        in_specs=[HBM] * 6,
        out_specs=[VM] * 8,
        scratch_shapes=[pltpu.SemaphoreType.DMA((8,))],
        compiler_params=PARAMS,
        cost_estimate=cost(1),
        name="load",
    )(*[pltpu.with_memory_space_constraint(x, pltpu.HBM) for x in given])
    near_state, owner, land, far_depth, far_flows, wet_mask = given
    xlow = lax.ppermute(xhi, "px", forth)
    xhigh = lax.ppermute(xlo, "px", back)
    send, zlo, zhi = pl.pallas_call(
        pack_kernel,
        out_shape=(shape(GRP, BLK, 128), vmem(3, CX, CY), vmem(3, CX, CY)),
        in_specs=[VM] * 6,
        out_specs=(VM,) * 3,
        compiler_params=PARAMS,
        cost_estimate=cost(2),
        name="pack",
    )(near_state, owner, land, far_depth, far_flows, wet_mask)
    got = lax.all_to_all(send, GROUP, split_axis=0, concat_axis=0, tiled=True)
    down = lax.ppermute(zhi, "dz", [(i, i + 1) for i in range(NDZ - 1)])
    up = lax.ppermute(zlo, "dz", [(i + 1, i) for i in range(NDZ - 1)])
    new_frac, sums = pl.pallas_call(
        near_kernel,
        out_shape=(shape(CX, CZ, CY), shape(GRP, ROWS, 128)),
        in_specs=[VM] * 6,
        out_specs=(VM,) * 2,
        compiler_params=PARAMS,
        cost_estimate=cost(2),
        name="near",
    )(near_state, got, xlow, xhigh, down, up)
    sums = lax.all_to_all(sums, GROUP, split_axis=0, concat_axis=0, tiled=True)
    pieces, top, bottom = pl.pallas_call(
        functools.partial(edge_kernel, column_height / (CZ * NDZ)),
        out_shape=(vmem(2, NPY, ROWS, 128), vmem(8, FY), vmem(8, FY)),
        in_specs=[VM] * 5,
        out_specs=(VM,) * 3,
        scratch_shapes=[vmem(8, 128, 128)],
        compiler_params=PARAMS,
        cost_estimate=cost(2),
        name="edge",
    )(got, sums, far_depth, far_flows, wet_mask)
    above = lax.ppermute(bottom, "px", forth)
    below = lax.ppermute(top, "px", back)
    part, head, tail = pl.pallas_call(
        far_kernel,
        out_shape=(shape(3, FX, FY), vmem(3, 8, FY), vmem(3, 8, FY)),
        in_specs=[VM] * 5,
        out_specs=(VM,) * 3,
        scratch_shapes=[vmem(8, 128, 128)],
        compiler_params=pltpu.CompilerParams(vmem_limit_bytes=20 << 20),
        cost_estimate=cost(5),
        name="far",
    )(got, pieces, far_depth, far_flows, wet_mask)
    far_new = pl.pallas_call(
        join_kernel,
        out_shape=shape(3, FX, FY),
        in_specs=[ANY] + [VM] * 4,
        out_specs=ANY,
        scratch_shapes=[pltpu.VMEM((2, 3, 8, FY), f32), pltpu.SemaphoreType.DMA((2,))],
        input_output_aliases={0: 0},
        compiler_params=PARAMS,
        cost_estimate=cost(1),
        name="join",
    )(part, head, tail, above, below)
    return (new_frac, far_new)


def solution(mesh):
    return jax.shard_map(
        local,
        mesh=mesh,
        in_specs=(
            P(None, "px", "dz", "py"),
            P("px", ("py", "dz"), None, None),
            P("px", ("py", "dz"), None),
            P("px", ("py", "dz")),
            P(None, "px", ("py", "dz")),
            P("px", ("py", "dz")),
        ),
        out_specs=(P("px", "dz", "py"), P(None, "px", ("py", "dz"))),
        check_vma=False,
    )
```

```python
import functools

import jax
import jax.numpy as jnp
from jax import lax
from jax.experimental import pallas as pl
from jax.experimental.pallas import tpu as pltpu
from jax.sharding import PartitionSpec as P


advect_coef = 0.25
diffuse_coef = 0.1
slope_coef = 0.5
flux_coef = 0.1
gravity = 1.0
column_height = 4.0

NPY = 4
NDZ = 4
GRP = NPY * NDZ
CX = 8
CZ = 48
CY = 256
FX = 64
FY = 256
ROWS = CX * 3 * 2
SIDE = CZ // 3
BLK = SIDE + 8

f32 = jnp.float32
GROUP = ("py", "dz")
VM = pl.BlockSpec(memory_space=pltpu.VMEM)
ANY = pl.BlockSpec(memory_space=pl.ANY)
PARAMS = pltpu.CompilerParams(vmem_limit_bytes=8 << 20)
HBM = pl.BlockSpec(memory_space=pltpu.HBM)


def lane_iota(shape):
    return lax.broadcasted_iota(jnp.int32, shape, len(shape) - 1)


def x_order(row):
    return 2 * row if row < 4 else 2 * (row - 4) + 1


def load_kernel(*refs):
    sources, copies, (xlo, xhi, zlo, zhi), sem = refs[:6], refs[6:12], refs[12:16], refs[16]
    moves = [(sources[0].at[:, 0], xlo), (sources[0].at[:, CX - 1], xhi), *zip(sources, copies)]
    moves = [pltpu.make_async_copy(a, b, sem.at[n]) for n, (a, b) in enumerate(moves)]
    for move in moves:
        move.start()
    for move in moves:
        move.wait()
    near = copies[0]
    for f in range(3):
        zlo[f] = near[f, :, 0, :]
        zhi[f] = near[f, :, CZ - 1, :]


def pack_kernel(near, owner, land, depth, flows, mask, out):
    py = lax.axis_index("py")
    dz = lax.axis_index("dz")
    me = py * NDZ + dz
    code = (owner[...] * (FX * FY) + land[...]).astype(f32)
    swap = pltpu.roll(code, 64, 1)
    odd = (me % 2) == 1
    codes = jnp.concatenate([jnp.where(odd, swap, code), jnp.where(odd, code, swap)], axis=0)
    lanes = lane_iota((8, 128))
    mine = jnp.where(odd, lanes, 127 - lanes) >= 64
    codes = jnp.where(mine, codes, 0.0)
    zero = jnp.zeros((SIDE, 128), f32)
    for b in range(GRP):
        out[b, 0:SIDE] = zero
        out[b, SIDE:BLK] = codes

    def edge(col):
        k = lane_iota((FX, 128))
        m = jnp.zeros((FX, 128), f32)
        for n, part in enumerate((depth[...], flows[0], flows[1], mask[...].astype(f32))):
            m = jnp.where(k == n, part[:, col : col + 1], m)
        turned = jnp.concatenate([m, m], axis=0).T
        return jnp.where(mine, codes, turned[0:8])

    @pl.when(me > 0)
    def _():
        out[me - 1, SIDE:BLK] = edge(0)

    @pl.when(me < GRP - 1)
    def _():
        out[me + 1, SIDE:BLK] = edge(FY - 1)

    def yface(dst, y):
        k = lane_iota((CZ, 128))
        m = jnp.zeros((CZ, 128), f32)
        for f in range(3):
            for x in range(CX):
                m = jnp.where(k == f * CX + x, near[f, x, :, y : y + 1], m)
        layers = [pltpu.roll(m[SIDE * n : SIDE * (n + 1)], 32 * n, 1) for n in range(3)]
        out[dst, 0:SIDE] = layers[0] + layers[1] + layers[2]

    @pl.when(py > 0)
    def _():
        yface(me - NDZ, 0)

    @pl.when(py < NPY - 1)
    def _():
        yface(me + NDZ, CY - 1)


def near_kernel(near, got, xlow, xhigh, down, up, frac, sums):
    py = lax.axis_index("py")
    me = py * NDZ + lax.axis_index("dz")

    def yface(at, inside):
        m = jnp.where(inside, got[at, 0:SIDE], 0.0)
        return jnp.concatenate([m] + [pltpu.roll(m, 128 - 32 * n, 1) for n in (1, 2)], axis=0)

    left = yface(jnp.maximum(me - NDZ, 0), py > 0)
    right = yface(jnp.minimum(me + NDZ, GRP - 1), py < NPY - 1)
    lane = lane_iota((CZ, CY))
    row = lax.broadcasted_iota(jnp.int32, (CZ, CY), 0)

    for p in range(CX):
        x = x_order(p)
        velx = near[1, x]
        vely = near[2, x]
        new = []
        for f in range(3):
            q = near[f, x]
            k = f * CX + x
            xp = near[f, x + 1] if x < CX - 1 else xhigh[f]
            xm = near[f, x - 1] if x > 0 else xlow[f]
            yp = jnp.where(lane == CY - 1, right[:, k : k + 1], pltpu.roll(q, CY - 1, 1))
            ym = jnp.where(lane == 0, left[:, k : k + 1], pltpu.roll(q, 1, 1))
            zp = jnp.where(row == CZ - 1, up[f, x : x + 1], pltpu.roll(q, CZ - 1, 0))
            zm = jnp.where(row == 0, down[f, x : x + 1], pltpu.roll(q, 1, 0))
            dx = xp - xm
            dy = yp - ym
            lap = xp + xm + yp + ym + zp + zm - 6.0 * q
            moved = q - advect_coef * (velx * dx + vely * dy) + diffuse_coef * lap
            if f == 0:
                fdx, fdy = dx, dy
            new.append(moved)
        frac[x] = new[0]
        parts = (
            new[0],
            new[0] * (new[1] - slope_coef * fdx),
            new[0] * (new[2] - slope_coef * fdy),
        )
        for f in range(3):
            total = jnp.sum(parts[f], axis=0, keepdims=True)
            for h in range(2):
                r = (f * 2 + h) * 8 + p
                sums[0, r : r + 1] = total[:, h * 128 : (h + 1) * 128]
    whole = sums[0]
    for b in range(1, GRP):
        sums[b] = whole


def decode(got, me, a, h):
    d = a * NDZ + 2 * h
    lanes = lane_iota((8, 128))
    code = jnp.where(lanes < 64, got[d, SIDE:BLK], got[d + 1, SIDE:BLK]).astype(jnp.int32)
    y = (code >> 14) * FY + (code & (FY - 1)) - me * FY
    y = jnp.where((y < -1) | (y > FY), -128, y)
    return y.astype(f32), ((code >> 8) & (FX - 1)).astype(f32)


def tall(row, rows):
    tile = jnp.broadcast_to(row, (16, 128)).astype(jnp.bfloat16)
    return jnp.concatenate([tile] * (rows // 16), axis=0)


def cell_rows(rows):
    return lax.broadcasted_iota(jnp.int32, (rows, 128), 0).astype(f32).astype(jnp.bfloat16)


OVER = (((1,), (1,)), ((), ()))


def spread(parts, wide):
    for m, part in enumerate(parts):
        wide[m * 8 : m * 8 + 8] = part


def gathered(wide, p):
    return wide[pl.ds(p, 16, stride=8), :].astype(jnp.bfloat16)


def pairs(build):
    for p in range(0, 8, 2):
        yield [jnp.concatenate(two, axis=1) for two in zip(build(p), build(p + 1))]


def edge_kernel(scale, got, sums, depth, flows, mask, pieces, top, bottom, wide):
    me = lax.axis_index("py") * NDZ + lax.axis_index("dz")
    ycell = cell_rows(FY)
    one = jnp.ones((FY, 128), jnp.bfloat16)
    zero = jnp.zeros((8, 128), f32)
    acc = jnp.zeros((16, FY), f32)
    for a in range(NPY):
        t = sums[a * NDZ]
        for b in range(1, NDZ):
            t = t + sums[a * NDZ + b]
        t = t * scale
        high = t.astype(jnp.bfloat16).astype(f32)
        low = t - high
        pieces[0, a] = high
        pieces[1, a] = low
        for h in range(2):
            g = a * 2 + h
            y, x = decode(got, me, a, h)
            rows = []
            for part in (high, low):
                for cell in (0, FX - 1):
                    for f in range(3):
                        r = (f * 2 + h) * 8
                        rows.append(jnp.where(x == cell, part[r : r + 8], 0.0))
                rows += [zero, zero]
            spread(rows, wide.at[g])

            def build(p):
                bits = jnp.where(ycell == tall(y[p : p + 1], FY), one, one * 0)
                return gathered(wide.at[g], p), bits

            for lhs, bits in pairs(build):
                acc = acc + lax.dot_general(lhs, bits, OVER, preferred_element_type=f32)
    acc = acc[0:8] + acc[8:16]
    blank = jnp.zeros((5, FY), f32)
    for e, out in ((0, top), (1, bottom)):
        at = 0 if e == 0 else FX - 1
        wet = mask[at : at + 1].astype(f32)
        h = depth[at : at + 1] + acc[e * 3 : e * 3 + 1]
        hu = (flows[0, at : at + 1] + acc[e * 3 + 1 : e * 3 + 2]) * wet
        hv = (flows[1, at : at + 1] + acc[e * 3 + 2 : e * 3 + 3]) * wet
        out[...] = jnp.concatenate([h, hu, hv, blank], axis=0)


def terms(h, hu, hv, ok):
    inv = 1.0 / jnp.where(ok, h, 1.0)
    cross = hu * hv * inv
    press = 0.5 * gravity * h * h
    xf = (hu, hu * hu * inv + press, cross)
    yf = (hv, cross, hv * hv * inv + press)
    s = (h, hu, hv)
    return [
        (
            0.25 * s[f] - flux_coef * xf[f],
            0.25 * s[f] + flux_coef * xf[f],
            0.25 * s[f] - flux_coef * yf[f],
            0.25 * s[f] + flux_coef * yf[f],
        )
        for f in range(3)
    ]


def far_kernel(
    got, pieces, depth, flows, mask, out, head, tail, wide
):
    me = lax.axis_index("py") * NDZ + lax.axis_index("dz")
    xcell = cell_rows(FX)
    ycell = cell_rows(FY)
    one = jnp.ones((FY, 128), jnp.bfloat16)
    none = jnp.zeros((FX, 128), jnp.bfloat16)
    zero = jnp.zeros((8, 128), f32)
    acc = jnp.zeros((6 * FX, FY), f32)
    side = jnp.zeros((16, FX), f32)
    for a in range(NPY):
        for h in range(2):
            g = a * 2 + h
            y, x = decode(got, me, a, h)
            rows = []
            for n in range(2):
                for cell in (-1, FY):
                    for f in range(3):
                        r = (f * 2 + h) * 8
                        rows.append(jnp.where(y == cell, pieces[n, a, r : r + 8], 0.0))
                rows += [zero, zero]
            spread(rows, wide.at[g])

            def build(p):
                bits = jnp.where(ycell == tall(y[p : p + 1], FY), one, one * 0)
                here = xcell == tall(x[p : p + 1], FX)
                parts = []
                for n in range(2):
                    for f in range(3):
                        r = (f * 2 + h) * 8 + p
                        value = tall(pieces[n, a, r : r + 1], FX)
                        parts.append(jnp.where(here, value, none))
                xbits = jnp.where(here, one[0:FX], none)
                return jnp.concatenate(parts, axis=0), bits, gathered(wide.at[g], p), xbits

            for lhs, bits, side_lhs, xbits in pairs(build):
                acc = acc + lax.dot_general(lhs, bits, OVER, preferred_element_type=f32)
                side = side + lax.dot_general(side_lhs, xbits, OVER, preferred_element_type=f32)
    source = acc[0 : 3 * FX] + acc[3 * FX :]
    side = side[0:8] + side[8:16]
    side = jnp.concatenate([side] * 16, axis=0)
    side = jnp.concatenate([side, side], axis=1).T
    wet = mask[...].astype(f32)
    raw = (depth[...], flows[0], flows[1])
    cells = []
    for f in range(3):
        s = raw[f] + source[f * FX : (f + 1) * FX]
        cells.append(s if f == 0 else s * wet)
    body = terms(*cells, True)
    sides = []
    for n in range(2):
        other = jnp.maximum(me - 1, 0) if n == 0 else jnp.minimum(me + 1, GRP - 1)
        block = got[other, SIDE:BLK]
        block = jnp.where((other % 2) == 1, block, pltpu.roll(block, 64, 1))
        e = jnp.concatenate([block] * 16, axis=0).T[0:FX]
        inside = (me > 0) if n == 0 else (me < GRP - 1)
        s = []
        for f in range(3):
            col = n * 3 + f
            v = e[:, f : f + 1] + side[0:FX, col : col + 1]
            v = v if f == 0 else v * e[:, 3:4]
            s.append(jnp.where(inside, v, 0.0))
        sides.append(terms(*s, inside))
    lane = lane_iota((FX, FY))
    row = lax.broadcasted_iota(jnp.int32, (FX, FY), 0)
    for f in range(3):
        xp = jnp.where(row == FX - 1, 0.0, pltpu.roll(body[f][0], FX - 1, 0))
        xm = jnp.where(row == 0, 0.0, pltpu.roll(body[f][1], 1, 0))
        yp = jnp.where(lane == FY - 1, sides[1][f][2], pltpu.roll(body[f][2], FY - 1, 1))
        ym = jnp.where(lane == 0, sides[0][f][3], pltpu.roll(body[f][3], 1, 1))
        new = (xp + xm) + (yp + ym)
        out[f] = new
        head[f] = new[0:8]
        tail[f] = new[FX - 8 : FX]


def join_kernel(part, head, tail, above, below, out, new, sem):
    px = lax.axis_index("px")
    up = terms(above[0:1], above[1:2], above[2:3], px > 0)
    dn = terms(below[0:1], below[1:2], below[2:3], px < lax.axis_size("px") - 1)
    row = lax.broadcasted_iota(jnp.int32, (8, FY), 0)
    for f in range(3):
        new[0, f] = head[f] + jnp.where(row == 0, up[f][1], 0.0)
        new[1, f] = tail[f] + jnp.where(row == 7, dn[f][0], 0.0)
    first = pltpu.make_async_copy(new.at[0], out.at[:, 0:8], sem.at[0])
    last = pltpu.make_async_copy(new.at[1], out.at[:, FX - 8 : FX], sem.at[1])
    first.start()
    last.start()
    first.wait()
    last.wait()


def shape(*dims):
    return jax.ShapeDtypeStruct(dims, f32)


def vmem(*dims):
    return pltpu.VMEM(dims, f32)


def cost(micros):
    return pl.CostEstimate(flops=0, bytes_accessed=micros * 3_000_000, transcendentals=0)


def local(near_state, column_owner, landing, far_depth, far_flows, wet_mask):
    n_px = lax.axis_size("px")
    forth = [(i, i + 1) for i in range(n_px - 1)]
    back = [(i + 1, i) for i in range(n_px - 1)]
    owner = column_owner.reshape(4, 128)
    land = landing.reshape(4, 128)
    given = (near_state, owner, land, far_depth, far_flows, wet_mask)
    *given, xlo, xhi, zlo, zhi = pl.pallas_call(
        load_kernel,
        out_shape=[pltpu.VMEM(x.shape, x.dtype) for x in given]
        + [vmem(3, CZ, CY)] * 2
        + [vmem(3, CX, CY)] * 2,
        in_specs=[HBM] * 6,
        out_specs=[VM] * 10,
        scratch_shapes=[pltpu.SemaphoreType.DMA((8,))],
        compiler_params=PARAMS,
        cost_estimate=cost(1),
        name="load",
    )(*[pltpu.with_memory_space_constraint(x, pltpu.HBM) for x in given])
    near_state, owner, land, far_depth, far_flows, wet_mask = given
    xlow = lax.ppermute(xhi, "px", forth)
    xhigh = lax.ppermute(xlo, "px", back)
    down = lax.ppermute(zhi, "dz", [(i, i + 1) for i in range(NDZ - 1)])
    up = lax.ppermute(zlo, "dz", [(i + 1, i) for i in range(NDZ - 1)])
    send = pl.pallas_call(
        pack_kernel,
        out_shape=shape(GRP, BLK, 128),
        in_specs=[VM] * 6,
        out_specs=VM,
        compiler_params=PARAMS,
        cost_estimate=cost(2),
        name="pack",
    )(near_state, owner, land, far_depth, far_flows, wet_mask)
    got = lax.all_to_all(send, GROUP, split_axis=0, concat_axis=0, tiled=True)
    new_frac, sums = pl.pallas_call(
        near_kernel,
        out_shape=(shape(CX, CZ, CY), shape(GRP, ROWS, 128)),
        in_specs=[VM] * 6,
        out_specs=(VM,) * 2,
        compiler_params=PARAMS,
        cost_estimate=cost(2),
        name="near",
    )(near_state, got, xlow, xhigh, down, up)
    sums = lax.all_to_all(sums, GROUP, split_axis=0, concat_axis=0, tiled=True)
    pieces, top, bottom = pl.pallas_call(
        functools.partial(edge_kernel, column_height / (CZ * NDZ)),
        out_shape=(vmem(2, NPY, ROWS, 128), vmem(8, FY), vmem(8, FY)),
        in_specs=[VM] * 5,
        out_specs=(VM,) * 3,
        scratch_shapes=[vmem(8, 128, 128)],
        compiler_params=PARAMS,
        cost_estimate=cost(2),
        name="edge",
    )(got, sums, far_depth, far_flows, wet_mask)
    above = lax.ppermute(bottom, "px", forth)
    below = lax.ppermute(top, "px", back)
    part, head, tail = pl.pallas_call(
        far_kernel,
        out_shape=(shape(3, FX, FY), vmem(3, 8, FY), vmem(3, 8, FY)),
        in_specs=[VM] * 5,
        out_specs=(VM,) * 3,
        scratch_shapes=[vmem(8, 128, 128)],
        compiler_params=pltpu.CompilerParams(vmem_limit_bytes=20 << 20),
        cost_estimate=cost(5),
        name="far",
    )(got, pieces, far_depth, far_flows, wet_mask)
    far_new = pl.pallas_call(
        join_kernel,
        out_shape=shape(3, FX, FY),
        in_specs=[ANY] + [VM] * 4,
        out_specs=ANY,
        scratch_shapes=[pltpu.VMEM((2, 3, 8, FY), f32), pltpu.SemaphoreType.DMA((2,))],
        input_output_aliases={0: 0},
        compiler_params=PARAMS,
        cost_estimate=cost(1),
        name="join",
    )(part, head, tail, above, below)
    return (new_frac, far_new)


def solution(mesh):
    return jax.shard_map(
        local,
        mesh=mesh,
        in_specs=(
            P(None, "px", "dz", "py"),
            P("px", ("py", "dz"), None, None),
            P("px", ("py", "dz"), None),
            P("px", ("py", "dz")),
            P(None, "px", ("py", "dz")),
            P("px", ("py", "dz")),
        ),
        out_specs=(P("px", "dz", "py"), P(None, "px", ("py", "dz"))),
        check_vma=False,
    )
```

```python
import functools

import jax
import jax.numpy as jnp
from jax import lax
from jax.experimental import pallas as pl
from jax.experimental.pallas import tpu as pltpu
from jax.sharding import PartitionSpec as P


advect_coef = 0.25
diffuse_coef = 0.1
slope_coef = 0.5
flux_coef = 0.1
gravity = 1.0
column_height = 4.0

NPY = 4
NDZ = 4
GRP = NPY * NDZ
CX = 8
CZ = 48
CY = 256
FX = 64
FY = 256
ROWS = CX * 3 * 2
BLK = ROWS + 8

f32 = jnp.float32
GROUP = ("py", "dz")
VM = pl.BlockSpec(memory_space=pltpu.VMEM)
ANY = pl.BlockSpec(memory_space=pl.ANY)
PARAMS = pltpu.CompilerParams(vmem_limit_bytes=8 << 20)
HBM = pl.BlockSpec(memory_space=pltpu.HBM)


def lane_iota(shape):
    return lax.broadcasted_iota(jnp.int32, shape, len(shape) - 1)


def x_order(row):
    return 2 * row if row < 4 else 2 * (row - 4) + 1


def load_kernel(*refs):
    sources, copies, (xlo, xhi), sem = refs[:6], refs[6:12], refs[12:14], refs[14]
    moves = [(sources[0].at[:, 0], xlo), (sources[0].at[:, CX - 1], xhi), *zip(sources, copies)]
    moves = [pltpu.make_async_copy(a, b, sem.at[n]) for n, (a, b) in enumerate(moves)]
    for move in moves:
        move.start()
    for move in moves:
        move.wait()


def pack_kernel(near, owner, land, depth, flows, mask, out):
    py = lax.axis_index("py")
    dz = lax.axis_index("dz")
    me = py * NDZ + dz
    code = (owner[...] * (FX * FY) + land[...]).astype(f32)
    swap = pltpu.roll(code, 64, 1)
    odd = (me % 2) == 1
    codes = jnp.concatenate([jnp.where(odd, swap, code), jnp.where(odd, code, swap)], axis=0)
    lanes = lane_iota((8, 128))
    mine = jnp.where(odd, lanes, 127 - lanes) >= 64
    codes = jnp.where(mine, codes, 0.0)
    zero = jnp.zeros((ROWS, 128), f32)
    for b in range(GRP):
        out[b, 0:ROWS] = zero
        out[b, ROWS:BLK] = codes

    def edge(col):
        k = lane_iota((FX, 128))
        m = jnp.zeros((FX, 128), f32)
        for n, part in enumerate((depth[...], flows[0], flows[1], mask[...].astype(f32))):
            m = jnp.where(k == n, part[:, col : col + 1], m)
        turned = jnp.concatenate([m, m], axis=0).T
        return jnp.where(mine, codes, turned[0:8])

    @pl.when(me > 0)
    def _():
        out[me - 1, ROWS:BLK] = edge(0)

    @pl.when(me < GRP - 1)
    def _():
        out[me + 1, ROWS:BLK] = edge(FY - 1)

    def zface(dst, z):
        for f in range(3):
            face = near[f, :, z, :]
            for h in range(2):
                r = (f * 2 + h) * 8
                out[dst, r : r + 8] = face[:, h * 128 : (h + 1) * 128]

    def yface(dst, y):
        k = lane_iota((CZ, 128))
        m = jnp.zeros((CZ, 128), f32)
        for f in range(3):
            for x in range(CX):
                m = jnp.where(k == f * CX + x, near[f, x, :, y : y + 1], m)
        out[dst, 0:ROWS] = m

    @pl.when(dz > 0)
    def _():
        zface(me - 1, 0)

    @pl.when(dz < NDZ - 1)
    def _():
        zface(me + 1, CZ - 1)

    @pl.when(py > 0)
    def _():
        yface(me - NDZ, 0)

    @pl.when(py < NPY - 1)
    def _():
        yface(me + NDZ, CY - 1)


def inner_kernel(near, xlow, xhigh, mid, vely):
    lane = lane_iota((CZ, CY))
    row = lax.broadcasted_iota(jnp.int32, (CZ, CY), 0)
    for x in range(CX):
        velx = near[1, x]
        velv = near[2, x]
        vely[x] = jnp.where(lane[:, 0:128] == 127, velv[:, 128:], velv[:, 0:128])
        for f in range(3):
            q = near[f, x]
            xp = near[f, x + 1] if x < CX - 1 else xhigh[f]
            xm = near[f, x - 1] if x > 0 else xlow[f]
            yp = jnp.where(lane == CY - 1, 0.0, pltpu.roll(q, CY - 1, 1))
            ym = jnp.where(lane == 0, 0.0, pltpu.roll(q, 1, 1))
            zp = jnp.where(row == CZ - 1, 0.0, pltpu.roll(q, CZ - 1, 0))
            zm = jnp.where(row == 0, 0.0, pltpu.roll(q, 1, 0))
            dx = xp - xm
            dy = yp - ym
            lap = xp + xm + yp + ym + zp + zm - 6.0 * q
            moved = q - advect_coef * (velx * dx + velv * dy) + diffuse_coef * lap
            if f == 0:
                fdx, fdy = dx, dy
            elif f == 1:
                moved = moved - slope_coef * fdx
            else:
                moved = moved - slope_coef * fdy
            mid[f, x] = moved


def near_kernel(mid, vely, got, frac, sums):
    py = lax.axis_index("py")
    dz = lax.axis_index("dz")
    me = py * NDZ + dz
    left = jnp.where(py > 0, got[jnp.maximum(me - NDZ, 0), 0:ROWS], 0.0)
    right = jnp.where(py < NPY - 1, got[jnp.minimum(me + NDZ, GRP - 1), 0:ROWS], 0.0)
    down = jnp.where(dz > 0, got[jnp.maximum(me - 1, 0), 0:ROWS], 0.0) * diffuse_coef
    up = jnp.where(dz < NDZ - 1, got[jnp.minimum(me + 1, GRP - 1), 0:ROWS], 0.0) * diffuse_coef
    lane = lane_iota((CZ, 128))
    row = lax.broadcasted_iota(jnp.int32, (8, 128), 0)
    for p in range(CX):
        x = x_order(p)
        for h in range(2):
            lanes = slice(h * 128, (h + 1) * 128)
            side, sign, edge = (left, 1.0, 0) if h == 0 else (right, -1.0, 127)
            coef = diffuse_coef + (sign * advect_coef) * vely[x]
            new = []
            for f in range(3):
                face = side[:, f * CX + x : f * CX + x + 1]
                term = face * coef
                if f == 2:
                    term = term + (sign * slope_coef) * side[:, x : x + 1]
                n = mid[f, x, :, lanes] + jnp.where(lane == edge, term, 0.0)
                r = (f * 2 + h) * 8 + x
                first = n[0:8] + jnp.where(row == 0, down[r : r + 1], 0.0)
                last = n[CZ - 8 : CZ] + jnp.where(row == 7, up[r : r + 1], 0.0)
                new.append(jnp.concatenate([first, n[8 : CZ - 8], last], axis=0))
            frac[x, :, lanes] = new[0]
            for f in range(3):
                part = new[0] if f == 0 else new[0] * new[f]
                r = (f * 2 + h) * 8 + p
                sums[0, r : r + 1] = jnp.sum(part, axis=0, keepdims=True)
    whole = sums[0]
    for b in range(1, GRP):
        sums[b] = whole


def decode(got, me, a, h):
    d = a * NDZ + 2 * h
    lanes = lane_iota((8, 128))
    code = jnp.where(lanes < 64, got[d, ROWS:BLK], got[d + 1, ROWS:BLK]).astype(jnp.int32)
    y = (code >> 14) * FY + (code & (FY - 1)) - me * FY
    y = jnp.where((y < -1) | (y > FY), -128, y)
    return y.astype(f32), ((code >> 8) & (FX - 1)).astype(f32)


def tall(row, rows):
    tile = jnp.broadcast_to(row, (16, 128)).astype(jnp.bfloat16)
    return jnp.concatenate([tile] * (rows // 16), axis=0)


def cell_rows(rows):
    return lax.broadcasted_iota(jnp.int32, (rows, 128), 0).astype(f32).astype(jnp.bfloat16)


OVER = (((1,), (1,)), ((), ()))


def spread(parts, wide):
    for m, part in enumerate(parts):
        wide[m * 8 : m * 8 + 8] = part


def gathered(wide, p):
    return wide[pl.ds(p, 16, stride=8), :].astype(jnp.bfloat16)


def pairs(build):
    for p in range(0, 8, 2):
        yield [jnp.concatenate(two, axis=1) for two in zip(build(p), build(p + 1))]


def edge_kernel(scale, got, sums, depth, flows, mask, pieces, top, bottom, wide):
    me = lax.axis_index("py") * NDZ + lax.axis_index("dz")
    ycell = cell_rows(FY)
    one = jnp.ones((FY, 128), jnp.bfloat16)
    zero = jnp.zeros((8, 128), f32)
    acc = jnp.zeros((16, FY), f32)
    for a in range(NPY):
        t = sums[a * NDZ]
        for b in range(1, NDZ):
            t = t + sums[a * NDZ + b]
        t = t * scale
        high = t.astype(jnp.bfloat16).astype(f32)
        low = t - high
        pieces[0, a] = high
        pieces[1, a] = low
        for h in range(2):
            g = a * 2 + h
            y, x = decode(got, me, a, h)
            rows = []
            for part in (high, low):
                for cell in (0, FX - 1):
                    for f in range(3):
                        r = (f * 2 + h) * 8
                        rows.append(jnp.where(x == cell, part[r : r + 8], 0.0))
                rows += [zero, zero]
            spread(rows, wide.at[g])

            def build(p):
                bits = jnp.where(ycell == tall(y[p : p + 1], FY), one, one * 0)
                return gathered(wide.at[g], p), bits

            for lhs, bits in pairs(build):
                acc = acc + lax.dot_general(lhs, bits, OVER, preferred_element_type=f32)
    acc = acc[0:8] + acc[8:16]
    blank = jnp.zeros((5, FY), f32)
    for e, out in ((0, top), (1, bottom)):
        at = 0 if e == 0 else FX - 1
        wet = mask[at : at + 1].astype(f32)
        h = depth[at : at + 1] + acc[e * 3 : e * 3 + 1]
        hu = (flows[0, at : at + 1] + acc[e * 3 + 1 : e * 3 + 2]) * wet
        hv = (flows[1, at : at + 1] + acc[e * 3 + 2 : e * 3 + 3]) * wet
        out[...] = jnp.concatenate([h, hu, hv, blank], axis=0)


def terms(h, hu, hv, ok):
    inv = 1.0 / jnp.where(ok, h, 1.0)
    cross = hu * hv * inv
    press = 0.5 * gravity * h * h
    xf = (hu, hu * hu * inv + press, cross)
    yf = (hv, cross, hv * hv * inv + press)
    s = (h, hu, hv)
    return [
        (
            0.25 * s[f] - flux_coef * xf[f],
            0.25 * s[f] + flux_coef * xf[f],
            0.25 * s[f] - flux_coef * yf[f],
            0.25 * s[f] + flux_coef * yf[f],
        )
        for f in range(3)
    ]


def far_kernel(
    got, pieces, depth, flows, mask, out, head, tail, wide
):
    me = lax.axis_index("py") * NDZ + lax.axis_index("dz")
    xcell = cell_rows(FX)
    ycell = cell_rows(FY)
    one = jnp.ones((FY, 128), jnp.bfloat16)
    none = jnp.zeros((FX, 128), jnp.bfloat16)
    zero = jnp.zeros((8, 128), f32)
    acc = jnp.zeros((6 * FX, FY), f32)
    side = jnp.zeros((16, FX), f32)
    for a in range(NPY):
        for h in range(2):
            g = a * 2 + h
            y, x = decode(got, me, a, h)
            rows = []
            for n in range(2):
                for cell in (-1, FY):
                    for f in range(3):
                        r = (f * 2 + h) * 8
                        rows.append(jnp.where(y == cell, pieces[n, a, r : r + 8], 0.0))
                rows += [zero, zero]
            spread(rows, wide.at[g])

            def build(p):
                bits = jnp.where(ycell == tall(y[p : p + 1], FY), one, one * 0)
                here = xcell == tall(x[p : p + 1], FX)
                parts = []
                for n in range(2):
                    for f in range(3):
                        r = (f * 2 + h) * 8 + p
                        value = tall(pieces[n, a, r : r + 1], FX)
                        parts.append(jnp.where(here, value, none))
                xbits = jnp.where(here, one[0:FX], none)
                return jnp.concatenate(parts, axis=0), bits, gathered(wide.at[g], p), xbits

            for lhs, bits, side_lhs, xbits in pairs(build):
                acc = acc + lax.dot_general(lhs, bits, OVER, preferred_element_type=f32)
                side = side + lax.dot_general(side_lhs, xbits, OVER, preferred_element_type=f32)
    source = acc[0 : 3 * FX] + acc[3 * FX :]
    side = side[0:8] + side[8:16]
    side = jnp.concatenate([side] * 16, axis=0)
    side = jnp.concatenate([side, side], axis=1).T
    wet = mask[...].astype(f32)
    raw = (depth[...], flows[0], flows[1])
    cells = []
    for f in range(3):
        s = raw[f] + source[f * FX : (f + 1) * FX]
        cells.append(s if f == 0 else s * wet)
    body = terms(*cells, True)
    sides = []
    for n in range(2):
        other = jnp.maximum(me - 1, 0) if n == 0 else jnp.minimum(me + 1, GRP - 1)
        block = got[other, ROWS:BLK]
        block = jnp.where((other % 2) == 1, block, pltpu.roll(block, 64, 1))
        e = jnp.concatenate([block] * 16, axis=0).T[0:FX]
        inside = (me > 0) if n == 0 else (me < GRP - 1)
        s = []
        for f in range(3):
            col = n * 3 + f
            v = e[:, f : f + 1] + side[0:FX, col : col + 1]
            v = v if f == 0 else v * e[:, 3:4]
            s.append(jnp.where(inside, v, 0.0))
        sides.append(terms(*s, inside))
    lane = lane_iota((FX, FY))
    row = lax.broadcasted_iota(jnp.int32, (FX, FY), 0)
    for f in range(3):
        xp = jnp.where(row == FX - 1, 0.0, pltpu.roll(body[f][0], FX - 1, 0))
        xm = jnp.where(row == 0, 0.0, pltpu.roll(body[f][1], 1, 0))
        yp = jnp.where(lane == FY - 1, sides[1][f][2], pltpu.roll(body[f][2], FY - 1, 1))
        ym = jnp.where(lane == 0, sides[0][f][3], pltpu.roll(body[f][3], 1, 1))
        new = (xp + xm) + (yp + ym)
        out[f] = new
        head[f] = new[0:8]
        tail[f] = new[FX - 8 : FX]


def join_kernel(part, head, tail, above, below, out, new, sem):
    px = lax.axis_index("px")
    up = terms(above[0:1], above[1:2], above[2:3], px > 0)
    dn = terms(below[0:1], below[1:2], below[2:3], px < lax.axis_size("px") - 1)
    row = lax.broadcasted_iota(jnp.int32, (8, FY), 0)
    for f in range(3):
        new[0, f] = head[f] + jnp.where(row == 0, up[f][1], 0.0)
        new[1, f] = tail[f] + jnp.where(row == 7, dn[f][0], 0.0)
    first = pltpu.make_async_copy(new.at[0], out.at[:, 0:8], sem.at[0])
    last = pltpu.make_async_copy(new.at[1], out.at[:, FX - 8 : FX], sem.at[1])
    first.start()
    last.start()
    first.wait()
    last.wait()


def shape(*dims):
    return jax.ShapeDtypeStruct(dims, f32)


def vmem(*dims):
    return pltpu.VMEM(dims, f32)


def cost(micros):
    return pl.CostEstimate(flops=0, bytes_accessed=micros * 3_000_000, transcendentals=0)


def local(near_state, column_owner, landing, far_depth, far_flows, wet_mask):
    n_px = lax.axis_size("px")
    forth = [(i, i + 1) for i in range(n_px - 1)]
    back = [(i + 1, i) for i in range(n_px - 1)]
    owner = column_owner.reshape(4, 128)
    land = landing.reshape(4, 128)
    given = (near_state, owner, land, far_depth, far_flows, wet_mask)
    *given, xlo, xhi = pl.pallas_call(
        load_kernel,
        out_shape=[pltpu.VMEM(x.shape, x.dtype) for x in given]
        + [vmem(3, CZ, CY)] * 2,
        in_specs=[HBM] * 6,
        out_specs=[VM] * 8,
        scratch_shapes=[pltpu.SemaphoreType.DMA((8,))],
        compiler_params=PARAMS,
        cost_estimate=cost(1),
        name="load",
    )(*[pltpu.with_memory_space_constraint(x, pltpu.HBM) for x in given])
    near_state, owner, land, far_depth, far_flows, wet_mask = given
    xlow = lax.ppermute(xhi, "px", forth)
    xhigh = lax.ppermute(xlo, "px", back)
    send = pl.pallas_call(
        pack_kernel,
        out_shape=shape(GRP, BLK, 128),
        in_specs=[VM] * 6,
        out_specs=VM,
        compiler_params=PARAMS,
        cost_estimate=cost(2),
        name="pack",
    )(near_state, owner, land, far_depth, far_flows, wet_mask)
    got = lax.all_to_all(send, GROUP, split_axis=0, concat_axis=0, tiled=True)
    mid, vely = pl.pallas_call(
        inner_kernel,
        out_shape=(vmem(3, CX, CZ, CY), vmem(CX, CZ, 128)),
        in_specs=[VM] * 3,
        out_specs=(VM,) * 2,
        compiler_params=PARAMS,
        cost_estimate=cost(2),
        name="inner",
    )(near_state, xlow, xhigh)
    new_frac, sums = pl.pallas_call(
        near_kernel,
        out_shape=(shape(CX, CZ, CY), shape(GRP, ROWS, 128)),
        in_specs=[VM] * 3,
        out_specs=(VM,) * 2,
        compiler_params=PARAMS,
        cost_estimate=cost(2),
        name="near",
    )(mid, vely, got)
    sums = lax.all_to_all(sums, GROUP, split_axis=0, concat_axis=0, tiled=True)
    pieces, top, bottom = pl.pallas_call(
        functools.partial(edge_kernel, column_height / (CZ * NDZ)),
        out_shape=(vmem(2, NPY, ROWS, 128), vmem(8, FY), vmem(8, FY)),
        in_specs=[VM] * 5,
        out_specs=(VM,) * 3,
        scratch_shapes=[vmem(8, 128, 128)],
        compiler_params=PARAMS,
        cost_estimate=cost(2),
        name="edge",
    )(got, sums, far_depth, far_flows, wet_mask)
    above = lax.ppermute(bottom, "px", forth)
    below = lax.ppermute(top, "px", back)
    part, head, tail = pl.pallas_call(
        far_kernel,
        out_shape=(shape(3, FX, FY), vmem(3, 8, FY), vmem(3, 8, FY)),
        in_specs=[VM] * 5,
        out_specs=(VM,) * 3,
        scratch_shapes=[vmem(8, 128, 128)],
        compiler_params=pltpu.CompilerParams(vmem_limit_bytes=20 << 20),
        cost_estimate=cost(5),
        name="far",
    )(got, pieces, far_depth, far_flows, wet_mask)
    far_new = pl.pallas_call(
        join_kernel,
        out_shape=shape(3, FX, FY),
        in_specs=[ANY] + [VM] * 4,
        out_specs=ANY,
        scratch_shapes=[pltpu.VMEM((2, 3, 8, FY), f32), pltpu.SemaphoreType.DMA((2,))],
        input_output_aliases={0: 0},
        compiler_params=PARAMS,
        cost_estimate=cost(1),
        name="join",
    )(part, head, tail, above, below)
    return (new_frac, far_new)


def solution(mesh):
    return jax.shard_map(
        local,
        mesh=mesh,
        in_specs=(
            P(None, "px", "dz", "py"),
            P("px", ("py", "dz"), None, None),
            P("px", ("py", "dz"), None),
            P("px", ("py", "dz")),
            P(None, "px", ("py", "dz")),
            P("px", ("py", "dz")),
        ),
        out_specs=(P("px", "dz", "py"), P(None, "px", ("py", "dz"))),
        check_vma=False,
    )
```

```python
import functools

import jax
import jax.numpy as jnp
from jax import lax
from jax.experimental import pallas as pl
from jax.experimental.pallas import tpu as pltpu
from jax.sharding import PartitionSpec as P


advect_coef = 0.25
diffuse_coef = 0.1
slope_coef = 0.5
flux_coef = 0.1
gravity = 1.0
column_height = 4.0

NPY = 4
NDZ = 4
GRP = NPY * NDZ
CX = 8
CZ = 48
CY = 256
FX = 64
FY = 256
ROWS = CX * 3 * 2
BLK = ROWS + 8

f32 = jnp.float32
GROUP = ("py", "dz")
VM = pl.BlockSpec(memory_space=pltpu.VMEM)
ANY = pl.BlockSpec(memory_space=pl.ANY)
PARAMS = pltpu.CompilerParams(vmem_limit_bytes=8 << 20)
HBM = pl.BlockSpec(memory_space=pltpu.HBM)


def lane_iota(shape):
    return lax.broadcasted_iota(jnp.int32, shape, len(shape) - 1)


def x_order(row):
    return 2 * row if row < 4 else 2 * (row - 4) + 1


def odd_px():
    return lax.rem(lax.axis_index("px"), 2) == 1


def swaps(count, first):
    low = range(first, count - 1, 2)
    return [(i, i + 1) for i in low] + [(i + 1, i) for i in low]


def load_kernel(*refs):
    sources, copies, (first, second), sem = refs[:6], refs[6:12], refs[12:14], refs[14]
    up = jnp.where(odd_px(), CX - 1, 0)
    near = sources[0]
    moves = [(near.at[:, up], first), (near.at[:, CX - 1 - up], second), *zip(sources, copies)]
    moves = [pltpu.make_async_copy(a, b, sem.at[n]) for n, (a, b) in enumerate(moves)]
    for move in moves:
        move.start()
    for move in moves:
        move.wait()


def pack_kernel(near, owner, land, depth, flows, mask, out):
    py = lax.axis_index("py")
    dz = lax.axis_index("dz")
    me = py * NDZ + dz
    code = (owner[...] * (FX * FY) + land[...]).astype(f32)
    swap = pltpu.roll(code, 64, 1)
    odd = (me % 2) == 1
    codes = jnp.concatenate([jnp.where(odd, swap, code), jnp.where(odd, code, swap)], axis=0)
    lanes = lane_iota((8, 128))
    mine = jnp.where(odd, lanes, 127 - lanes) >= 64
    codes = jnp.where(mine, codes, 0.0)
    zero = jnp.zeros((ROWS, 128), f32)
    for b in range(GRP):
        out[b, 0:ROWS] = zero
        out[b, ROWS:BLK] = codes

    def edge(col):
        k = lane_iota((FX, 128))
        m = jnp.zeros((FX, 128), f32)
        for n, part in enumerate((depth[...], flows[0], flows[1], mask[...].astype(f32))):
            m = jnp.where(k == n, part[:, col : col + 1], m)
        turned = jnp.concatenate([m, m], axis=0).T
        return jnp.where(mine, codes, turned[0:8])

    @pl.when(me > 0)
    def _():
        out[me - 1, ROWS:BLK] = edge(0)

    @pl.when(me < GRP - 1)
    def _():
        out[me + 1, ROWS:BLK] = edge(FY - 1)

    def zface(dst, z):
        for f in range(3):
            face = near[f, :, z, :]
            for h in range(2):
                r = (f * 2 + h) * 8
                out[dst, r : r + 8] = face[:, h * 128 : (h + 1) * 128]

    def yface(dst, y):
        k = lane_iota((CZ, 128))
        m = jnp.zeros((CZ, 128), f32)
        for f in range(3):
            for x in range(CX):
                m = jnp.where(k == f * CX + x, near[f, x, :, y : y + 1], m)
        out[dst, 0:ROWS] = m

    @pl.when(dz > 0)
    def _():
        zface(me - 1, 0)

    @pl.when(dz < NDZ - 1)
    def _():
        zface(me + 1, CZ - 1)

    @pl.when(py > 0)
    def _():
        yface(me - NDZ, 0)

    @pl.when(py < NPY - 1)
    def _():
        yface(me + NDZ, CY - 1)


def inner_kernel(near, first, second, mid, vely):
    odd = odd_px()
    lane = lane_iota((CZ, CY))
    row = lax.broadcasted_iota(jnp.int32, (CZ, CY), 0)
    for x in range(CX):
        velx = near[1, x]
        velv = near[2, x]
        vely[x] = jnp.where(lane[:, 0:128] == 127, velv[:, 128:], velv[:, 0:128])
        for f in range(3):
            q = near[f, x]
            xp = near[f, x + 1] if x < CX - 1 else jnp.where(odd, first[f], second[f])
            xm = near[f, x - 1] if x > 0 else jnp.where(odd, second[f], first[f])
            yp = jnp.where(lane == CY - 1, 0.0, pltpu.roll(q, CY - 1, 1))
            ym = jnp.where(lane == 0, 0.0, pltpu.roll(q, 1, 1))
            zp = jnp.where(row == CZ - 1, 0.0, pltpu.roll(q, CZ - 1, 0))
            zm = jnp.where(row == 0, 0.0, pltpu.roll(q, 1, 0))
            dx = xp - xm
            dy = yp - ym
            lap = xp + xm + yp + ym + zp + zm - 6.0 * q
            moved = q - advect_coef * (velx * dx + velv * dy) + diffuse_coef * lap
            if f == 0:
                fdx, fdy = dx, dy
            elif f == 1:
                moved = moved - slope_coef * fdx
            else:
                moved = moved - slope_coef * fdy
            mid[f, x] = moved


def near_kernel(mid, vely, got, frac, sums):
    py = lax.axis_index("py")
    dz = lax.axis_index("dz")
    me = py * NDZ + dz
    left = jnp.where(py > 0, got[jnp.maximum(me - NDZ, 0), 0:ROWS], 0.0)
    right = jnp.where(py < NPY - 1, got[jnp.minimum(me + NDZ, GRP - 1), 0:ROWS], 0.0)
    down = jnp.where(dz > 0, got[jnp.maximum(me - 1, 0), 0:ROWS], 0.0) * diffuse_coef
    up = jnp.where(dz < NDZ - 1, got[jnp.minimum(me + 1, GRP - 1), 0:ROWS], 0.0) * diffuse_coef
    lane = lane_iota((CZ, 128))
    row = lax.broadcasted_iota(jnp.int32, (8, 128), 0)
    for p in range(CX):
        x = x_order(p)
        for h in range(2):
            lanes = slice(h * 128, (h + 1) * 128)
            side, sign, edge = (left, 1.0, 0) if h == 0 else (right, -1.0, 127)
            coef = diffuse_coef + (sign * advect_coef) * vely[x]
            new = []
            for f in range(3):
                face = side[:, f * CX + x : f * CX + x + 1]
                term = face * coef
                if f == 2:
                    term = term + (sign * slope_coef) * side[:, x : x + 1]
                n = mid[f, x, :, lanes] + jnp.where(lane == edge, term, 0.0)
                r = (f * 2 + h) * 8 + x
                first = n[0:8] + jnp.where(row == 0, down[r : r + 1], 0.0)
                last = n[CZ - 8 : CZ] + jnp.where(row == 7, up[r : r + 1], 0.0)
                new.append(jnp.concatenate([first, n[8 : CZ - 8], last], axis=0))
            frac[x, :, lanes] = new[0]
            for f in range(3):
                part = new[0] if f == 0 else new[0] * new[f]
                r = (f * 2 + h) * 8 + p
                sums[0, r : r + 1] = jnp.sum(part, axis=0, keepdims=True)
    whole = sums[0]
    for b in range(1, GRP):
        sums[b] = whole


def decode(got, me, a, h):
    d = a * NDZ + 2 * h
    lanes = lane_iota((8, 128))
    code = jnp.where(lanes < 64, got[d, ROWS:BLK], got[d + 1, ROWS:BLK]).astype(jnp.int32)
    y = (code >> 14) * FY + (code & (FY - 1)) - me * FY
    y = jnp.where((y < -1) | (y > FY), -128, y)
    return y.astype(f32), ((code >> 8) & (FX - 1)).astype(f32)


def tall(row, rows):
    tile = jnp.broadcast_to(row, (16, 128)).astype(jnp.bfloat16)
    return jnp.concatenate([tile] * (rows // 16), axis=0)


def cell_rows(rows):
    return lax.broadcasted_iota(jnp.int32, (rows, 128), 0).astype(f32).astype(jnp.bfloat16)


OVER = (((1,), (1,)), ((), ()))


def spread(parts, wide):
    for m, part in enumerate(parts):
        wide[m * 8 : m * 8 + 8] = part


def gathered(wide, p):
    return wide[pl.ds(p, 16, stride=8), :].astype(jnp.bfloat16)


def pairs(build):
    for p in range(0, 8, 2):
        yield [jnp.concatenate(two, axis=1) for two in zip(build(p), build(p + 1))]


def edge_kernel(scale, got, sums, depth, flows, mask, pieces, send1, send2, wide):
    me = lax.axis_index("py") * NDZ + lax.axis_index("dz")
    ycell = cell_rows(FY)
    one = jnp.ones((FY, 128), jnp.bfloat16)
    zero = jnp.zeros((8, 128), f32)
    acc = jnp.zeros((16, FY), f32)
    for a in range(NPY):
        t = sums[a * NDZ]
        for b in range(1, NDZ):
            t = t + sums[a * NDZ + b]
        t = t * scale
        high = t.astype(jnp.bfloat16).astype(f32)
        low = t - high
        pieces[0, a] = high
        pieces[1, a] = low
        for h in range(2):
            g = a * 2 + h
            y, x = decode(got, me, a, h)
            rows = []
            for part in (high, low):
                for cell in (0, FX - 1):
                    for f in range(3):
                        r = (f * 2 + h) * 8
                        rows.append(jnp.where(x == cell, part[r : r + 8], 0.0))
                rows += [zero, zero]
            spread(rows, wide.at[g])

            def build(p):
                bits = jnp.where(ycell == tall(y[p : p + 1], FY), one, one * 0)
                return gathered(wide.at[g], p), bits

            for lhs, bits in pairs(build):
                acc = acc + lax.dot_general(lhs, bits, OVER, preferred_element_type=f32)
    acc = acc[0:8] + acc[8:16]
    blank = jnp.zeros((5, FY), f32)
    ends = []
    for e in range(2):
        at = 0 if e == 0 else FX - 1
        wet = mask[at : at + 1].astype(f32)
        h = depth[at : at + 1] + acc[e * 3 : e * 3 + 1]
        hu = (flows[0, at : at + 1] + acc[e * 3 + 1 : e * 3 + 2]) * wet
        hv = (flows[1, at : at + 1] + acc[e * 3 + 2 : e * 3 + 3]) * wet
        ends.append(jnp.concatenate([h, hu, hv, blank], axis=0))
    odd = odd_px()
    send1[...] = jnp.where(odd, ends[1], ends[0])
    send2[...] = jnp.where(odd, ends[0], ends[1])


def terms(h, hu, hv, ok):
    inv = 1.0 / jnp.where(ok, h, 1.0)
    cross = hu * hv * inv
    press = 0.5 * gravity * h * h
    xf = (hu, hu * hu * inv + press, cross)
    yf = (hv, cross, hv * hv * inv + press)
    s = (h, hu, hv)
    return [
        (
            0.25 * s[f] - flux_coef * xf[f],
            0.25 * s[f] + flux_coef * xf[f],
            0.25 * s[f] - flux_coef * yf[f],
            0.25 * s[f] + flux_coef * yf[f],
        )
        for f in range(3)
    ]


def far_kernel(
    got, pieces, depth, flows, mask, out, head, tail, wide
):
    me = lax.axis_index("py") * NDZ + lax.axis_index("dz")
    xcell = cell_rows(FX)
    ycell = cell_rows(FY)
    one = jnp.ones((FY, 128), jnp.bfloat16)
    none = jnp.zeros((FX, 128), jnp.bfloat16)
    zero = jnp.zeros((8, 128), f32)
    acc = jnp.zeros((6 * FX, FY), f32)
    side = jnp.zeros((16, FX), f32)
    for a in range(NPY):
        for h in range(2):
            g = a * 2 + h
            y, x = decode(got, me, a, h)
            rows = []
            for n in range(2):
                for cell in (-1, FY):
                    for f in range(3):
                        r = (f * 2 + h) * 8
                        rows.append(jnp.where(y == cell, pieces[n, a, r : r + 8], 0.0))
                rows += [zero, zero]
            spread(rows, wide.at[g])

            def build(p):
                bits = jnp.where(ycell == tall(y[p : p + 1], FY), one, one * 0)
                here = xcell == tall(x[p : p + 1], FX)
                parts = []
                for n in range(2):
                    for f in range(3):
                        r = (f * 2 + h) * 8 + p
                        value = tall(pieces[n, a, r : r + 1], FX)
                        parts.append(jnp.where(here, value, none))
                xbits = jnp.where(here, one[0:FX], none)
                return jnp.concatenate(parts, axis=0), bits, gathered(wide.at[g], p), xbits

            for lhs, bits, side_lhs, xbits in pairs(build):
                acc = acc + lax.dot_general(lhs, bits, OVER, preferred_element_type=f32)
                side = side + lax.dot_general(side_lhs, xbits, OVER, preferred_element_type=f32)
    source = acc[0 : 3 * FX] + acc[3 * FX :]
    side = side[0:8] + side[8:16]
    side = jnp.concatenate([side] * 16, axis=0)
    side = jnp.concatenate([side, side], axis=1).T
    wet = mask[...].astype(f32)
    raw = (depth[...], flows[0], flows[1])
    cells = []
    for f in range(3):
        s = raw[f] + source[f * FX : (f + 1) * FX]
        cells.append(s if f == 0 else s * wet)
    body = terms(*cells, True)
    sides = []
    for n in range(2):
        other = jnp.maximum(me - 1, 0) if n == 0 else jnp.minimum(me + 1, GRP - 1)
        block = got[other, ROWS:BLK]
        block = jnp.where((other % 2) == 1, block, pltpu.roll(block, 64, 1))
        e = jnp.concatenate([block] * 16, axis=0).T[0:FX]
        inside = (me > 0) if n == 0 else (me < GRP - 1)
        s = []
        for f in range(3):
            col = n * 3 + f
            v = e[:, f : f + 1] + side[0:FX, col : col + 1]
            v = v if f == 0 else v * e[:, 3:4]
            s.append(jnp.where(inside, v, 0.0))
        sides.append(terms(*s, inside))
    lane = lane_iota((FX, FY))
    row = lax.broadcasted_iota(jnp.int32, (FX, FY), 0)
    for f in range(3):
        xp = jnp.where(row == FX - 1, 0.0, pltpu.roll(body[f][0], FX - 1, 0))
        xm = jnp.where(row == 0, 0.0, pltpu.roll(body[f][1], 1, 0))
        yp = jnp.where(lane == FY - 1, sides[1][f][2], pltpu.roll(body[f][2], FY - 1, 1))
        ym = jnp.where(lane == 0, sides[0][f][3], pltpu.roll(body[f][3], 1, 1))
        new = (xp + xm) + (yp + ym)
        out[f] = new
        head[f] = new[0:8]
        tail[f] = new[FX - 8 : FX]


def join_kernel(part, head, tail, got1, got2, out, new, sem):
    px = lax.axis_index("px")
    odd = odd_px()
    above = jnp.where(odd, got2[...], got1[...])
    below = jnp.where(odd, got1[...], got2[...])
    up = terms(above[0:1], above[1:2], above[2:3], px > 0)
    dn = terms(below[0:1], below[1:2], below[2:3], px < lax.axis_size("px") - 1)
    row = lax.broadcasted_iota(jnp.int32, (8, FY), 0)
    for f in range(3):
        new[0, f] = head[f] + jnp.where(row == 0, up[f][1], 0.0)
        new[1, f] = tail[f] + jnp.where(row == 7, dn[f][0], 0.0)
    first = pltpu.make_async_copy(new.at[0], out.at[:, 0:8], sem.at[0])
    last = pltpu.make_async_copy(new.at[1], out.at[:, FX - 8 : FX], sem.at[1])
    first.start()
    last.start()
    first.wait()
    last.wait()


def shape(*dims):
    return jax.ShapeDtypeStruct(dims, f32)


def vmem(*dims):
    return pltpu.VMEM(dims, f32)


def cost(micros):
    return pl.CostEstimate(flops=0, bytes_accessed=micros * 3_000_000, transcendentals=0)


def local(near_state, column_owner, landing, far_depth, far_flows, wet_mask):
    n_px = lax.axis_size("px")
    owner = column_owner.reshape(4, 128)
    land = landing.reshape(4, 128)
    given = (near_state, owner, land, far_depth, far_flows, wet_mask)
    *given, face1, face2 = pl.pallas_call(
        load_kernel,
        out_shape=[pltpu.VMEM(x.shape, x.dtype) for x in given]
        + [vmem(3, CZ, CY)] * 2,
        in_specs=[HBM] * 6,
        out_specs=[VM] * 8,
        scratch_shapes=[pltpu.SemaphoreType.DMA((8,))],
        compiler_params=PARAMS,
        cost_estimate=cost(1),
        name="load",
    )(*[pltpu.with_memory_space_constraint(x, pltpu.HBM) for x in given])
    near_state, owner, land, far_depth, far_flows, wet_mask = given
    face1 = lax.ppermute(face1, "px", swaps(n_px, 1))
    face2 = lax.ppermute(face2, "px", swaps(n_px, 0))
    send = pl.pallas_call(
        pack_kernel,
        out_shape=shape(GRP, BLK, 128),
        in_specs=[VM] * 6,
        out_specs=VM,
        compiler_params=PARAMS,
        cost_estimate=cost(2),
        name="pack",
    )(near_state, owner, land, far_depth, far_flows, wet_mask)
    got = lax.all_to_all(send, GROUP, split_axis=0, concat_axis=0, tiled=True)
    mid, vely = pl.pallas_call(
        inner_kernel,
        out_shape=(vmem(3, CX, CZ, CY), vmem(CX, CZ, 128)),
        in_specs=[VM] * 3,
        out_specs=(VM,) * 2,
        compiler_params=PARAMS,
        cost_estimate=cost(2),
        name="inner",
    )(near_state, face1, face2)
    new_frac, sums = pl.pallas_call(
        near_kernel,
        out_shape=(shape(CX, CZ, CY), shape(GRP, ROWS, 128)),
        in_specs=[VM] * 3,
        out_specs=(VM,) * 2,
        compiler_params=PARAMS,
        cost_estimate=cost(2),
        name="near",
    )(mid, vely, got)
    sums = lax.all_to_all(sums, GROUP, split_axis=0, concat_axis=0, tiled=True)
    pieces, end1, end2 = pl.pallas_call(
        functools.partial(edge_kernel, column_height / (CZ * NDZ)),
        out_shape=(vmem(2, NPY, ROWS, 128), vmem(8, FY), vmem(8, FY)),
        in_specs=[VM] * 5,
        out_specs=(VM,) * 3,
        scratch_shapes=[vmem(8, 128, 128)],
        compiler_params=PARAMS,
        cost_estimate=cost(2),
        name="edge",
    )(got, sums, far_depth, far_flows, wet_mask)
    end1 = lax.ppermute(end1, "px", swaps(n_px, 1))
    end2 = lax.ppermute(end2, "px", swaps(n_px, 0))
    part, head, tail = pl.pallas_call(
        far_kernel,
        out_shape=(shape(3, FX, FY), vmem(3, 8, FY), vmem(3, 8, FY)),
        in_specs=[VM] * 5,
        out_specs=(VM,) * 3,
        scratch_shapes=[vmem(8, 128, 128)],
        compiler_params=pltpu.CompilerParams(vmem_limit_bytes=20 << 20),
        cost_estimate=cost(5),
        name="far",
    )(got, pieces, far_depth, far_flows, wet_mask)
    far_new = pl.pallas_call(
        join_kernel,
        out_shape=shape(3, FX, FY),
        in_specs=[ANY] + [VM] * 4,
        out_specs=ANY,
        scratch_shapes=[pltpu.VMEM((2, 3, 8, FY), f32), pltpu.SemaphoreType.DMA((2,))],
        input_output_aliases={0: 0},
        compiler_params=PARAMS,
        cost_estimate=cost(1),
        name="join",
    )(part, head, tail, end1, end2)
    return (new_frac, far_new)


def solution(mesh):
    return jax.shard_map(
        local,
        mesh=mesh,
        in_specs=(
            P(None, "px", "dz", "py"),
            P("px", ("py", "dz"), None, None),
            P("px", ("py", "dz"), None),
            P("px", ("py", "dz")),
            P(None, "px", ("py", "dz")),
            P("px", ("py", "dz")),
        ),
        out_specs=(P("px", "dz", "py"), P(None, "px", ("py", "dz"))),
        check_vma=False,
    )
```

```python
import functools

import jax
import jax.numpy as jnp
from jax import lax
from jax.experimental import pallas as pl
from jax.experimental.pallas import tpu as pltpu
from jax.sharding import PartitionSpec as P


advect_coef = 0.25
diffuse_coef = 0.1
slope_coef = 0.5
flux_coef = 0.1
gravity = 1.0
column_height = 4.0

NPY = 4
NDZ = 4
GRP = NPY * NDZ
CX = 8
CZ = 48
CY = 256
FX = 64
FY = 256
ROWS = CX * 3 * 2
BLK = ROWS + 8

f32 = jnp.float32
GROUP = ("py", "dz")
VM = pl.BlockSpec(memory_space=pltpu.VMEM)
ANY = pl.BlockSpec(memory_space=pl.ANY)
PARAMS = pltpu.CompilerParams(vmem_limit_bytes=8 << 20)
HBM = pl.BlockSpec(memory_space=pltpu.HBM)


def lane_iota(shape):
    return lax.broadcasted_iota(jnp.int32, shape, len(shape) - 1)


def x_order(row):
    return 2 * row if row < 4 else 2 * (row - 4) + 1


def odd_px():
    return lax.rem(lax.axis_index("px"), 2) == 1


def swaps(count, first):
    low = range(first, count - 1, 2)
    return [(i, i + 1) for i in low] + [(i + 1, i) for i in low]


def load_kernel(*refs):
    sources, copies, (first, second), sem = refs[:6], refs[6:12], refs[12:14], refs[14]
    up = jnp.where(odd_px(), CX - 1, 0)
    near = sources[0]
    moves = [(near.at[:, up], first), (near.at[:, CX - 1 - up], second), *zip(sources, copies)]
    moves = [pltpu.make_async_copy(a, b, sem.at[n]) for n, (a, b) in enumerate(moves)]
    for move in moves:
        move.start()
    for move in moves:
        move.wait()


def pack_kernel(near, owner, land, depth, flows, mask, out):
    py = lax.axis_index("py")
    dz = lax.axis_index("dz")
    me = py * NDZ + dz
    code = (owner[...] * (FX * FY) + land[...]).astype(f32)
    swap = pltpu.roll(code, 64, 1)
    odd = (me % 2) == 1
    codes = jnp.concatenate([jnp.where(odd, swap, code), jnp.where(odd, code, swap)], axis=0)
    lanes = lane_iota((8, 128))
    mine = jnp.where(odd, lanes, 127 - lanes) >= 64
    codes = jnp.where(mine, codes, 0.0)
    zero = jnp.zeros((ROWS, 128), f32)
    for b in range(GRP):
        out[b, 0:ROWS] = zero
        out[b, ROWS:BLK] = codes

    def edge(col):
        k = lane_iota((FX, 128))
        m = jnp.zeros((FX, 128), f32)
        for n, part in enumerate((depth[...], flows[0], flows[1], mask[...].astype(f32))):
            m = jnp.where(k == n, part[:, col : col + 1], m)
        turned = jnp.concatenate([m, m], axis=0).T
        return jnp.where(mine, codes, turned[0:8])

    @pl.when(me > 0)
    def _():
        out[me - 1, ROWS:BLK] = edge(0)

    @pl.when(me < GRP - 1)
    def _():
        out[me + 1, ROWS:BLK] = edge(FY - 1)

    def zface(dst, z):
        for f in range(3):
            face = near[f, :, z, :]
            for h in range(2):
                r = (f * 2 + h) * 8
                out[dst, r : r + 8] = face[:, h * 128 : (h + 1) * 128]

    def yface(dst, y):
        k = lane_iota((CZ, 128))
        m = jnp.zeros((CZ, 128), f32)
        for f in range(3):
            for x in range(CX):
                m = jnp.where(k == f * CX + x, near[f, x, :, y : y + 1], m)
        out[dst, 0:ROWS] = m

    @pl.when(dz > 0)
    def _():
        zface(me - 1, 0)

    @pl.when(dz < NDZ - 1)
    def _():
        zface(me + 1, CZ - 1)

    @pl.when(py > 0)
    def _():
        yface(me - NDZ, 0)

    @pl.when(py < NPY - 1)
    def _():
        yface(me + NDZ, CY - 1)


def inner_kernel(near, first, second, mid, vely):
    odd = odd_px()
    lane = lane_iota((CZ, CY))
    row = lax.broadcasted_iota(jnp.int32, (CZ, CY), 0)
    for x in range(CX):
        velx = near[1, x]
        velv = near[2, x]
        vely[x] = jnp.where(lane[:, 0:128] == 127, velv[:, 128:], velv[:, 0:128])
        for f in range(3):
            q = near[f, x]
            xp = near[f, x + 1] if x < CX - 1 else jnp.where(odd, first[f], second[f])
            xm = near[f, x - 1] if x > 0 else jnp.where(odd, second[f], first[f])
            yp = jnp.where(lane == CY - 1, 0.0, pltpu.roll(q, CY - 1, 1))
            ym = jnp.where(lane == 0, 0.0, pltpu.roll(q, 1, 1))
            zp = jnp.where(row == CZ - 1, 0.0, pltpu.roll(q, CZ - 1, 0))
            zm = jnp.where(row == 0, 0.0, pltpu.roll(q, 1, 0))
            dx = xp - xm
            dy = yp - ym
            lap = xp + xm + yp + ym + zp + zm - 6.0 * q
            moved = q - advect_coef * (velx * dx + velv * dy) + diffuse_coef * lap
            if f == 0:
                fdx, fdy = dx, dy
            elif f == 1:
                moved = moved - slope_coef * fdx
            else:
                moved = moved - slope_coef * fdy
            mid[f, x] = moved


def near_kernel(mid, vely, got, frac, sums):
    py = lax.axis_index("py")
    dz = lax.axis_index("dz")
    me = py * NDZ + dz
    left = jnp.where(py > 0, got[jnp.maximum(me - NDZ, 0), 0:ROWS], 0.0)
    right = jnp.where(py < NPY - 1, got[jnp.minimum(me + NDZ, GRP - 1), 0:ROWS], 0.0)
    down = jnp.where(dz > 0, got[jnp.maximum(me - 1, 0), 0:ROWS], 0.0) * diffuse_coef
    up = jnp.where(dz < NDZ - 1, got[jnp.minimum(me + 1, GRP - 1), 0:ROWS], 0.0) * diffuse_coef
    lane = lane_iota((CZ, 128))
    row = lax.broadcasted_iota(jnp.int32, (8, 128), 0)
    for p in range(CX):
        x = x_order(p)
        for h in range(2):
            lanes = slice(h * 128, (h + 1) * 128)
            side, sign, edge = (left, 1.0, 0) if h == 0 else (right, -1.0, 127)
            coef = diffuse_coef + (sign * advect_coef) * vely[x]
            new = []
            for f in range(3):
                face = side[:, f * CX + x : f * CX + x + 1]
                term = face * coef
                if f == 2:
                    term = term + (sign * slope_coef) * side[:, x : x + 1]
                n = mid[f, x, :, lanes] + jnp.where(lane == edge, term, 0.0)
                r = (f * 2 + h) * 8 + x
                first = n[0:8] + jnp.where(row == 0, down[r : r + 1], 0.0)
                last = n[CZ - 8 : CZ] + jnp.where(row == 7, up[r : r + 1], 0.0)
                new.append(jnp.concatenate([first, n[8 : CZ - 8], last], axis=0))
            frac[x, :, lanes] = new[0]
            for f in range(3):
                part = new[0] if f == 0 else new[0] * new[f]
                r = (f * 2 + h) * 8 + p
                sums[0, r : r + 1] = jnp.sum(part, axis=0, keepdims=True)
    whole = sums[0]
    for b in range(1, GRP):
        sums[b] = whole


def decode(got, me, a, h):
    d = a * NDZ + 2 * h
    lanes = lane_iota((8, 128))
    code = jnp.where(lanes < 64, got[d, ROWS:BLK], got[d + 1, ROWS:BLK]).astype(jnp.int32)
    y = (code >> 14) * FY + (code & (FY - 1)) - me * FY
    y = jnp.where((y < -1) | (y > FY), -128, y)
    return y.astype(f32), ((code >> 8) & (FX - 1)).astype(f32)


def tall(row, rows):
    tile = jnp.broadcast_to(row, (16, 128)).astype(jnp.bfloat16)
    return jnp.concatenate([tile] * (rows // 16), axis=0)


def cell_rows(rows):
    return lax.broadcasted_iota(jnp.int32, (rows, 128), 0).astype(f32).astype(jnp.bfloat16)


OVER = (((1,), (1,)), ((), ()))


def spread(parts, wide):
    for m, part in enumerate(parts):
        wide[m * 8 : m * 8 + 8] = part


def gathered(wide, p):
    return wide[pl.ds(p, 16, stride=8), :].astype(jnp.bfloat16)


def pairs(build):
    for p in range(0, 8, 2):
        yield [jnp.concatenate(two, axis=1) for two in zip(build(p), build(p + 1))]


def edge_kernel(scale, got, sums, depth, flows, mask, pieces, send1, send2, wide):
    me = lax.axis_index("py") * NDZ + lax.axis_index("dz")
    ycell = cell_rows(FY)
    one = jnp.ones((FY, 128), jnp.bfloat16)
    zero = jnp.zeros((8, 128), f32)
    acc = jnp.zeros((16, FY), f32)
    for a in range(NPY):
        t = sums[a * NDZ]
        for b in range(1, NDZ):
            t = t + sums[a * NDZ + b]
        t = t * scale
        high = t.astype(jnp.bfloat16).astype(f32)
        low = t - high
        pieces[0, a] = high
        pieces[1, a] = low
        for h in range(2):
            g = a * 2 + h
            y, x = decode(got, me, a, h)
            rows = []
            for part in (high, low):
                for cell in (0, FX - 1):
                    for f in range(3):
                        r = (f * 2 + h) * 8
                        rows.append(jnp.where(x == cell, part[r : r + 8], 0.0))
                rows += [zero, zero]
            spread(rows, wide.at[g])

            def build(p):
                bits = jnp.where(ycell == tall(y[p : p + 1], FY), one, one * 0)
                return gathered(wide.at[g], p), bits

            for lhs, bits in pairs(build):
                acc = acc + lax.dot_general(lhs, bits, OVER, preferred_element_type=f32)
    acc = acc[0:8] + acc[8:16]
    blank = jnp.zeros((5, FY), f32)
    ends = []
    for e in range(2):
        at = 0 if e == 0 else FX - 1
        wet = mask[at : at + 1].astype(f32)
        h = depth[at : at + 1] + acc[e * 3 : e * 3 + 1]
        hu = (flows[0, at : at + 1] + acc[e * 3 + 1 : e * 3 + 2]) * wet
        hv = (flows[1, at : at + 1] + acc[e * 3 + 2 : e * 3 + 3]) * wet
        ends.append(jnp.concatenate([h, hu, hv, blank], axis=0))
    odd = odd_px()
    send1[...] = jnp.where(odd, ends[1], ends[0])
    send2[...] = jnp.where(odd, ends[0], ends[1])


def terms(h, hu, hv, ok):
    inv = 1.0 / jnp.where(ok, h, 1.0)
    cross = hu * hv * inv
    press = 0.5 * gravity * h * h
    xf = (hu, hu * hu * inv + press, cross)
    yf = (hv, cross, hv * hv * inv + press)
    s = (h, hu, hv)
    return [
        (
            0.25 * s[f] - flux_coef * xf[f],
            0.25 * s[f] + flux_coef * xf[f],
            0.25 * s[f] - flux_coef * yf[f],
            0.25 * s[f] + flux_coef * yf[f],
        )
        for f in range(3)
    ]


def far_kernel(
    got, pieces, depth, flows, mask, out, wide
):
    me = lax.axis_index("py") * NDZ + lax.axis_index("dz")
    xcell = cell_rows(FX)
    ycell = cell_rows(FY)
    one = jnp.ones((FY, 128), jnp.bfloat16)
    none = jnp.zeros((FX, 128), jnp.bfloat16)
    zero = jnp.zeros((8, 128), f32)
    acc = jnp.zeros((6 * FX, FY), f32)
    side = jnp.zeros((16, FX), f32)
    for a in range(NPY):
        for h in range(2):
            g = a * 2 + h
            y, x = decode(got, me, a, h)
            rows = []
            for n in range(2):
                for cell in (-1, FY):
                    for f in range(3):
                        r = (f * 2 + h) * 8
                        rows.append(jnp.where(y == cell, pieces[n, a, r : r + 8], 0.0))
                rows += [zero, zero]
            spread(rows, wide.at[g])

            def build(p):
                bits = jnp.where(ycell == tall(y[p : p + 1], FY), one, one * 0)
                here = xcell == tall(x[p : p + 1], FX)
                parts = []
                for n in range(2):
                    for f in range(3):
                        r = (f * 2 + h) * 8 + p
                        value = tall(pieces[n, a, r : r + 1], FX)
                        parts.append(jnp.where(here, value, none))
                xbits = jnp.where(here, one[0:FX], none)
                return jnp.concatenate(parts, axis=0), bits, gathered(wide.at[g], p), xbits

            for lhs, bits, side_lhs, xbits in pairs(build):
                acc = acc + lax.dot_general(lhs, bits, OVER, preferred_element_type=f32)
                side = side + lax.dot_general(side_lhs, xbits, OVER, preferred_element_type=f32)
    source = acc[0 : 3 * FX] + acc[3 * FX :]
    side = side[0:8] + side[8:16]
    side = jnp.concatenate([side, side], axis=1)
    sides = []
    for n in range(2):
        other = jnp.maximum(me - 1, 0) if n == 0 else jnp.minimum(me + 1, GRP - 1)
        e = got[other, ROWS:BLK]
        e = jnp.where((other % 2) == 1, e, pltpu.roll(e, 64, 1))
        inside = (me > 0) if n == 0 else (me < GRP - 1)
        s = []
        for f in range(3):
            v = e[f : f + 1] + side[n * 3 + f : n * 3 + f + 1]
            v = v if f == 0 else v * e[3:4]
            s.append(jnp.where(inside, v, 0.0))
        sides += [t[3 - n] for t in terms(*s, inside)]
    sides = jnp.concatenate(sides + [jnp.zeros((2, 128), f32)], axis=0)
    sides = jnp.concatenate([sides] * 16, axis=0).T[0:FX]
    wet = mask[...].astype(f32)
    raw = (depth[...], flows[0], flows[1])
    cells = []
    for f in range(3):
        s = raw[f] + source[f * FX : (f + 1) * FX]
        cells.append(s if f == 0 else s * wet)
    body = terms(*cells, True)
    lane = lane_iota((FX, FY))
    row = lax.broadcasted_iota(jnp.int32, (FX, FY), 0)
    for f in range(3):
        xp = jnp.where(row == FX - 1, 0.0, pltpu.roll(body[f][0], FX - 1, 0))
        xm = jnp.where(row == 0, 0.0, pltpu.roll(body[f][1], 1, 0))
        yp = jnp.where(lane == FY - 1, sides[:, 3 + f : 4 + f], pltpu.roll(body[f][2], FY - 1, 1))
        ym = jnp.where(lane == 0, sides[:, f : f + 1], pltpu.roll(body[f][3], 1, 1))
        new = (xp + xm) + (yp + ym)
        out[f] = new


def join_kernel(part, got1, got2, out, new, sem):
    inner = pltpu.make_async_copy(part.at[:, 8 : FX - 8], out.at[:, 8 : FX - 8], sem.at[2])
    inner.start()
    px = lax.axis_index("px")
    odd = odd_px()
    above = jnp.where(odd, got2[...], got1[...])
    below = jnp.where(odd, got1[...], got2[...])
    up = terms(above[0:1], above[1:2], above[2:3], px > 0)
    dn = terms(below[0:1], below[1:2], below[2:3], px < lax.axis_size("px") - 1)
    row = lax.broadcasted_iota(jnp.int32, (8, FY), 0)
    for f in range(3):
        new[0, f] = part[f, 0:8] + jnp.where(row == 0, up[f][1], 0.0)
        new[1, f] = part[f, FX - 8 : FX] + jnp.where(row == 7, dn[f][0], 0.0)
    first = pltpu.make_async_copy(new.at[0], out.at[:, 0:8], sem.at[0])
    last = pltpu.make_async_copy(new.at[1], out.at[:, FX - 8 : FX], sem.at[1])
    first.start()
    last.start()
    first.wait()
    last.wait()
    inner.wait()


def shape(*dims):
    return jax.ShapeDtypeStruct(dims, f32)


def vmem(*dims):
    return pltpu.VMEM(dims, f32)


def cost(micros):
    return pl.CostEstimate(flops=0, bytes_accessed=micros * 3_000_000, transcendentals=0)


def local(near_state, column_owner, landing, far_depth, far_flows, wet_mask):
    n_px = lax.axis_size("px")
    owner = column_owner.reshape(4, 128)
    land = landing.reshape(4, 128)
    given = (near_state, owner, land, far_depth, far_flows, wet_mask)
    *given, face1, face2 = pl.pallas_call(
        load_kernel,
        out_shape=[pltpu.VMEM(x.shape, x.dtype) for x in given]
        + [vmem(3, CZ, CY)] * 2,
        in_specs=[HBM] * 6,
        out_specs=[VM] * 8,
        scratch_shapes=[pltpu.SemaphoreType.DMA((8,))],
        compiler_params=PARAMS,
        cost_estimate=cost(1),
        name="load",
    )(*[pltpu.with_memory_space_constraint(x, pltpu.HBM) for x in given])
    near_state, owner, land, far_depth, far_flows, wet_mask = given
    face1 = lax.ppermute(face1, "px", swaps(n_px, 1))
    face2 = lax.ppermute(face2, "px", swaps(n_px, 0))
    send = pl.pallas_call(
        pack_kernel,
        out_shape=shape(GRP, BLK, 128),
        in_specs=[VM] * 6,
        out_specs=VM,
        compiler_params=PARAMS,
        cost_estimate=cost(2),
        name="pack",
    )(near_state, owner, land, far_depth, far_flows, wet_mask)
    got = lax.all_to_all(send, GROUP, split_axis=0, concat_axis=0, tiled=True)
    mid, vely = pl.pallas_call(
        inner_kernel,
        out_shape=(vmem(3, CX, CZ, CY), vmem(CX, CZ, 128)),
        in_specs=[VM] * 3,
        out_specs=(VM,) * 2,
        compiler_params=PARAMS,
        cost_estimate=cost(2),
        name="inner",
    )(near_state, face1, face2)
    new_frac, sums = pl.pallas_call(
        near_kernel,
        out_shape=(shape(CX, CZ, CY), shape(GRP, ROWS, 128)),
        in_specs=[VM] * 3,
        out_specs=(VM,) * 2,
        compiler_params=PARAMS,
        cost_estimate=cost(2),
        name="near",
    )(mid, vely, got)
    sums = lax.all_to_all(sums, GROUP, split_axis=0, concat_axis=0, tiled=True)
    pieces, end1, end2 = pl.pallas_call(
        functools.partial(edge_kernel, column_height / (CZ * NDZ)),
        out_shape=(vmem(2, NPY, ROWS, 128), vmem(8, FY), vmem(8, FY)),
        in_specs=[VM] * 5,
        out_specs=(VM,) * 3,
        scratch_shapes=[vmem(8, 128, 128)],
        compiler_params=PARAMS,
        cost_estimate=cost(2),
        name="edge",
    )(got, sums, far_depth, far_flows, wet_mask)
    end1 = lax.ppermute(end1, "px", swaps(n_px, 1))
    end2 = lax.ppermute(end2, "px", swaps(n_px, 0))
    part = pl.pallas_call(
        far_kernel,
        out_shape=vmem(3, FX, FY),
        in_specs=[VM] * 5,
        out_specs=VM,
        scratch_shapes=[vmem(8, 128, 128)],
        compiler_params=pltpu.CompilerParams(vmem_limit_bytes=20 << 20),
        cost_estimate=cost(5),
        name="far",
    )(got, pieces, far_depth, far_flows, wet_mask)
    far_new = pl.pallas_call(
        join_kernel,
        out_shape=shape(3, FX, FY),
        in_specs=[VM] * 3,
        out_specs=ANY,
        scratch_shapes=[pltpu.VMEM((2, 3, 8, FY), f32), pltpu.SemaphoreType.DMA((3,))],
        compiler_params=PARAMS,
        cost_estimate=cost(1),
        name="join",
    )(part, end1, end2)
    return (new_frac, far_new)


def solution(mesh):
    return jax.shard_map(
        local,
        mesh=mesh,
        in_specs=(
            P(None, "px", "dz", "py"),
            P("px", ("py", "dz"), None, None),
            P("px", ("py", "dz"), None),
            P("px", ("py", "dz")),
            P(None, "px", ("py", "dz")),
            P("px", ("py", "dz")),
        ),
        out_specs=(P("px", "dz", "py"), P(None, "px", ("py", "dz"))),
        check_vma=False,
    )
```

```python
import functools

import jax
import jax.numpy as jnp
from jax import lax
from jax.experimental import pallas as pl
from jax.experimental.pallas import tpu as pltpu
from jax.sharding import PartitionSpec as P


advect_coef = 0.25
diffuse_coef = 0.1
slope_coef = 0.5
flux_coef = 0.1
gravity = 1.0
column_height = 4.0

NPY = 4
NDZ = 4
GRP = NPY * NDZ
CX = 8
CZ = 48
CY = 256
FX = 64
FY = 256
ROWS = CX * 3 * 2
SIDE = CZ // 3
BLK = SIDE + 8

f32 = jnp.float32
GROUP = ("py", "dz")
VM = pl.BlockSpec(memory_space=pltpu.VMEM)
ANY = pl.BlockSpec(memory_space=pl.ANY)
PARAMS = pltpu.CompilerParams(vmem_limit_bytes=8 << 20)
HBM = pl.BlockSpec(memory_space=pltpu.HBM)


def lane_iota(shape):
    return lax.broadcasted_iota(jnp.int32, shape, len(shape) - 1)


def x_order(row):
    return 2 * row if row < 4 else 2 * (row - 4) + 1


def odd_px():
    return lax.rem(lax.axis_index("px"), 2) == 1


def swaps(count, first):
    low = range(first, count - 1, 2)
    return [(i, i + 1) for i in low] + [(i + 1, i) for i in low]


def load_kernel(*refs):
    sources, copies, (first, second), sem = refs[:6], refs[6:12], refs[12:14], refs[14]
    up = jnp.where(odd_px(), CX - 1, 0)
    near = sources[0]
    moves = [(near.at[:, up], first), (near.at[:, CX - 1 - up], second), *zip(sources, copies)]
    moves = [pltpu.make_async_copy(a, b, sem.at[n]) for n, (a, b) in enumerate(moves)]
    for move in moves:
        move.start()
    for move in moves:
        move.wait()


def pack_kernel(near, owner, land, depth, flows, mask, out, z1, z2):
    py = lax.axis_index("py")
    dz = lax.axis_index("dz")
    me = py * NDZ + dz
    code = (owner[...] * (FX * FY) + land[...]).astype(f32)
    swap = pltpu.roll(code, 64, 1)
    odd = (me % 2) == 1
    codes = jnp.concatenate([jnp.where(odd, swap, code), jnp.where(odd, code, swap)], axis=0)
    lanes = lane_iota((8, 128))
    mine = jnp.where(odd, lanes, 127 - lanes) >= 64
    codes = jnp.where(mine, codes, 0.0)
    zero = jnp.zeros((SIDE, 128), f32)
    for b in range(GRP):
        out[b, 0:SIDE] = zero
        out[b, SIDE:BLK] = codes

    def edge(col):
        k = lane_iota((FX, 128))
        m = jnp.zeros((FX, 128), f32)
        for n, part in enumerate((depth[...], flows[0], flows[1], mask[...].astype(f32))):
            m = jnp.where(k == n, part[:, col : col + 1], m)
        turned = jnp.concatenate([m, m], axis=0).T
        return jnp.where(mine, codes, turned[0:8])

    @pl.when(me > 0)
    def _():
        out[me - 1, SIDE:BLK] = edge(0)

    @pl.when(me < GRP - 1)
    def _():
        out[me + 1, SIDE:BLK] = edge(FY - 1)

    odd_dz = lax.rem(dz, 2) == 1
    for f in range(3):
        low = near[f, :, 0, :]
        high = near[f, :, CZ - 1, :]
        z1[f] = jnp.where(odd_dz, high, low)
        z2[f] = jnp.where(odd_dz, low, high)

    def yface(dst, y):
        k = lane_iota((CZ, 128))
        m = jnp.zeros((CZ, 128), f32)
        for f in range(3):
            for x in range(CX):
                m = jnp.where(k == f * CX + x, near[f, x, :, y : y + 1], m)
        layers = [pltpu.roll(m[SIDE * n : SIDE * (n + 1)], 32 * n, 1) for n in range(3)]
        out[dst, 0:SIDE] = layers[0] + layers[1] + layers[2]

    @pl.when(py > 0)
    def _():
        yface(me - NDZ, 0)

    @pl.when(py < NPY - 1)
    def _():
        yface(me + NDZ, CY - 1)


def inner_kernel(near, first, second, mid, vely):
    odd = odd_px()
    lane = lane_iota((CZ, CY))
    row = lax.broadcasted_iota(jnp.int32, (CZ, CY), 0)
    for x in range(CX):
        velx = near[1, x]
        velv = near[2, x]
        vely[x] = jnp.where(lane[:, 0:128] == 127, velv[:, 128:], velv[:, 0:128])
        for f in range(3):
            q = near[f, x]
            xp = near[f, x + 1] if x < CX - 1 else jnp.where(odd, first[f], second[f])
            xm = near[f, x - 1] if x > 0 else jnp.where(odd, second[f], first[f])
            yp = jnp.where(lane == CY - 1, 0.0, pltpu.roll(q, CY - 1, 1))
            ym = jnp.where(lane == 0, 0.0, pltpu.roll(q, 1, 1))
            zp = jnp.where(row == CZ - 1, 0.0, pltpu.roll(q, CZ - 1, 0))
            zm = jnp.where(row == 0, 0.0, pltpu.roll(q, 1, 0))
            dx = xp - xm
            dy = yp - ym
            lap = xp + xm + yp + ym + zp + zm - 6.0 * q
            moved = q - advect_coef * (velx * dx + velv * dy) + diffuse_coef * lap
            if f == 0:
                fdx, fdy = dx, dy
            elif f == 1:
                moved = moved - slope_coef * fdx
            else:
                moved = moved - slope_coef * fdy
            mid[f, x] = moved


def near_kernel(mid, vely, got, z1, z2, frac, sums):
    py = lax.axis_index("py")
    dz = lax.axis_index("dz")
    me = py * NDZ + dz
    odd_dz = lax.rem(dz, 2) == 1
    up = [jnp.where(odd_dz, z1[f], z2[f]) * diffuse_coef for f in range(3)]
    down = [jnp.where(odd_dz, z2[f], z1[f]) * diffuse_coef for f in range(3)]

    def yface(at, inside):
        m = jnp.where(inside, got[at, 0:SIDE], 0.0)
        return jnp.concatenate([m] + [pltpu.roll(m, 128 - 32 * n, 1) for n in (1, 2)], axis=0)

    left = yface(jnp.maximum(me - NDZ, 0), py > 0)
    right = yface(jnp.minimum(me + NDZ, GRP - 1), py < NPY - 1)
    lane = lane_iota((CZ, 128))
    row = lax.broadcasted_iota(jnp.int32, (8, 128), 0)
    for p in range(CX):
        x = x_order(p)
        for h in range(2):
            lanes = slice(h * 128, (h + 1) * 128)
            side, sign, edge = (left, 1.0, 0) if h == 0 else (right, -1.0, 127)
            coef = diffuse_coef + (sign * advect_coef) * vely[x]
            new = []
            for f in range(3):
                face = side[:, f * CX + x : f * CX + x + 1]
                term = face * coef
                if f == 2:
                    term = term + (sign * slope_coef) * side[:, x : x + 1]
                n = mid[f, x, :, lanes] + jnp.where(lane == edge, term, 0.0)
                first = n[0:8] + jnp.where(row == 0, down[f][x : x + 1, lanes], 0.0)
                last = n[CZ - 8 : CZ] + jnp.where(row == 7, up[f][x : x + 1, lanes], 0.0)
                new.append(jnp.concatenate([first, n[8 : CZ - 8], last], axis=0))
            frac[x, :, lanes] = new[0]
            for f in range(3):
                part = new[0] if f == 0 else new[0] * new[f]
                r = (f * 2 + h) * 8 + p
                sums[0, r : r + 1] = jnp.sum(part, axis=0, keepdims=True)
    whole = sums[0]
    for b in range(1, GRP):
        sums[b] = whole


def decode(got, me, a, h):
    d = a * NDZ + 2 * h
    lanes = lane_iota((8, 128))
    code = jnp.where(lanes < 64, got[d, SIDE:BLK], got[d + 1, SIDE:BLK]).astype(jnp.int32)
    y = (code >> 14) * FY + (code & (FY - 1)) - me * FY
    y = jnp.where((y < -1) | (y > FY), -128, y)
    return y.astype(f32), ((code >> 8) & (FX - 1)).astype(f32)


def tall(row, rows):
    tile = jnp.broadcast_to(row, (16, 128)).astype(jnp.bfloat16)
    return jnp.concatenate([tile] * (rows // 16), axis=0)


def cell_rows(rows):
    return lax.broadcasted_iota(jnp.int32, (rows, 128), 0).astype(f32).astype(jnp.bfloat16)


OVER = (((1,), (1,)), ((), ()))


def spread(parts, wide):
    for m, part in enumerate(parts):
        wide[m * 8 : m * 8 + 8] = part


def gathered(wide, p):
    return wide[pl.ds(p, 16, stride=8), :].astype(jnp.bfloat16)


def pairs(build):
    for p in range(0, 8, 2):
        yield [jnp.concatenate(two, axis=1) for two in zip(build(p), build(p + 1))]


def edge_kernel(scale, got, sums, depth, flows, mask, pieces, send1, send2, wide):
    me = lax.axis_index("py") * NDZ + lax.axis_index("dz")
    ycell = cell_rows(FY)
    one = jnp.ones((FY, 128), jnp.bfloat16)
    zero = jnp.zeros((8, 128), f32)
    acc = jnp.zeros((16, FY), f32)
    for a in range(NPY):
        t = sums[a * NDZ]
        for b in range(1, NDZ):
            t = t + sums[a * NDZ + b]
        t = t * scale
        high = t.astype(jnp.bfloat16).astype(f32)
        low = t - high
        pieces[0, a] = high
        pieces[1, a] = low
        for h in range(2):
            g = a * 2 + h
            y, x = decode(got, me, a, h)
            rows = []
            for part in (high, low):
                for cell in (0, FX - 1):
                    for f in range(3):
                        r = (f * 2 + h) * 8
                        rows.append(jnp.where(x == cell, part[r : r + 8], 0.0))
                rows += [zero, zero]
            spread(rows, wide.at[g])

            def build(p):
                bits = jnp.where(ycell == tall(y[p : p + 1], FY), one, one * 0)
                return gathered(wide.at[g], p), bits

            for lhs, bits in pairs(build):
                acc = acc + lax.dot_general(lhs, bits, OVER, preferred_element_type=f32)
    acc = acc[0:8] + acc[8:16]
    blank = jnp.zeros((5, FY), f32)
    ends = []
    for e in range(2):
        at = 0 if e == 0 else FX - 1
        wet = mask[at : at + 1].astype(f32)
        h = depth[at : at + 1] + acc[e * 3 : e * 3 + 1]
        hu = (flows[0, at : at + 1] + acc[e * 3 + 1 : e * 3 + 2]) * wet
        hv = (flows[1, at : at + 1] + acc[e * 3 + 2 : e * 3 + 3]) * wet
        ends.append(jnp.concatenate([h, hu, hv, blank], axis=0))
    odd = odd_px()
    send1[...] = jnp.where(odd, ends[1], ends[0])
    send2[...] = jnp.where(odd, ends[0], ends[1])


def terms(h, hu, hv, ok):
    inv = 1.0 / jnp.where(ok, h, 1.0)
    cross = hu * hv * inv
    press = 0.5 * gravity * h * h
    xf = (hu, hu * hu * inv + press, cross)
    yf = (hv, cross, hv * hv * inv + press)
    s = (h, hu, hv)
    return [
        (
            0.25 * s[f] - flux_coef * xf[f],
            0.25 * s[f] + flux_coef * xf[f],
            0.25 * s[f] - flux_coef * yf[f],
            0.25 * s[f] + flux_coef * yf[f],
        )
        for f in range(3)
    ]


def far_kernel(
    got, pieces, depth, flows, mask, out, wide
):
    me = lax.axis_index("py") * NDZ + lax.axis_index("dz")
    xcell = cell_rows(FX)
    ycell = cell_rows(FY)
    one = jnp.ones((FY, 128), jnp.bfloat16)
    none = jnp.zeros((FX, 128), jnp.bfloat16)
    zero = jnp.zeros((8, 128), f32)
    acc = jnp.zeros((6 * FX, FY), f32)
    side = jnp.zeros((16, FX), f32)
    for a in range(NPY):
        for h in range(2):
            g = a * 2 + h
            y, x = decode(got, me, a, h)
            rows = []
            for n in range(2):
                for cell in (-1, FY):
                    for f in range(3):
                        r = (f * 2 + h) * 8
                        rows.append(jnp.where(y == cell, pieces[n, a, r : r + 8], 0.0))
                rows += [zero, zero]
            spread(rows, wide.at[g])

            def build(p):
                bits = jnp.where(ycell == tall(y[p : p + 1], FY), one, one * 0)
                here = xcell == tall(x[p : p + 1], FX)
                parts = []
                for n in range(2):
                    for f in range(3):
                        r = (f * 2 + h) * 8 + p
                        value = tall(pieces[n, a, r : r + 1], FX)
                        parts.append(jnp.where(here, value, none))
                xbits = jnp.where(here, one[0:FX], none)
                return jnp.concatenate(parts, axis=0), bits, gathered(wide.at[g], p), xbits

            for lhs, bits, side_lhs, xbits in pairs(build):
                acc = acc + lax.dot_general(lhs, bits, OVER, preferred_element_type=f32)
                side = side + lax.dot_general(side_lhs, xbits, OVER, preferred_element_type=f32)
    source = acc[0 : 3 * FX] + acc[3 * FX :]
    side = side[0:8] + side[8:16]
    side = jnp.concatenate([side, side], axis=1)
    sides = []
    for n in range(2):
        other = jnp.maximum(me - 1, 0) if n == 0 else jnp.minimum(me + 1, GRP - 1)
        e = got[other, SIDE:BLK]
        e = jnp.where((other % 2) == 1, e, pltpu.roll(e, 64, 1))
        inside = (me > 0) if n == 0 else (me < GRP - 1)
        s = []
        for f in range(3):
            v = e[f : f + 1] + side[n * 3 + f : n * 3 + f + 1]
            v = v if f == 0 else v * e[3:4]
            s.append(jnp.where(inside, v, 0.0))
        sides += [t[3 - n] for t in terms(*s, inside)]
    sides = jnp.concatenate(sides + [jnp.zeros((2, 128), f32)], axis=0)
    sides = jnp.concatenate([sides] * 16, axis=0).T[0:FX]
    wet = mask[...].astype(f32)
    raw = (depth[...], flows[0], flows[1])
    cells = []
    for f in range(3):
        s = raw[f] + source[f * FX : (f + 1) * FX]
        cells.append(s if f == 0 else s * wet)
    body = terms(*cells, True)
    lane = lane_iota((FX, FY))
    row = lax.broadcasted_iota(jnp.int32, (FX, FY), 0)
    for f in range(3):
        xp = jnp.where(row == FX - 1, 0.0, pltpu.roll(body[f][0], FX - 1, 0))
        xm = jnp.where(row == 0, 0.0, pltpu.roll(body[f][1], 1, 0))
        yp = jnp.where(lane == FY - 1, sides[:, 3 + f : 4 + f], pltpu.roll(body[f][2], FY - 1, 1))
        ym = jnp.where(lane == 0, sides[:, f : f + 1], pltpu.roll(body[f][3], 1, 1))
        new = (xp + xm) + (yp + ym)
        out[f] = new


def join_kernel(part, got1, got2, out, new, sem):
    inner = pltpu.make_async_copy(part.at[:, 8 : FX - 8], out.at[:, 8 : FX - 8], sem.at[2])
    inner.start()
    px = lax.axis_index("px")
    odd = odd_px()
    above = jnp.where(odd, got2[...], got1[...])
    below = jnp.where(odd, got1[...], got2[...])
    up = terms(above[0:1], above[1:2], above[2:3], px > 0)
    dn = terms(below[0:1], below[1:2], below[2:3], px < lax.axis_size("px") - 1)
    row = lax.broadcasted_iota(jnp.int32, (8, FY), 0)
    for f in range(3):
        new[0, f] = part[f, 0:8] + jnp.where(row == 0, up[f][1], 0.0)
        new[1, f] = part[f, FX - 8 : FX] + jnp.where(row == 7, dn[f][0], 0.0)
    first = pltpu.make_async_copy(new.at[0], out.at[:, 0:8], sem.at[0])
    last = pltpu.make_async_copy(new.at[1], out.at[:, FX - 8 : FX], sem.at[1])
    first.start()
    last.start()
    first.wait()
    last.wait()
    inner.wait()


def shape(*dims):
    return jax.ShapeDtypeStruct(dims, f32)


def vmem(*dims):
    return pltpu.VMEM(dims, f32)


def cost(micros):
    return pl.CostEstimate(flops=0, bytes_accessed=micros * 3_000_000, transcendentals=0)


def local(near_state, column_owner, landing, far_depth, far_flows, wet_mask):
    n_px = lax.axis_size("px")
    owner = column_owner.reshape(4, 128)
    land = landing.reshape(4, 128)
    given = (near_state, owner, land, far_depth, far_flows, wet_mask)
    *given, face1, face2 = pl.pallas_call(
        load_kernel,
        out_shape=[pltpu.VMEM(x.shape, x.dtype) for x in given]
        + [vmem(3, CZ, CY)] * 2,
        in_specs=[HBM] * 6,
        out_specs=[VM] * 8,
        scratch_shapes=[pltpu.SemaphoreType.DMA((8,))],
        compiler_params=PARAMS,
        cost_estimate=cost(1),
        name="load",
    )(*[pltpu.with_memory_space_constraint(x, pltpu.HBM) for x in given])
    near_state, owner, land, far_depth, far_flows, wet_mask = given
    face1 = lax.ppermute(face1, "px", swaps(n_px, 1))
    face2 = lax.ppermute(face2, "px", swaps(n_px, 0))
    send, z1, z2 = pl.pallas_call(
        pack_kernel,
        out_shape=(shape(GRP, BLK, 128), vmem(3, CX, CY), vmem(3, CX, CY)),
        in_specs=[VM] * 6,
        out_specs=(VM,) * 3,
        compiler_params=PARAMS,
        cost_estimate=cost(2),
        name="pack",
    )(near_state, owner, land, far_depth, far_flows, wet_mask)
    got = lax.all_to_all(send, GROUP, split_axis=0, concat_axis=0, tiled=True)
    z1 = lax.ppermute(z1, "dz", swaps(NDZ, 1))
    z2 = lax.ppermute(z2, "dz", swaps(NDZ, 0))
    mid, vely = pl.pallas_call(
        inner_kernel,
        out_shape=(vmem(3, CX, CZ, CY), vmem(CX, CZ, 128)),
        in_specs=[VM] * 3,
        out_specs=(VM,) * 2,
        compiler_params=PARAMS,
        cost_estimate=cost(2),
        name="inner",
    )(near_state, face1, face2)
    new_frac, sums = pl.pallas_call(
        near_kernel,
        out_shape=(shape(CX, CZ, CY), shape(GRP, ROWS, 128)),
        in_specs=[VM] * 5,
        out_specs=(VM,) * 2,
        compiler_params=PARAMS,
        cost_estimate=cost(2),
        name="near",
    )(mid, vely, got, z1, z2)
    sums = lax.all_to_all(sums, GROUP, split_axis=0, concat_axis=0, tiled=True)
    pieces, end1, end2 = pl.pallas_call(
        functools.partial(edge_kernel, column_height / (CZ * NDZ)),
        out_shape=(vmem(2, NPY, ROWS, 128), vmem(8, FY), vmem(8, FY)),
        in_specs=[VM] * 5,
        out_specs=(VM,) * 3,
        scratch_shapes=[vmem(8, 128, 128)],
        compiler_params=PARAMS,
        cost_estimate=cost(2),
        name="edge",
    )(got, sums, far_depth, far_flows, wet_mask)
    end1 = lax.ppermute(end1, "px", swaps(n_px, 1))
    end2 = lax.ppermute(end2, "px", swaps(n_px, 0))
    part = pl.pallas_call(
        far_kernel,
        out_shape=vmem(3, FX, FY),
        in_specs=[VM] * 5,
        out_specs=VM,
        scratch_shapes=[vmem(8, 128, 128)],
        compiler_params=pltpu.CompilerParams(vmem_limit_bytes=20 << 20),
        cost_estimate=cost(5),
        name="far",
    )(got, pieces, far_depth, far_flows, wet_mask)
    far_new = pl.pallas_call(
        join_kernel,
        out_shape=shape(3, FX, FY),
        in_specs=[VM] * 3,
        out_specs=ANY,
        scratch_shapes=[pltpu.VMEM((2, 3, 8, FY), f32), pltpu.SemaphoreType.DMA((3,))],
        compiler_params=PARAMS,
        cost_estimate=cost(1),
        name="join",
    )(part, end1, end2)
    return (new_frac, far_new)


def solution(mesh):
    return jax.shard_map(
        local,
        mesh=mesh,
        in_specs=(
            P(None, "px", "dz", "py"),
            P("px", ("py", "dz"), None, None),
            P("px", ("py", "dz"), None),
            P("px", ("py", "dz")),
            P(None, "px", ("py", "dz")),
            P("px", ("py", "dz")),
        ),
        out_specs=(P("px", "dz", "py"), P(None, "px", ("py", "dz"))),
        check_vma=False,
    )
```

```python
import functools

import jax
import jax.numpy as jnp
from jax import lax
from jax.experimental import pallas as pl
from jax.experimental.pallas import tpu as pltpu
from jax.sharding import PartitionSpec as P


advect_coef = 0.25
diffuse_coef = 0.1
slope_coef = 0.5
flux_coef = 0.1
gravity = 1.0
column_height = 4.0

NPY = 4
NDZ = 4
GRP = NPY * NDZ
CX = 8
CZ = 48
CY = 256
FX = 64
FY = 256
ROWS = CX * 3 * 2
SIDE = CZ // 3
BLK = SIDE + 8

f32 = jnp.float32
GROUP = ("py", "dz")
VM = pl.BlockSpec(memory_space=pltpu.VMEM)
ANY = pl.BlockSpec(memory_space=pl.ANY)
PARAMS = pltpu.CompilerParams(vmem_limit_bytes=8 << 20)
HBM = pl.BlockSpec(memory_space=pltpu.HBM)


def lane_iota(shape):
    return lax.broadcasted_iota(jnp.int32, shape, len(shape) - 1)


def x_order(row):
    return 2 * row if row < 4 else 2 * (row - 4) + 1


def odd_px():
    return lax.rem(lax.axis_index("px"), 2) == 1


def swaps(count, first):
    low = range(first, count - 1, 2)
    return [(i, i + 1) for i in low] + [(i + 1, i) for i in low]


def load_kernel(*refs):
    sources, copies, (first, second), sem = refs[:6], refs[6:12], refs[12:14], refs[14]
    up = jnp.where(odd_px(), CX - 1, 0)
    near = sources[0]
    moves = [(near.at[:, up], first), (near.at[:, CX - 1 - up], second), *zip(sources, copies)]
    moves = [pltpu.make_async_copy(a, b, sem.at[n]) for n, (a, b) in enumerate(moves)]
    for move in moves:
        move.start()
    for move in moves:
        move.wait()


def pack_kernel(near, owner, land, depth, flows, mask, out, z1, z2):
    py = lax.axis_index("py")
    dz = lax.axis_index("dz")
    me = py * NDZ + dz
    code = (owner[...] * (FX * FY) + land[...]).astype(f32)
    swap = pltpu.roll(code, 64, 1)
    odd = (me % 2) == 1
    codes = jnp.concatenate([jnp.where(odd, swap, code), jnp.where(odd, code, swap)], axis=0)
    lanes = lane_iota((8, 128))
    mine = jnp.where(odd, lanes, 127 - lanes) >= 64
    codes = jnp.where(mine, codes, 0.0)
    zero = jnp.zeros((SIDE, 128), f32)
    for b in range(GRP):
        out[b, 0:SIDE] = zero
        out[b, SIDE:BLK] = codes

    def edge(col):
        k = lane_iota((FX, 128))
        m = jnp.zeros((FX, 128), f32)
        for n, part in enumerate((depth[...], flows[0], flows[1], mask[...].astype(f32))):
            m = jnp.where(k == n, part[:, col : col + 1], m)
        turned = jnp.concatenate([m, m], axis=0).T
        return jnp.where(mine, codes, turned[0:8])

    @pl.when(me > 0)
    def _():
        out[me - 1, SIDE:BLK] = edge(0)

    @pl.when(me < GRP - 1)
    def _():
        out[me + 1, SIDE:BLK] = edge(FY - 1)

    odd_dz = lax.rem(dz, 2) == 1
    for f in range(3):
        low = near[f, :, 0, :]
        high = near[f, :, CZ - 1, :]
        z1[f] = jnp.where(odd_dz, high, low)
        z2[f] = jnp.where(odd_dz, low, high)

    def yface(dst, y):
        k = lane_iota((CZ, 128))
        m = jnp.zeros((CZ, 128), f32)
        for f in range(3):
            for x in range(CX):
                m = jnp.where(k == f * CX + x, near[f, x, :, y : y + 1], m)
        layers = [pltpu.roll(m[SIDE * n : SIDE * (n + 1)], 32 * n, 1) for n in range(3)]
        out[dst, 0:SIDE] = layers[0] + layers[1] + layers[2]

    @pl.when(py > 0)
    def _():
        yface(me - NDZ, 0)

    @pl.when(py < NPY - 1)
    def _():
        yface(me + NDZ, CY - 1)


def inner_kernel(near, first, second, mid, vely):
    odd = odd_px()
    lane = lane_iota((CZ, CY))
    row = lax.broadcasted_iota(jnp.int32, (CZ, CY), 0)
    for x in range(CX):
        velx = near[1, x]
        velv = near[2, x]
        vely[x] = jnp.where(lane[:, 0:128] == 127, velv[:, 128:], velv[:, 0:128])
        for f in range(3):
            q = near[f, x]
            xp = near[f, x + 1] if x < CX - 1 else jnp.where(odd, first[f], second[f])
            xm = near[f, x - 1] if x > 0 else jnp.where(odd, second[f], first[f])
            yp = jnp.where(lane == CY - 1, 0.0, pltpu.roll(q, CY - 1, 1))
            ym = jnp.where(lane == 0, 0.0, pltpu.roll(q, 1, 1))
            zp = jnp.where(row == CZ - 1, 0.0, pltpu.roll(q, CZ - 1, 0))
            zm = jnp.where(row == 0, 0.0, pltpu.roll(q, 1, 0))
            dx = xp - xm
            dy = yp - ym
            lap = xp + xm + yp + ym + zp + zm - 6.0 * q
            moved = q - advect_coef * (velx * dx + velv * dy) + diffuse_coef * lap
            if f == 0:
                fdx, fdy = dx, dy
            elif f == 1:
                moved = moved - slope_coef * fdx
            else:
                moved = moved - slope_coef * fdy
            mid[f, x] = moved


def near_kernel(mid, vely, got, z1, z2, frac, sums):
    py = lax.axis_index("py")
    dz = lax.axis_index("dz")
    me = py * NDZ + dz
    odd_dz = lax.rem(dz, 2) == 1
    up = [jnp.where(odd_dz, z1[f], z2[f]) * diffuse_coef for f in range(3)]
    down = [jnp.where(odd_dz, z2[f], z1[f]) * diffuse_coef for f in range(3)]

    def yface(at, inside):
        m = jnp.where(inside, got[at, 0:SIDE], 0.0)
        return jnp.concatenate([m] + [pltpu.roll(m, 128 - 32 * n, 1) for n in (1, 2)], axis=0)

    left = yface(jnp.maximum(me - NDZ, 0), py > 0)
    right = yface(jnp.minimum(me + NDZ, GRP - 1), py < NPY - 1)
    lane = lane_iota((CZ, 128))
    row = lax.broadcasted_iota(jnp.int32, (8, 128), 0)
    for p in range(CX):
        x = x_order(p)
        for h in range(2):
            lanes = slice(h * 128, (h + 1) * 128)
            side, sign, edge = (left, 1.0, 0) if h == 0 else (right, -1.0, 127)
            coef = diffuse_coef + (sign * advect_coef) * vely[x]
            new = []
            for f in range(3):
                face = side[:, f * CX + x : f * CX + x + 1]
                term = face * coef
                if f == 2:
                    term = term + (sign * slope_coef) * side[:, x : x + 1]
                n = mid[f, x, :, lanes] + jnp.where(lane == edge, term, 0.0)
                first = n[0:8] + jnp.where(row == 0, down[f][x : x + 1, lanes], 0.0)
                last = n[CZ - 8 : CZ] + jnp.where(row == 7, up[f][x : x + 1, lanes], 0.0)
                new.append(jnp.concatenate([first, n[8 : CZ - 8], last], axis=0))
            frac[x, :, lanes] = new[0]
            for f in range(3):
                part = new[0] if f == 0 else new[0] * new[f]
                r = (f * 2 + h) * 8 + p
                sums[0, r : r + 1] = jnp.sum(part, axis=0, keepdims=True)
    whole = sums[0]
    for b in range(1, GRP):
        sums[b] = whole


def decode(got, me, a, h):
    d = a * NDZ + 2 * h
    lanes = lane_iota((8, 128))
    code = jnp.where(lanes < 64, got[d, SIDE:BLK], got[d + 1, SIDE:BLK]).astype(jnp.int32)
    y = (code >> 14) * FY + (code & (FY - 1)) - me * FY
    y = jnp.where((y < -1) | (y > FY), -128, y)
    return y.astype(f32), ((code >> 8) & (FX - 1)).astype(f32)


def tall(row, rows):
    tile = jnp.broadcast_to(row, (16, 128)).astype(jnp.bfloat16)
    return jnp.concatenate([tile] * (rows // 16), axis=0)


def cell_rows(rows):
    return lax.broadcasted_iota(jnp.int32, (rows, 128), 0).astype(f32).astype(jnp.bfloat16)


OVER = (((1,), (1,)), ((), ()))


def spread(parts, wide):
    for m, part in enumerate(parts):
        wide[m * 8 : m * 8 + 8] = part


def gathered(wide, p):
    return wide[pl.ds(p, 16, stride=8), :].astype(jnp.bfloat16)


def pairs(build):
    for p in range(0, 8, 2):
        yield [jnp.concatenate(two, axis=1) for two in zip(build(p), build(p + 1))]


def edge_kernel(scale, got, sums, depth, flows, mask, pieces, send1, send2, wide):
    me = lax.axis_index("py") * NDZ + lax.axis_index("dz")
    ycell = cell_rows(FY)
    one = jnp.ones((FY, 128), jnp.bfloat16)
    zero = jnp.zeros((8, 128), f32)
    acc = jnp.zeros((16, FY), f32)
    for a in range(NPY):
        t = sums[a * NDZ]
        for b in range(1, NDZ):
            t = t + sums[a * NDZ + b]
        t = t * scale
        high = t.astype(jnp.bfloat16).astype(f32)
        low = t - high
        pieces[0, a] = high
        pieces[1, a] = low
        for h in range(2):
            g = a * 2 + h
            y, x = decode(got, me, a, h)
            rows = []
            for part in (high, low):
                for cell in (0, FX - 1):
                    for f in range(3):
                        r = (f * 2 + h) * 8
                        rows.append(jnp.where(x == cell, part[r : r + 8], 0.0))
                rows += [zero, zero]
            spread(rows, wide.at[g])

            def build(p):
                bits = jnp.where(ycell == tall(y[p : p + 1], FY), one, one * 0)
                return gathered(wide.at[g], p), bits

            for lhs, bits in pairs(build):
                acc = acc + lax.dot_general(lhs, bits, OVER, preferred_element_type=f32)
    acc = acc[0:8] + acc[8:16]
    blank = jnp.zeros((5, FY), f32)
    ends = []
    for e in range(2):
        at = 0 if e == 0 else FX - 1
        wet = mask[at : at + 1].astype(f32)
        h = depth[at : at + 1] + acc[e * 3 : e * 3 + 1]
        hu = (flows[0, at : at + 1] + acc[e * 3 + 1 : e * 3 + 2]) * wet
        hv = (flows[1, at : at + 1] + acc[e * 3 + 2 : e * 3 + 3]) * wet
        ends.append(jnp.concatenate([h, hu, hv, blank], axis=0))
    odd = odd_px()
    send1[...] = jnp.where(odd, ends[1], ends[0])
    send2[...] = jnp.where(odd, ends[0], ends[1])


def terms(h, hu, hv, ok):
    inv = 1.0 / jnp.where(ok, h, 1.0)
    cross = hu * hv * inv
    press = 0.5 * gravity * h * h
    xf = (hu, hu * hu * inv + press, cross)
    yf = (hv, cross, hv * hv * inv + press)
    s = (h, hu, hv)
    return [
        (
            0.25 * s[f] - flux_coef * xf[f],
            0.25 * s[f] + flux_coef * xf[f],
            0.25 * s[f] - flux_coef * yf[f],
            0.25 * s[f] + flux_coef * yf[f],
        )
        for f in range(3)
    ]


def far_kernel(
    got, pieces, depth, flows, mask, frac, out, frac_out, wide, sem
):
    keep = pltpu.make_async_copy(frac, frac_out, sem)
    keep.start()
    me = lax.axis_index("py") * NDZ + lax.axis_index("dz")
    xcell = cell_rows(FX)
    ycell = cell_rows(FY)
    one = jnp.ones((FY, 128), jnp.bfloat16)
    none = jnp.zeros((FX, 128), jnp.bfloat16)
    zero = jnp.zeros((8, 128), f32)
    acc = jnp.zeros((6 * FX, FY), f32)
    side = jnp.zeros((16, FX), f32)
    for a in range(NPY):
        for h in range(2):
            g = a * 2 + h
            y, x = decode(got, me, a, h)
            rows = []
            for n in range(2):
                for cell in (-1, FY):
                    for f in range(3):
                        r = (f * 2 + h) * 8
                        rows.append(jnp.where(y == cell, pieces[n, a, r : r + 8], 0.0))
                rows += [zero, zero]
            spread(rows, wide.at[g])

            def build(p):
                bits = jnp.where(ycell == tall(y[p : p + 1], FY), one, one * 0)
                here = xcell == tall(x[p : p + 1], FX)
                parts = []
                for n in range(2):
                    for f in range(3):
                        r = (f * 2 + h) * 8 + p
                        value = tall(pieces[n, a, r : r + 1], FX)
                        parts.append(jnp.where(here, value, none))
                xbits = jnp.where(here, one[0:FX], none)
                return jnp.concatenate(parts, axis=0), bits, gathered(wide.at[g], p), xbits

            for lhs, bits, side_lhs, xbits in pairs(build):
                acc = acc + lax.dot_general(lhs, bits, OVER, preferred_element_type=f32)
                side = side + lax.dot_general(side_lhs, xbits, OVER, preferred_element_type=f32)
    source = acc[0 : 3 * FX] + acc[3 * FX :]
    side = side[0:8] + side[8:16]
    side = jnp.concatenate([side, side], axis=1)
    sides = []
    for n in range(2):
        other = jnp.maximum(me - 1, 0) if n == 0 else jnp.minimum(me + 1, GRP - 1)
        e = got[other, SIDE:BLK]
        e = jnp.where((other % 2) == 1, e, pltpu.roll(e, 64, 1))
        inside = (me > 0) if n == 0 else (me < GRP - 1)
        s = []
        for f in range(3):
            v = e[f : f + 1] + side[n * 3 + f : n * 3 + f + 1]
            v = v if f == 0 else v * e[3:4]
            s.append(jnp.where(inside, v, 0.0))
        sides += [t[3 - n] for t in terms(*s, inside)]
    sides = jnp.concatenate(sides + [jnp.zeros((2, 128), f32)], axis=0)
    sides = jnp.concatenate([sides] * 16, axis=0).T[0:FX]
    wet = mask[...].astype(f32)
    raw = (depth[...], flows[0], flows[1])
    cells = []
    for f in range(3):
        s = raw[f] + source[f * FX : (f + 1) * FX]
        cells.append(s if f == 0 else s * wet)
    body = terms(*cells, True)
    lane = lane_iota((FX, FY))
    row = lax.broadcasted_iota(jnp.int32, (FX, FY), 0)
    for f in range(3):
        xp = jnp.where(row == FX - 1, 0.0, pltpu.roll(body[f][0], FX - 1, 0))
        xm = jnp.where(row == 0, 0.0, pltpu.roll(body[f][1], 1, 0))
        yp = jnp.where(lane == FY - 1, sides[:, 3 + f : 4 + f], pltpu.roll(body[f][2], FY - 1, 1))
        ym = jnp.where(lane == 0, sides[:, f : f + 1], pltpu.roll(body[f][3], 1, 1))
        new = (xp + xm) + (yp + ym)
        out[f] = new
    keep.wait()


def join_kernel(part, got1, got2, out, new, sem):
    inner = pltpu.make_async_copy(part.at[:, 8 : FX - 8], out.at[:, 8 : FX - 8], sem.at[2])
    inner.start()
    px = lax.axis_index("px")
    odd = odd_px()
    above = jnp.where(odd, got2[...], got1[...])
    below = jnp.where(odd, got1[...], got2[...])
    up = terms(above[0:1], above[1:2], above[2:3], px > 0)
    dn = terms(below[0:1], below[1:2], below[2:3], px < lax.axis_size("px") - 1)
    row = lax.broadcasted_iota(jnp.int32, (8, FY), 0)
    for f in range(3):
        new[0, f] = part[f, 0:8] + jnp.where(row == 0, up[f][1], 0.0)
        new[1, f] = part[f, FX - 8 : FX] + jnp.where(row == 7, dn[f][0], 0.0)
    first = pltpu.make_async_copy(new.at[0], out.at[:, 0:8], sem.at[0])
    last = pltpu.make_async_copy(new.at[1], out.at[:, FX - 8 : FX], sem.at[1])
    first.start()
    last.start()
    first.wait()
    last.wait()
    inner.wait()


def shape(*dims):
    return jax.ShapeDtypeStruct(dims, f32)


def vmem(*dims):
    return pltpu.VMEM(dims, f32)


def cost(micros):
    return pl.CostEstimate(flops=0, bytes_accessed=micros * 3_000_000, transcendentals=0)


def local(near_state, column_owner, landing, far_depth, far_flows, wet_mask):
    n_px = lax.axis_size("px")
    owner = column_owner.reshape(4, 128)
    land = landing.reshape(4, 128)
    given = (near_state, owner, land, far_depth, far_flows, wet_mask)
    *given, face1, face2 = pl.pallas_call(
        load_kernel,
        out_shape=[pltpu.VMEM(x.shape, x.dtype) for x in given]
        + [vmem(3, CZ, CY)] * 2,
        in_specs=[HBM] * 6,
        out_specs=[VM] * 8,
        scratch_shapes=[pltpu.SemaphoreType.DMA((8,))],
        compiler_params=PARAMS,
        cost_estimate=cost(1),
        name="load",
    )(*[pltpu.with_memory_space_constraint(x, pltpu.HBM) for x in given])
    near_state, owner, land, far_depth, far_flows, wet_mask = given
    face1 = lax.ppermute(face1, "px", swaps(n_px, 1))
    face2 = lax.ppermute(face2, "px", swaps(n_px, 0))
    send, z1, z2 = pl.pallas_call(
        pack_kernel,
        out_shape=(shape(GRP, BLK, 128), vmem(3, CX, CY), vmem(3, CX, CY)),
        in_specs=[VM] * 6,
        out_specs=(VM,) * 3,
        compiler_params=PARAMS,
        cost_estimate=cost(2),
        name="pack",
    )(near_state, owner, land, far_depth, far_flows, wet_mask)
    got = lax.all_to_all(send, GROUP, split_axis=0, concat_axis=0, tiled=True)
    z1 = lax.ppermute(z1, "dz", swaps(NDZ, 1))
    z2 = lax.ppermute(z2, "dz", swaps(NDZ, 0))
    mid, vely = pl.pallas_call(
        inner_kernel,
        out_shape=(vmem(3, CX, CZ, CY), vmem(CX, CZ, 128)),
        in_specs=[VM] * 3,
        out_specs=(VM,) * 2,
        compiler_params=PARAMS,
        cost_estimate=cost(2),
        name="inner",
    )(near_state, face1, face2)
    new_frac, sums = pl.pallas_call(
        near_kernel,
        out_shape=(vmem(CX, CZ, CY), shape(GRP, ROWS, 128)),
        in_specs=[VM] * 5,
        out_specs=(VM,) * 2,
        compiler_params=PARAMS,
        cost_estimate=cost(2),
        name="near",
    )(mid, vely, got, z1, z2)
    sums = lax.all_to_all(sums, GROUP, split_axis=0, concat_axis=0, tiled=True)
    pieces, end1, end2 = pl.pallas_call(
        functools.partial(edge_kernel, column_height / (CZ * NDZ)),
        out_shape=(vmem(2, NPY, ROWS, 128), vmem(8, FY), vmem(8, FY)),
        in_specs=[VM] * 5,
        out_specs=(VM,) * 3,
        scratch_shapes=[vmem(8, 128, 128)],
        compiler_params=PARAMS,
        cost_estimate=cost(2),
        name="edge",
    )(got, sums, far_depth, far_flows, wet_mask)
    end1 = lax.ppermute(end1, "px", swaps(n_px, 1))
    end2 = lax.ppermute(end2, "px", swaps(n_px, 0))
    part, new_frac = pl.pallas_call(
        far_kernel,
        out_shape=(vmem(3, FX, FY), shape(CX, CZ, CY)),
        in_specs=[VM] * 6,
        out_specs=(VM, ANY),
        scratch_shapes=[vmem(8, 128, 128), pltpu.SemaphoreType.DMA(())],
        compiler_params=pltpu.CompilerParams(vmem_limit_bytes=20 << 20),
        cost_estimate=cost(5),
        name="far",
    )(got, pieces, far_depth, far_flows, wet_mask, new_frac)
    far_new = pl.pallas_call(
        join_kernel,
        out_shape=shape(3, FX, FY),
        in_specs=[VM] * 3,
        out_specs=ANY,
        scratch_shapes=[pltpu.VMEM((2, 3, 8, FY), f32), pltpu.SemaphoreType.DMA((3,))],
        compiler_params=PARAMS,
        cost_estimate=cost(1),
        name="join",
    )(part, end1, end2)
    return (new_frac, far_new)


def solution(mesh):
    return jax.shard_map(
        local,
        mesh=mesh,
        in_specs=(
            P(None, "px", "dz", "py"),
            P("px", ("py", "dz"), None, None),
            P("px", ("py", "dz"), None),
            P("px", ("py", "dz")),
            P(None, "px", ("py", "dz")),
            P("px", ("py", "dz")),
        ),
        out_specs=(P("px", "dz", "py"), P(None, "px", ("py", "dz"))),
        check_vma=False,
    )
```
